128 devices in a mesh: dom: 16 (over y, x_hi, core), cls: 8 (over x_lo, z).
Axes of the slice: x: 4 (x_hi: 2, x_lo: 2; x = x_hi * 2 + x_lo), y: 4, z: 4, core: 2. Of those that a mesh axis runs over, the one named last changes fastest.
Arguments:
- particles: bfloat16 [16384, 9216], P(('dom', 'cls')), may hold values from -6 to 6
- references: bfloat16 [200, 9216], P('cls', 'dom'), may hold values from -0.0625 to 0.0625
- owner: int32 [16384, 1], P(('dom', 'cls')), may hold values from 0 to 7; in each aligned block of 128 rows (0 to 127, 128 to 255, ...) at most 32 rows name the same one
- class_offset: int32 [16384], P(('dom', 'cls')), may hold values from 0 to 24
- rotation: int32 [16384], P(('dom', 'cls')), may hold values from 0 to 71
- shifts: int32 [16384, 2], P(('dom', 'cls')), may hold values from -6 to 6
- ctf_group: int32 [16384], P(('dom', 'cls')), may hold values from 0 to 255, as said below
- ctf_table: float32 [256, 64], replicated, may hold values from -6 to 6
Outputs:
- best_score: float32 [16384], P(('dom', 'cls'))
- new_references: float32 [200, 9216], P('cls', 'dom')
The draws below stay inside these ranges and needn't reach their ends.
Inputs may be any that keep to these rules, and one draw needn't show every extreme that they name: Among the particles of one device no owner index is named more than 32 times, a bound that some block reaches. `ctf_group`: the particles of device block i (rows i * 128 to (i + 1) * 128 - 1) use only groups i * 2 to (i + 1) * 2 - 1.
All inputs are finite; a program needn't handle non-finite values.
Results may differ from the reference program's by a relative error of at most 0.0029.
Values may be sent and summed in bfloat16 or wider, within the bound.
No kernel may reach another device: no remote copies, remote signals or barrier semaphores. Data moves between devices by JAX's collectives and lax.ppermute only.
A program may use at most 128 MiB of HBM per device.

```python
import math
import jax
import jax.numpy as jnp
import numpy as np
from jax import lax

A = 72
R = 64
CLASSES = 200
BOX = 128
SHIFT = 6
GPD = 2
P_DEV = 128
P_ALL = 16384
CPD = 25
CAP = 32
GROUPS = 256
N_CLS = 8


def draw_ctf_group(key, part):
    first_rows = jnp.arange(P_ALL, dtype=jnp.int32) // P_DEV * GPD
    return first_rows + jax.random.randint(key, (P_ALL,), 0, GPD, dtype=jnp.int32)


def draw_ctf_table(key, part):
    level = jnp.arange(GROUPS, dtype=jnp.float32) / (GROUPS - 1)
    scale_rows = 10.0 ** (0.5 * level)
    values_out = jnp.clip(0.6 * jax.random.normal(key, (GROUPS, R), jnp.float32), -1.0, 1.0)
    return values_out * scale_rows[:, None]


def with_ends(result, rng, low, top_value):
    longest = result.shape.index(max(result.shape))
    spots = []
    for shift in (0, 1):
        where = [jax.random.randint(jax.random.fold_in(rng, axis), (), 0, length) for axis, length in enumerate(result.shape)]
        where[longest] = (where[longest] + shift) % result.shape[longest]
        spots.append(tuple(where))
    return result.at[spots[0]].set(low).at[spots[1]].set(top_value)


def block_levels(own_key, dims, cuts, low, largest):
    gain = 1.0
    for position, shards_of in cuts:
        draws = jax.random.uniform(jax.random.fold_in(jax.random.fold_in(own_key, 6), position), (shards_of,), jnp.float32, low / len(cuts), largest / len(cuts))
        gain = gain * jnp.repeat(jnp.exp(draws), dims[position] // shards_of).reshape((-1,) + (1,) * (len(dims) - 1 - position))
    return gain


def shared_out(key, own, number, rows, count, top, limit, lean):
    order = jax.random.permutation(key, count)
    crowded, usual = load_shares(count, rows * top, limit, lean, True), load_shares(count, rows * top, limit, lean, False)
    places = jnp.arange(count)

    def named(tallies, turn):
        used = int((tallies > 0).sum())
        fixed = max(1, used // 4)
        moved = fixed + (places - fixed + turn * (used - fixed)) % max(1, count - fixed)
        return jnp.zeros((count,), jnp.int32).at[order[jnp.where(places < fixed, places, moved)]].set(jnp.asarray(tallies, jnp.int32))

    tallies = jnp.where(number % 4 == 0, named(crowded, number // 4), named(usual, number - number // 4 - 1))
    mixed = jax.random.permutation(jax.random.fold_in(own, 3), count)
    giver, taker = mixed[0:count // 2 * 2:2], mixed[1:count // 2 * 2:2]
    slack = jnp.minimum(tallies[giver] - 1, limit - tallies[taker]) // 2
    slack = jnp.where((giver == order[0]) | (taker == order[0]) | (tallies[taker] == 0), 0, jnp.maximum(slack, 0))
    moved = jax.random.randint(jax.random.fold_in(own, 4), (count // 2,), 0, 1 << 20) % (slack + 1)
    tallies = tallies.at[giver].add(-moved).at[taker].add(moved)
    items = jnp.searchsorted(jnp.cumsum(tallies), jnp.arange(rows * top), side="right").astype(jnp.int32)
    grid = items.reshape(top, rows).T
    grid = grid[jax.random.permutation(jax.random.fold_in(own, 1), rows)]
    turn = jax.random.randint(jax.random.fold_in(own, 2), (rows, 1), 0, top)
    return jnp.take_along_axis(grid, (jnp.arange(top)[None, :] + turn) % top, axis=1)


def load_shares(count, total, bound, lean, full):
    weights = [(1 << 20) // math.isqrt(grade ** lean) + 1 for grade in range(1, count + 1)]
    largest = bound if full else min(bound, max(-(-total // count), total * weights[0] // sum(weights)))
    least = 1 if total - largest >= count - 1 else 0
    given, spare = [largest] + [least] * (count - 1), total - largest - least * (count - 1)
    while spare > 0:
        movable = [i for i in range(1, count) if given[i] < largest] or [i for i in range(1, count) if given[i] < bound]
        pool, left = sum([weights[i] for i in movable]), spare
        for i in movable:
            addition = min(bound - given[i], max(1, left * weights[i] // pool), spare)
            given[i] = given[i] + addition
            spare = spare - addition
    return np.array(given)


def centred(stream_key, shape, spread, most, shards=(), kind=jnp.bfloat16):
    drawn = spread * jax.random.normal(stream_key, shape, jnp.float32)
    if shards:
        drawn = drawn * block_levels(stream_key, shape, shards, -0.22, 0.18)
    return jnp.clip(drawn, -most, most).astype(kind)


def setup_inputs(seed: int = 0) -> dict:
    arg_keys = jax.random.split(jax.random.key(seed), 9)
    particles = centred(arg_keys[0], (P_ALL, 2 * A * R), 1.0, 6.0, ((0, 128),))
    references = centred(arg_keys[1], (CLASSES, 2 * A * R), (2 * A * R) ** -0.5, 0.0625, ((0, 8), (1, 16)))
    owner_keys = jax.random.split(jax.random.fold_in(arg_keys[2], 1), P_ALL // P_DEV)
    owner_turns = jax.random.permutation(jax.random.fold_in(arg_keys[2], 3), P_ALL // P_DEV)
    owner = jax.vmap(lambda own, number: shared_out(jax.random.fold_in(arg_keys[2], 2), own, number, P_DEV, N_CLS, 1, CAP, 1))(owner_keys, owner_turns).reshape((P_ALL, 1))
    class_offset = with_ends(jax.random.randint(arg_keys[3], (P_ALL,), 0, CPD), jax.random.fold_in(arg_keys[3], 1), 0, CPD - 1).astype(jnp.int32)
    rotation = with_ends(jax.random.randint(arg_keys[4], (P_ALL,), 0, A), jax.random.fold_in(arg_keys[4], 1), 0, A - 1).astype(jnp.int32)
    shifts = with_ends(jax.random.randint(arg_keys[5], (P_ALL, 2), 0 - SHIFT, SHIFT + 1), jax.random.fold_in(arg_keys[5], 1), 0 - SHIFT, SHIFT).astype(jnp.int32)
    ctf_group = draw_ctf_group(jax.random.fold_in(arg_keys[8], 71), 0)
    ctf_table = draw_ctf_table(jax.random.fold_in(arg_keys[8], 71), 0)
    return {"particles": particles, "references": references, "owner": owner, "class_offset": class_offset, "rotation": rotation, "shifts": shifts, "ctf_group": ctf_group, "ctf_table": ctf_table}


tau_reg = 1.0


def angle_tables(angles):
    index_grid = (jnp.arange(angles, dtype=jnp.int32)[:, None] * jnp.arange(angles, dtype=jnp.int32)[None, :]) % angles
    turn_grid = 2.0 * math.pi * index_grid.astype(jnp.float32) / angles
    cosine = jnp.cos(turn_grid)
    sine_part = jnp.sin(turn_grid)
    forward = jnp.concatenate([cosine, -sine_part], axis=0).astype(jnp.bfloat16)
    inverse = (jnp.concatenate([cosine, -sine_part], axis=1) / angles).astype(jnp.bfloat16)
    return forward, inverse


def prepare(particle_rows, shift_rows, group_rows, ctf_table):
    count_rows = particle_rows.shape[0]
    cycle_count = ctf_table.shape[1]
    angles = particle_rows.shape[1] // (2 * cycle_count)
    values_in = particle_rows.reshape(count_rows, angles, 2, cycle_count).astype(jnp.float32)
    angle_grid = 2.0 * math.pi * jnp.arange(angles, dtype=jnp.float32) / angles
    radius = jnp.arange(1, cycle_count + 1, dtype=jnp.float32)
    freq_x = jnp.cos(angle_grid)[:, None] * radius[None, :]
    freq_y = jnp.sin(angle_grid)[:, None] * radius[None, :]
    move_x = shift_rows[:, 0].astype(jnp.float32)[:, None, None]
    move_y = shift_rows[:, 1].astype(jnp.float32)[:, None, None]
    phase_grid = 2.0 * math.pi * (move_x * freq_x[None] + move_y * freq_y[None]) / BOX
    cosine = jnp.cos(phase_grid)
    sine_part = jnp.sin(phase_grid)
    selector = (group_rows[:, None] == jnp.arange(ctf_table.shape[0], dtype=jnp.int32)[None, :]).astype(jnp.float32)
    ctf_rows = jnp.dot(selector, ctf_table, precision=lax.Precision.HIGHEST, preferred_element_type=jnp.float32)
    real_in = values_in[:, :, 0, :]
    imag_in = values_in[:, :, 1, :]
    real_out = (real_in * cosine - imag_in * sine_part) * ctf_rows[:, None, :]
    imag_out = (real_in * sine_part + imag_in * cosine) * ctf_rows[:, None, :]
    weighted = jnp.stack([real_out, imag_out], axis=2).reshape(count_rows, angles * 2 * cycle_count)
    return weighted.astype(jnp.bfloat16), ctf_rows


def spectra_of(flat_rows, forward, cycle_count):
    angles = forward.shape[1]
    shaped = flat_rows.reshape(flat_rows.shape[0], angles, 2 * cycle_count)
    spectra = jnp.einsum('ja,nac->jnc', forward.astype(jnp.float32), shaped.astype(jnp.float32),
                         precision=lax.Precision.HIGHEST).astype(jnp.bfloat16)
    return jnp.concatenate([spectra[:angles], spectra[angles:]], axis=2)


def paired(ref_spectra, cycle_count):
    half_width = 2 * cycle_count
    swapped = jnp.concatenate([-ref_spectra[:, :, half_width:], ref_spectra[:, :, :half_width]], axis=2)
    return jnp.concatenate([ref_spectra, swapped], axis=1)


def best_scores(part_spectra, ref_pairs, inverse):
    angles = part_spectra.shape[0]
    count_rows = part_spectra.shape[1]
    classes = ref_pairs.shape[1] // 2
    cross_terms = jnp.einsum('mnc,mkc->mnk', part_spectra.astype(jnp.float32), ref_pairs.astype(jnp.float32),
                             precision=lax.Precision.HIGHEST).astype(jnp.bfloat16)
    stacked = jnp.concatenate([cross_terms[:, :, :classes].reshape(angles, count_rows * classes),
                               cross_terms[:, :, classes:].reshape(angles, count_rows * classes)], axis=0)
    correlation = jnp.dot(inverse, stacked, preferred_element_type=jnp.float32)
    return jnp.max(correlation.reshape(angles, count_rows, classes), axis=(0, 2))


def rotate_back(weighted, rotation_rows, cycle_count):
    angles = weighted.shape[1] // (2 * cycle_count)
    shaped = weighted.reshape(weighted.shape[0], angles, 2 * cycle_count)
    doubled = jnp.concatenate([shaped, shaped], axis=1)

    def one_row(row_block, start):
        return lax.dynamic_slice_in_dim(row_block, start.astype(jnp.int32), angles, 0)

    turned = jax.vmap(one_row)(doubled, rotation_rows.astype(jnp.int32))
    return turned.reshape(weighted.shape)


def weight_columns(weights, angles):
    return jnp.tile(jnp.concatenate([weights, weights], axis=1), (1, angles))


def reference(particles, references, owner, class_offset, rotation, shifts, ctf_group, ctf_table):
    forward, inverse = angle_tables(A)
    ref_pairs = paired(spectra_of(references, forward, R), R)
    class_index = owner[:, 0] * CPD + class_offset
    blocks = P_ALL // P_DEV

    def block_step(totals, pieces):
        sums_now, weights_now = totals
        rows_in, shift_in, group_in, rotation_in, class_in = pieces
        weighted, ctf_rows = prepare(rows_in, shift_in, group_in, ctf_table)
        scores = best_scores(spectra_of(weighted, forward, R), ref_pairs, inverse)
        contrib = rotate_back(weighted, rotation_in, R)
        selector = class_in[:, None] == jnp.arange(CLASSES, dtype=jnp.int32)[None, :]
        sums_now = sums_now + jnp.dot(selector.astype(jnp.bfloat16).T, contrib, preferred_element_type=jnp.float32)
        weights_now = weights_now + jnp.dot(selector.astype(jnp.float32).T, ctf_rows * ctf_rows,
                                            precision=lax.Precision.HIGHEST, preferred_element_type=jnp.float32)
        return (sums_now, weights_now), scores

    sequence = (particles.reshape(blocks, P_DEV, 2 * A * R), shifts.reshape(blocks, P_DEV, 2),
                ctf_group.reshape(blocks, P_DEV), rotation.reshape(blocks, P_DEV), class_index.reshape(blocks, P_DEV))
    start_values = (jnp.zeros((CLASSES, 2 * A * R), jnp.float32), jnp.zeros((CLASSES, R), jnp.float32))
    (class_sums, weights), scores = lax.scan(block_step, start_values, sequence)
    new_references = class_sums / (weight_columns(weights, A) + tau_reg)
    return scores.reshape(P_ALL), new_references
```

```python
import math

import jax
import jax.numpy as jnp
import numpy as np
from jax import lax
from jax.experimental import pallas as pl
from jax.experimental.pallas import tpu as pltpu
from jax.sharding import PartitionSpec as P

A = 72
M = 37
R = 64
BOX = 128
TAU = 1.0
AXES = ("dom", "cls")
BF = jnp.bfloat16
F32 = jnp.float32
VMEM_LIMIT = 56 * 1024 * 1024
K_INV = 640


def tables():
    m = np.arange(M)[:, None]
    a = np.arange(A)[None, :]
    turn = 2.0 * np.pi * ((m * a) % A) / A
    fwd = np.stack([np.cos(turn), -np.sin(turn)], axis=1).reshape(2 * M, A)
    gain = np.where((np.arange(M) == 0) | (np.arange(M) == A // 2), 1.0, 2.0)[:, None]
    inv = np.stack([np.cos(turn) / A, -np.sin(turn) / A], axis=1).astype(BF).astype(np.float32)
    inv = (inv * gain[:, None, :]).reshape(2 * M, A).T
    eye = np.eye(8, dtype=np.float32)
    fwd_k = np.kron(fwd.astype(np.float32), eye).astype(BF)
    inv_k = np.zeros((A * 8, K_INV), np.float32)
    inv_k[:, : 2 * M * 8] = np.kron(inv, eye)
    return fwd_k, inv_k.astype(BF)


def freq_tables():
    angle = 2.0 * np.pi * np.arange(A // 2) / A
    radius = np.tile(np.arange(1, R + 1), 2)
    fx = np.cos(angle)[:, None] * radius[None, :] / BOX
    fy = np.sin(angle)[:, None] * radius[None, :] / BOX
    return fx.astype(np.float32), fy.astype(np.float32)


def cos_poly():
    n = 8
    nodes = (np.cos((np.arange(64) + 0.5) * np.pi / 64) + 1.0) / 8.0
    return [float(c) for c in np.polynomial.chebyshev.Chebyshev.fit(
        nodes, np.cos(2.0 * np.pi * np.sqrt(nodes)), n - 1, domain=[0.0, 0.25]
    ).convert(kind=np.polynomial.Polynomial).coef]


COEF = cos_poly()


def prep_kernel(sc, x_ref, aux_ref, ctf_ref, fx_ref, fy_ref, w_ref, c0, c1, c2, c3, ws, us):
    sx = aux_ref[:, 0:1].astype(F32)
    sy = aux_ref[:, 1:2].astype(F32)
    rot = aux_ref[:, 2:3]
    second = aux_ref[:, 3:4] > 0
    lane = lax.broadcasted_iota(jnp.int32, (16, 128), 1)
    left = lane < R
    shift = jnp.where(left, 0.0, -0.25).astype(F32)
    sxb = jnp.broadcast_to(sx, (16, 128))
    syb = jnp.broadcast_to(sy, (16, 128))
    ctf = jnp.where(second, ctf_ref[1:2, :], ctf_ref[0:1, :])
    ctf_s = jnp.where(left, -ctf, ctf)
    for b in range(A // 4):
        done = []
        for a in (2 * b, 2 * b + 1):
            u = sxb * fx_ref[a : a + 1, :] + syb * fy_ref[a : a + 1, :]
            v = (u - jnp.round(u)) + shift
            v = v - jnp.round(v)
            q = v * v
            e = jnp.full_like(q, COEF[-1])
            for k in COEF[-2::-1]:
                e = e * q + k
            er = pltpu.roll(e, R, 1)
            cc = jnp.where(left, e, er) * ctf
            ss = jnp.where(left, er, e) * ctf_s
            x0 = x_ref[:, a * 128 : (a + 1) * 128].astype(F32)
            h = a + A // 2
            x1 = x_ref[:, h * 128 : (h + 1) * 128].astype(F32)
            w0 = x0 * cc + pltpu.roll(x0, R, 1) * ss
            w1 = x1 * cc - pltpu.roll(x1, R, 1) * ss
            ws[:, a * 128 : (a + 1) * 128] = w0
            ws[:, h * 128 : (h + 1) * 128] = w1
            done.append((w0, w1))
        for half in (0, 1):
            row = (2 * b + half * (A // 2)) * 8
            for g in (0, 1):
                w_ref[g, row : row + 16, :] = jnp.concatenate(
                    [done[0][half][8 * g : 8 * g + 8], done[1][half][8 * g : 8 * g + 8]], axis=0
                ).astype(BF)
    rotb = jnp.broadcast_to(rot, (16, 128))
    bit = [(rotb & (1 << k)) != 0 for k in range(7)]
    for r in range(8):
        t = [ws[:, (r + 8 * n) * 128 : (r + 8 * n + 1) * 128] for n in range(9)]
        for k in range(4):
            t = [jnp.where(bit[3 + k], t[(n + (1 << k)) % 9], t[n]) for n in range(9)]
        for n in range(9):
            us[:, (r + 8 * n) * 128 : (r + 8 * n + 1) * 128] = t[n]
    for j0 in range(0, A, 8):
        t = [us[:, ((j0 + i) % A) * 128 : ((j0 + i) % A + 1) * 128] for i in range(15)]
        t = [jnp.where(bit[0], t[i + 1], t[i]) for i in range(14)]
        t = [jnp.where(bit[1], t[i + 2], t[i]) for i in range(12)]
        for i in range(8):
            ws[:, (j0 + i) * 128 : (j0 + i + 1) * 128] = jnp.where(bit[2], t[i + 4], t[i])
    meta = jnp.where(lane == 0, aux_ref[:, 4:5], jnp.where(lane == 1, aux_ref[:, 5:6], 0))
    meta = meta.astype(F32).astype(BF)
    width = 18 * 128
    for dy, c_ref in enumerate((c0, c1, c2, c3)):
        dest = lax.rem(sc[0] + dy, 4)
        start = pl.multiple_of(dest * width, 128)
        c_ref[:, 0:width] = ws[:, pl.ds(start, width)].astype(BF)
        c_ref[:, width : width + 128] = meta


def prep(sc, particles, aux, ctf2, fx, fy):
    n = particles.shape[0]
    full = lambda i, s: (0, 0)
    block = lambda i, s: (i, 0)
    return pl.pallas_call(
        prep_kernel,
        grid_spec=pltpu.PrefetchScalarGridSpec(
            num_scalar_prefetch=1,
            grid=(n // 16,),
            in_specs=[
                pl.BlockSpec((16, A * 128), block),
                pl.BlockSpec((16, 8), block),
                pl.BlockSpec((2, 128), full),
                pl.BlockSpec((A // 2, 128), full),
                pl.BlockSpec((A // 2, 128), full),
            ],
            out_specs=[pl.BlockSpec((2, A * 8, 128), lambda i, s: (i, 0, 0))]
            + [pl.BlockSpec((16, 19 * 128), block)] * 4,
            scratch_shapes=[pltpu.VMEM((16, A * 128), F32), pltpu.VMEM((16, A * 128), F32)],
        ),
        out_shape=[jax.ShapeDtypeStruct((n // 8, A * 8, 128), BF)]
        + [jax.ShapeDtypeStruct((n, 19 * 128), BF)] * 4,
        compiler_params=pltpu.CompilerParams(vmem_limit_bytes=VMEM_LIMIT),
        cost_estimate=pl.CostEstimate(flops=40_000_000, bytes_accessed=8_000_000, transcendentals=0),
        name="prep",
    )(sc, particles, aux, ctf2, fx, fy)


def spread(out, dst, rows):
    for m in range(M):
        for i in range(2):
            r = 16 * m + 8 * i
            dst[m, rows, 128 * i : 128 * i + 128] = jnp.concatenate(
                [out[r : r + 8, 0:128], out[r : r + 8, 128:256]], axis=0
            ).astype(BF)


def spectra_kernel(w_ref, f_ref, p_ref):
    g = pl.program_id(0)
    y = jnp.concatenate([w_ref[0], w_ref[1]], axis=1)
    out = jnp.dot(f_ref[...], y, preferred_element_type=F32)
    spread(out, p_ref, pl.ds(0, 16))


def spectra(w, fwd_k):
    n = w.shape[0] * 8
    return pl.pallas_call(
        spectra_kernel,
        grid=(n // 16,),
        in_specs=[
            pl.BlockSpec((2, A * 8, 128), lambda i: (i, 0, 0)),
            pl.BlockSpec((2 * M * 8, A * 8), lambda i: (0, 0)),
        ],
        out_specs=pl.BlockSpec((M, 16, 256), lambda i: (0, i, 0)),
        out_shape=jax.ShapeDtypeStruct((M, n, 256), BF),
        compiler_params=pltpu.CompilerParams(vmem_limit_bytes=VMEM_LIMIT),
        cost_estimate=pl.CostEstimate(flops=2_000_000_000, bytes_accessed=5_000_000, transcendentals=0),
        name="spectra",
    )(w, fwd_k)


def ref_kernel(sc, b0, b1, b2, b3, f_ref, r_ref, s):
    for dy, b in enumerate((b0, b1, b2, b3)):
        src = lax.rem(sc[0] + 4 - dy, 4)
        for xh in range(2):
            for t in range(9):
                v = b[xh, :, t * 128 : (t + 1) * 128].astype(F32)
                row = pl.multiple_of((src * 2 + xh) * 72 + 8 * t, 8)
                s[pl.ds(row, 8), 0:128] = v[0:8]
                s[pl.ds(row, 8), 128:256] = v[8:16]
    out = jnp.dot(f_ref[...], s[...].astype(BF), preferred_element_type=F32)
    spread(out, r_ref, pl.ds(0, 16))


def ref_spectra(sc, blocks, fwd_k):
    v = pl.BlockSpec(memory_space=pltpu.VMEM)
    return pl.pallas_call(
        ref_kernel,
        in_specs=[pl.BlockSpec(memory_space=pltpu.SMEM)] + [v] * 5,
        out_specs=v,
        out_shape=jax.ShapeDtypeStruct((M, 16, 256), BF),
        scratch_shapes=[pltpu.VMEM((A * 8, 256), F32)],
        compiler_params=pltpu.CompilerParams(vmem_limit_bytes=VMEM_LIMIT),
        cost_estimate=pl.CostEstimate(flops=200_000_000, bytes_accessed=1_500_000, transcendentals=0),
        name="ref_spectra",
    )(sc, *blocks, fwd_k)


def score_kernel(p_ref, r0, r1, r2, r3, r4, r5, r6, r7, inv_ref, o_ref, xs, mx):
    blocks = (r0, r1, r2, r3, r4, r5, r6, r7)
    xs[:, 2 * M * 8 :, :] = jnp.zeros((16, K_INV - 2 * M * 8, 256), BF)

    @pl.loop(0, M)
    def _(m):
        p = p_ref[m]
        re, im = p[:, 0:128], p[:, 128:256]
        lhs = jnp.concatenate([p, jnp.concatenate([im, -re], axis=1)], axis=0)
        rhs = jnp.concatenate([b[i, m] for b in blocks for i in range(2)], axis=0)
        x = lax.dot_general(lhs, rhs, (((1,), (1,)), ((), ())), preferred_element_type=F32)
        row = pl.multiple_of(m * 16, 16)
        for g in range(16):
            xs[g, pl.ds(row, 16), :] = jnp.concatenate(
                [x[8 * g : 8 * g + 8], x[128 + 8 * g : 136 + 8 * g]], axis=0
            ).astype(BF)

    @pl.loop(0, 16)
    def _(g):
        y = jnp.dot(inv_ref[...], xs[g], preferred_element_type=F32)
        best = y[0:8]
        for t in range(1, A):
            best = jnp.maximum(best, y[8 * t : 8 * t + 8])
        mx[pl.ds(pl.multiple_of(g * 8, 8), 8), :] = best

    o_ref[...] = jnp.max(mx[...], axis=1, keepdims=True)


def scores_of(p, blocks, inv_k):
    n = p.shape[1]
    v = pl.BlockSpec(memory_space=pltpu.VMEM)
    return pl.pallas_call(
        score_kernel,
        in_specs=[v] * 10,
        out_specs=v,
        out_shape=jax.ShapeDtypeStruct((n, 1), F32),
        scratch_shapes=[pltpu.VMEM((16, K_INV, 256), BF), pltpu.VMEM((n, 256), F32)],
        compiler_params=pltpu.CompilerParams(vmem_limit_bytes=VMEM_LIMIT),
        cost_estimate=pl.CostEstimate(flops=6_000_000_000, bytes_accessed=8_000_000, transcendentals=0),
        name="scores",
    )(p, *blocks, inv_k)


def sums_kernel(sc, c0, c1, c2, c3, tab_ref, mine, other, acc):
    width = 18 * 128
    lane = lax.broadcasted_iota(jnp.int32, (128, 256), 1).astype(F32)
    picks, groups = [], []
    for c in (c0, c1, c2, c3):
        meta = c[:, width : width + 128].astype(F32)
        picks.append(jnp.where(lane == meta[:, 0:1], 1.0, 0.0).astype(F32).T.astype(BF))
        groups.append(jnp.where(lane == meta[:, 1:2], 1.0, 0.0).astype(BF))
    pick = jnp.concatenate(picks, axis=1)
    group = jnp.concatenate(groups, axis=0)
    count = jnp.dot(pick, group, preferred_element_type=F32)
    tab = tab_ref[...]
    wsum = jnp.dot(count, tab * tab, precision=lax.Precision.HIGHEST, preferred_element_type=F32)
    for t in range(9):
        cols = slice(256 * t, 256 * t + 256)
        x = jnp.concatenate([c[:, cols] for c in (c0, c1, c2, c3)], axis=0)
        acc[:, cols] = jnp.dot(pick, x, preferred_element_type=F32)
    left = lax.broadcasted_iota(jnp.int32, (256, 128), 1) < R
    for ref, core in ((mine, sc[2]), (other, 1 - sc[2])):
        for xh in range(2):
            start = pl.multiple_of((9 * xh + 4 * core) * 128, 128)
            ref[xh] = acc[:, pl.ds(start, 640)]
            mid = acc[:, (9 * xh + 4) * 128 : (9 * xh + 5) * 128]
            keep = jnp.logical_xor(left, core == 1)
            ref[xh, :, pl.ds(pl.multiple_of((1 - core) * 512, 128), 128)] = jnp.where(keep, mid, wsum)


def class_sums(sc, cs, tab):
    v = pl.BlockSpec(memory_space=pltpu.VMEM)
    shape = jax.ShapeDtypeStruct((2, 256, 640), F32)
    return pl.pallas_call(
        sums_kernel,
        in_specs=[pl.BlockSpec(memory_space=pltpu.SMEM)] + [v] * 5,
        out_specs=[v, v],
        out_shape=[shape, shape],
        scratch_shapes=[pltpu.VMEM((256, 18 * 128), F32)],
        compiler_params=pltpu.CompilerParams(vmem_limit_bytes=VMEM_LIMIT),
        cost_estimate=pl.CostEstimate(flops=700_000_000, bytes_accessed=5_000_000, transcendentals=0),
        name="class_sums",
    )(sc, *cs, tab)


def cut_x_kernel(sc, a_ref, b_ref, o0, o1, o2, o3):
    for dx, o in enumerate((o0, o1, o2, o3)):
        x = lax.rem(sc[1] + dx, 4)
        xh, xl = x // 2, lax.rem(x, 2)
        rows = pl.ds(pl.multiple_of(xl * 128, 128), 128)
        o[...] = a_ref[xh, rows, :] + b_ref[xh, rows, :]


def cut_x(sc, a, b):
    v = pl.BlockSpec(memory_space=pltpu.VMEM)
    return pl.pallas_call(
        cut_x_kernel,
        in_specs=[pl.BlockSpec(memory_space=pltpu.SMEM), v, v],
        out_specs=[v] * 4,
        out_shape=[jax.ShapeDtypeStruct((128, 640), F32)] * 4,
        compiler_params=pltpu.CompilerParams(vmem_limit_bytes=VMEM_LIMIT),
        cost_estimate=pl.CostEstimate(flops=400_000, bytes_accessed=3_900_000, transcendentals=0),
        name="cut_x",
    )(sc, a, b)


def cut_z_kernel(sc, a0, a1, a2, a3, o0, o1, o2, o3):
    for dz, o in enumerate((o0, o1, o2, o3)):
        z = lax.rem(sc[3] + dz, 4)
        rows = pl.ds(pl.multiple_of(z * 32, 32), 32)
        o[...] = (a0[rows, :] + a1[rows, :]) + (a2[rows, :] + a3[rows, :])


def cut_z(sc, parts):
    v = pl.BlockSpec(memory_space=pltpu.VMEM)
    return pl.pallas_call(
        cut_z_kernel,
        in_specs=[pl.BlockSpec(memory_space=pltpu.SMEM)] + [v] * 4,
        out_specs=[v] * 4,
        out_shape=[jax.ShapeDtypeStruct((32, 640), F32)] * 4,
        compiler_params=pltpu.CompilerParams(vmem_limit_bytes=VMEM_LIMIT),
        cost_estimate=pl.CostEstimate(flops=400_000, bytes_accessed=1_700_000, transcendentals=0),
        name="cut_z",
    )(sc, *parts)


def final_kernel(sc, a0, a1, a2, a3, o_ref):
    s = (a0[...] + a1[...]) + (a2[...] + a3[...])
    odd = sc[2] == 1
    left = lax.broadcasted_iota(jnp.int32, (32, 128), 1) < R
    tile = [s[:, 128 * t : 128 * t + 128] for t in range(5)]
    held = jnp.where(odd, tile[0], tile[4])
    turned = pltpu.roll(held, R, 1)
    weight = jnp.where(jnp.logical_xor(left, odd), turned, held)
    tile = [t / (weight + TAU) for t in tile]
    rolled = [pltpu.roll(t, R, 1) for t in tile]
    later = [jnp.where(left, rolled[t], rolled[t + 1]) for t in range(4)] + [rolled[4]]
    for t in range(4):
        o_ref[:, 128 * t : 128 * t + 128] = jnp.where(odd, later[t], tile[t])[0:25]
    o_ref[:, 512:576] = jnp.where(odd, later[4], tile[4])[0:25, 0:R]


def final(sc, parts):
    v = pl.BlockSpec(memory_space=pltpu.VMEM)
    return pl.pallas_call(
        final_kernel,
        in_specs=[pl.BlockSpec(memory_space=pltpu.SMEM)] + [v] * 4,
        out_specs=v,
        out_shape=jax.ShapeDtypeStruct((25, 576), F32),
        name="final",
    )(sc, *parts)


def place(y, x, z, core):
    return ((y % 4) * 4 + (x % 4) // 2 * 2 + core % 2) * 8 + (x % 2) * 4 + z % 4


def permutation(move):
    return [
        (place(y, x, z, c), place(*move(y, x, z, c)))
        for y in range(4)
        for x in range(4)
        for z in range(4)
        for c in range(2)
    ]


CORE = permutation(lambda y, x, z, c: (y, x, z, c + 1))
HIGH = permutation(lambda y, x, z, c: (y, x + 2, z, c))
LOW = permutation(lambda y, x, z, c: (y, x ^ 1, z, c))
YS = [permutation(lambda y, x, z, c, d=d: (y + d, x, z, c)) for d in range(4)]
XS = [permutation(lambda y, x, z, c, d=d: (y, x + d, z, c)) for d in range(4)]
ZS = [permutation(lambda y, x, z, c, d=d: (y, x, z + d, c)) for d in range(4)]


def move(value, pairs):
    return lax.ppermute(value, AXES, pairs)


def per_device(particles, references, owner, class_offset, rotation, shifts, ctf_group, ctf_table):
    fwd_np, inv_np = tables()
    fwd_k, inv_k = jnp.asarray(fwd_np), jnp.asarray(inv_np)
    fx, fy = (jnp.asarray(t) for t in freq_tables())
    dom, cls = lax.axis_index("dom"), lax.axis_index("cls")
    y, xh, core = dom // 4, dom // 2 % 2, dom % 2
    xl, z = cls // 4, cls % 4
    sc = jnp.stack([y, xh * 2 + xl, core, z]).astype(jnp.int32)

    low, high = references[0:16], references[9:25]
    first = core == 0
    keep = jnp.where(first, low, high)
    give = jnp.where(first, high, low)
    got = move(give, CORE)
    block = jnp.where(
        first, jnp.concatenate([keep, got], axis=1), jnp.concatenate([got, keep], axis=1)
    )
    far = move(block, HIGH)
    lower = xh == 0
    pair = jnp.stack([jnp.where(lower, block, far), jnp.where(lower, far, block)])
    blocks = [pair] + [move(pair, YS[d]) for d in (1, 2, 3)]

    first_group = 2 * (dom * 8 + cls)
    rows = lax.dynamic_slice_in_dim(ctf_table, first_group, 2, 0)
    ctf2 = jnp.concatenate([rows, rows], axis=1)
    zero = jnp.zeros_like(rotation)
    aux = jnp.stack(
        [
            shifts[:, 0],
            shifts[:, 1],
            rotation,
            ctf_group - first_group,
            owner[:, 0] * 32 + class_offset,
            ctf_group,
            zero,
            zero,
        ],
        axis=1,
    )
    weighted, *sent = prep(sc, particles, aux, ctf2, fx, fy)
    held = [sent[0]] + [move(sent[d], YS[d]) for d in (1, 2, 3)]
    part = spectra(weighted, fwd_k)

    own = ref_spectra(sc, blocks, fwd_k)
    both = jnp.stack([own, move(own, LOW)])
    line = [both] + [move(both, ZS[d]) for d in (1, 2, 3)]
    line = line + [move(b, CORE) for b in line]
    scores = scores_of(part, line, inv_k)[:, 0]

    tab = jnp.concatenate([ctf_table, ctf_table], axis=1)
    mine, other = class_sums(sc, held, tab)
    cut = cut_x(sc, mine, move(other, CORE))
    cut = [cut[0]] + [move(cut[d], XS[d]) for d in (1, 2, 3)]
    cut = cut_z(sc, cut)
    cut = [cut[0]] + [move(cut[d], ZS[d]) for d in (1, 2, 3)]
    return scores, final(sc, cut)


def solution(mesh):
    return jax.shard_map(
        per_device,
        mesh=mesh,
        in_specs=(
            P(("dom", "cls"), None),
            P("cls", "dom"),
            P(("dom", "cls"), None),
            P(("dom", "cls")),
            P(("dom", "cls")),
            P(("dom", "cls"), None),
            P(("dom", "cls")),
            P(),
        ),
        out_specs=(P(("dom", "cls")), P("cls", "dom")),
        check_vma=False,
    )
```

```python
import functools

import jax
import jax.numpy as jnp
import numpy as np
from jax import lax
from jax.experimental import pallas as pl
from jax.experimental.pallas import tpu as pltpu
from jax.sharding import PartitionSpec as P

A = 72
M = 37
R = 64
BOX = 128
TAU = 1.0
AXES = ("dom", "cls")
BF = jnp.bfloat16
F32 = jnp.float32
MIB = 1024 * 1024
VMEM_LIMIT = 16 * MIB
K_INV = 640


def tables():
    m = np.arange(M)[:, None]
    a = np.arange(A)[None, :]
    turn = 2.0 * np.pi * ((m * a) % A) / A
    fwd = np.stack([np.cos(turn), -np.sin(turn)], axis=1).reshape(2 * M, A)
    gain = np.where((np.arange(M) == 0) | (np.arange(M) == A // 2), 1.0, 2.0)[:, None]
    inv = np.stack([np.cos(turn) / A, -np.sin(turn) / A], axis=1).astype(BF).astype(np.float32)
    inv = (inv * gain[:, None, :]).reshape(2 * M, A).T
    eye = np.eye(8, dtype=np.float32)
    fwd_k = np.kron(fwd.astype(np.float32), eye).astype(BF)
    inv_k = np.zeros((A * 8, K_INV), np.float32)
    inv_k[:, : 2 * M * 8] = np.kron(inv, eye)
    return fwd_k, inv_k.astype(BF)


def freq_tables():
    angle = 2.0 * np.pi * np.arange(A // 2) / A
    radius = np.tile(np.arange(1, R + 1), 2)
    fx = np.cos(angle)[:, None] * radius[None, :] / BOX
    fy = np.sin(angle)[:, None] * radius[None, :] / BOX
    return fx.astype(np.float32), fy.astype(np.float32)


def cos_poly():
    n = 7
    nodes = (np.cos((np.arange(64) + 0.5) * np.pi / 64) + 1.0) / 8.0
    return [float(c) for c in np.polynomial.chebyshev.Chebyshev.fit(
        nodes, np.cos(2.0 * np.pi * np.sqrt(nodes)), n - 1, domain=[0.0, 0.25]
    ).convert(kind=np.polynomial.Polynomial).coef]


COEF = cos_poly()


def prep_kernel(first, x_ref, shift_ref, rot_ref, own_ref, off_ref, grp_ref, tab_ref, fx_ref, fy_ref, *refs):
    w_ref, c0, c1, c2, c3, ws, us, aux, tab = refs[-9:]
    dom, cls = lax.axis_index("dom"), lax.axis_index("cls")
    mine = 2 * (dom * 8 + cls)
    step = pl.program_id(0)

    @pl.when(step == 0)
    def _():
        shift_rows = shift_ref[...].astype(F32)
        group = grp_ref[...]
        rows = [
            shift_rows,
            rot_ref[...].astype(F32),
            (group - mine).astype(F32),
            (own_ref[...] * 32 + off_ref[...]).astype(F32),
            group.astype(F32),
            jnp.zeros((122, 128), F32),
        ]
        aux[...] = jnp.concatenate(rows, axis=0).T
        flipped = tab_ref[...].T
        tab[...] = jnp.concatenate([flipped, flipped], axis=1)

    here = aux[pl.ds(pl.multiple_of((step + first) * 16, 16), 16), :]
    lane = lax.broadcasted_iota(jnp.int32, (16, 128), 1)
    left = lane < R
    shift = jnp.where(left, 0.0, -0.25).astype(F32)
    sxb = jnp.broadcast_to(here[:, 0:1], (16, 128))
    syb = jnp.broadcast_to(here[:, 1:2], (16, 128))
    ctf = jnp.where(here[:, 3:4] > 0.5, tab[pl.ds(mine + 1, 1), :], tab[pl.ds(mine, 1), :])
    ctf_s = jnp.where(left, -ctf, ctf)
    for b in range(A // 4):
        done = []
        for a in (2 * b, 2 * b + 1):
            v = (sxb * fx_ref[a : a + 1, :] + syb * fy_ref[a : a + 1, :]) + shift
            v = v - jnp.round(v)
            q = v * v
            e = jnp.full_like(q, COEF[-1])
            for k in COEF[-2::-1]:
                e = e * q + k
            er = pltpu.roll(e, R, 1)
            cc = jnp.where(left, e, er) * ctf
            ss = jnp.where(left, er, e) * ctf_s
            x0 = x_ref[:, a * 128 : (a + 1) * 128].astype(F32)
            h = a + A // 2
            x1 = x_ref[:, h * 128 : (h + 1) * 128].astype(F32)
            w0 = x0 * cc + pltpu.roll(x0, R, 1) * ss
            w1 = x1 * cc - pltpu.roll(x1, R, 1) * ss
            ws[:, a * 128 : (a + 1) * 128] = w0
            ws[:, h * 128 : (h + 1) * 128] = w1
            done.append((w0, w1))
        for half in (0, 1):
            row = (2 * b + half * (A // 2)) * 8
            for g in (0, 1):
                w_ref[g, row : row + 16, :] = jnp.concatenate(
                    [done[0][half][8 * g : 8 * g + 8], done[1][half][8 * g : 8 * g + 8]], axis=0
                ).astype(BF)
    rotb = jnp.broadcast_to(here[:, 2:3], (16, 128)).astype(jnp.int32)
    bit = [(rotb & (1 << k)) != 0 for k in range(7)]
    for r in range(8):
        t = [ws[:, (r + 8 * n) * 128 : (r + 8 * n + 1) * 128] for n in range(9)]
        for k in range(4):
            t = [jnp.where(bit[3 + k], t[(n + (1 << k)) % 9], t[n]) for n in range(9)]
        for n in range(9):
            us[:, (r + 8 * n) * 128 : (r + 8 * n + 1) * 128] = t[n]
    for j0 in range(0, A, 8):
        t = [us[:, ((j0 + i) % A) * 128 : ((j0 + i) % A + 1) * 128] for i in range(15)]
        t = [jnp.where(bit[0], t[i + 1], t[i]) for i in range(14)]
        t = [jnp.where(bit[1], t[i + 2], t[i]) for i in range(12)]
        for i in range(8):
            ws[:, (j0 + i) * 128 : (j0 + i + 1) * 128] = jnp.where(bit[2], t[i + 4], t[i])
    meta = jnp.where(lane == 0, here[:, 4:5], jnp.where(lane == 1, here[:, 5:6], 0.0)).astype(BF)
    width = 18 * 128
    for dy, c_ref in enumerate((c0, c1, c2, c3)):
        dest = lax.rem(dom // 4 + dy, 4)
        start = pl.multiple_of(dest * width, 128)
        c_ref[:, 0:width] = ws[:, pl.ds(start, width)].astype(BF)
        c_ref[:, width : width + 128] = meta


def prep(particles, rows, table, fx, fy, first, steps, held=None):
    n = particles.shape[0]
    whole = lambda a: pl.BlockSpec(a.shape, lambda i: (0,) * a.ndim)
    block = lambda i: (i + first, 0)
    args = [particles, *rows, table, fx, fy]
    specs = [pl.BlockSpec((16, A * 128), block)] + [whole(a) for a in args[1:]]
    alias = {}
    if held is not None:
        alias = {len(args) + i: i for i in range(5)}
        args += held
        specs += [pl.BlockSpec(memory_space=pl.ANY)] * 5
    return pl.pallas_call(
        functools.partial(prep_kernel, first),
        grid=(steps,),
        in_specs=specs,
        out_specs=[pl.BlockSpec((2, A * 8, 128), lambda i: (i + first, 0, 0))]
        + [pl.BlockSpec((16, 19 * 128), block)] * 4,
        scratch_shapes=[
            pltpu.VMEM((16, A * 128), F32),
            pltpu.VMEM((16, A * 128), F32),
            pltpu.VMEM((128, 128), F32),
            pltpu.VMEM((256, 128), F32),
        ],
        out_shape=[jax.ShapeDtypeStruct((n // 8, A * 8, 128), BF)]
        + [jax.ShapeDtypeStruct((n, 19 * 128), BF)] * 4,
        input_output_aliases=alias,
        compiler_params=pltpu.CompilerParams(vmem_limit_bytes=8 * MIB),
        cost_estimate=pl.CostEstimate(
            flops=5_000_000 * steps, bytes_accessed=1_000_000 * steps, transcendentals=0
        ),
        name="prep",
    )(*args)


def spectra_kernel(w_ref, f_ref, p_ref, s):
    for g in range(8):
        y = jnp.concatenate([w_ref[2 * g], w_ref[2 * g + 1]], axis=1)
        s[:, 256 * g : 256 * g + 256] = jnp.dot(f_ref[...], y, preferred_element_type=F32)

    @pl.loop(0, M)
    def _(m):
        for i in range(2):
            row = pl.multiple_of(m * 16 + 8 * i, 8)
            v = jnp.concatenate([s[pl.ds(row, 8), 128 * g : 128 * g + 128] for g in range(16)], axis=0)
            p_ref[m, :, 128 * i : 128 * i + 128] = v.T.astype(BF)


def spectra(w, fwd_k):
    v = pl.BlockSpec(memory_space=pltpu.VMEM)
    return pl.pallas_call(
        spectra_kernel,
        in_specs=[v, v],
        out_specs=v,
        out_shape=jax.ShapeDtypeStruct((M, 128, 256), BF),
        scratch_shapes=[pltpu.VMEM((2 * M * 8, 2048), F32)],
        compiler_params=pltpu.CompilerParams(vmem_limit_bytes=16 * MIB),
        cost_estimate=pl.CostEstimate(flops=4_000_000_000, bytes_accessed=5_000_000, transcendentals=0),
        name="spectra",
    )(w, fwd_k)


def ref_kernel(b_ref, f_ref, r_ref, s):
    for y in range(4):
        for xh in range(2):
            for t in range(9):
                v = b_ref[y, xh, :, t * 128 : (t + 1) * 128].astype(F32)
                row = (y * 2 + xh) * 72 + 8 * t
                s[row : row + 8, 0:128] = v[0:8]
                s[row : row + 8, 128:256] = v[8:16]
    out = jnp.dot(f_ref[...], s[...].astype(BF), preferred_element_type=F32)
    for m in range(M):
        for i in range(2):
            r = 16 * m + 8 * i
            r_ref[m, :, 128 * i : 128 * i + 128] = jnp.concatenate(
                [out[r : r + 8, 0:128], out[r : r + 8, 128:256]], axis=0
            ).astype(BF)


def ref_spectra(blocks, fwd_k):
    v = pl.BlockSpec(memory_space=pltpu.VMEM)
    return pl.pallas_call(
        ref_kernel,
        in_specs=[v, v],
        out_specs=v,
        out_shape=jax.ShapeDtypeStruct((M, 16, 256), BF),
        scratch_shapes=[pltpu.VMEM((A * 8, 256), F32)],
        compiler_params=pltpu.CompilerParams(vmem_limit_bytes=8 * MIB),
        cost_estimate=pl.CostEstimate(flops=200_000_000, bytes_accessed=1_500_000, transcendentals=0),
        name="ref_spectra",
    )(blocks, fwd_k)


def score_kernel(*refs):
    p_ref, blocks, inv_ref, o_ref, xs = refs[0], refs[1:17], refs[17], refs[18], refs[19]
    xs[:, 2 * M * 8 :, :] = jnp.zeros((16, K_INV - 2 * M * 8, 256), BF)

    @pl.loop(0, M)
    def _(m):
        upper = p_ref[m]
        re, im = upper[:, 0:128], upper[:, 128:256]
        rhs = jnp.concatenate([upper, jnp.concatenate([im, -re], axis=1)], axis=0)
        lhs = jnp.concatenate([b[m] for b in blocks], axis=0)
        x = jnp.dot(lhs, rhs, preferred_element_type=F32)
        row = pl.multiple_of(m * 16, 16)
        for g in range(16):
            for h in range(2):
                k = 16 * g + 8 * h
                xs[g, pl.ds(row, 16), 128 * h : 128 * h + 128] = jnp.concatenate(
                    [x[k : k + 8, 0:128], x[k : k + 8, 128:256]], axis=0
                ).astype(BF)

    def one(g, best):
        y = jnp.dot(inv_ref[...], xs[g], preferred_element_type=F32)
        for t in range(A):
            best = jnp.maximum(best, y[8 * t : 8 * t + 8])
        return best

    best = lax.fori_loop(0, 16, one, jnp.full((8, 256), -jnp.inf, F32))
    best = jnp.max(best, axis=0, keepdims=True)
    o_ref[...] = jnp.maximum(best[:, 0:128], best[:, 128:256])


def scores_of(p, blocks, inv_k):
    v = pl.BlockSpec(memory_space=pltpu.VMEM)
    return pl.pallas_call(
        score_kernel,
        in_specs=[v] * 18,
        out_specs=v,
        out_shape=jax.ShapeDtypeStruct((1, 128), F32),
        scratch_shapes=[pltpu.VMEM((16, K_INV, 256), BF)],
        compiler_params=pltpu.CompilerParams(vmem_limit_bytes=20 * MIB),
        cost_estimate=pl.CostEstimate(flops=6_000_000_000, bytes_accessed=8_000_000, transcendentals=0),
        name="scores",
    )(p, *blocks, inv_k)


def sums_kernel(sc, c0, c1, c2, c3, tab_ref, mine, other, acc):
    width = 18 * 128
    lane = lax.broadcasted_iota(jnp.int32, (128, 256), 1).astype(F32)
    picks, groups = [], []
    for c in (c0, c1, c2, c3):
        meta = c[:, width : width + 128].astype(F32)
        picks.append(jnp.where(lane == meta[:, 0:1], 1.0, 0.0).astype(F32).T.astype(BF))
        groups.append(jnp.where(lane == meta[:, 1:2], 1.0, 0.0).astype(BF))
    pick = jnp.concatenate(picks, axis=1)
    group = jnp.concatenate(groups, axis=0)
    count = jnp.dot(pick, group, preferred_element_type=F32)
    flipped = tab_ref[...].T
    tab = jnp.concatenate([flipped, flipped], axis=1)
    wsum = jnp.dot(count, tab * tab, precision=lax.Precision.HIGHEST, preferred_element_type=F32)
    for t in range(9):
        cols = slice(256 * t, 256 * t + 256)
        x = jnp.concatenate([c[:, cols] for c in (c0, c1, c2, c3)], axis=0)
        acc[:, cols] = jnp.dot(pick, x, preferred_element_type=F32)
    left = lax.broadcasted_iota(jnp.int32, (256, 128), 1) < R
    for ref, core in ((mine, sc[2]), (other, 1 - sc[2])):
        for xh in range(2):
            start = pl.multiple_of((9 * xh + 4 * core) * 128, 128)
            ref[xh] = acc[:, pl.ds(start, 640)]
            mid = acc[:, (9 * xh + 4) * 128 : (9 * xh + 5) * 128]
            keep = jnp.logical_xor(left, core == 1)
            ref[xh, :, pl.ds(pl.multiple_of((1 - core) * 512, 128), 128)] = jnp.where(keep, mid, wsum)


def class_sums(sc, cs, tab):
    v = pl.BlockSpec(memory_space=pltpu.VMEM)
    shape = jax.ShapeDtypeStruct((2, 256, 640), F32)
    return pl.pallas_call(
        sums_kernel,
        in_specs=[pl.BlockSpec(memory_space=pltpu.SMEM)] + [v] * 5,
        out_specs=[v, v],
        out_shape=[shape, shape],
        scratch_shapes=[pltpu.VMEM((256, 18 * 128), F32)],
        compiler_params=pltpu.CompilerParams(vmem_limit_bytes=VMEM_LIMIT),
        cost_estimate=pl.CostEstimate(flops=700_000_000, bytes_accessed=5_000_000, transcendentals=0),
        name="class_sums",
    )(sc, *cs, tab)


def cut_x_kernel(sc, a_ref, b_ref, o0, o1, o2, o3):
    for dx, o in enumerate((o0, o1, o2, o3)):
        x = lax.rem(sc[1] + dx, 4)
        xh, xl = x // 2, lax.rem(x, 2)
        rows = pl.ds(pl.multiple_of(xl * 128, 128), 128)
        o[...] = a_ref[xh, rows, :] + b_ref[xh, rows, :]


def cut_x(sc, a, b):
    v = pl.BlockSpec(memory_space=pltpu.VMEM)
    return pl.pallas_call(
        cut_x_kernel,
        in_specs=[pl.BlockSpec(memory_space=pltpu.SMEM), v, v],
        out_specs=[v] * 4,
        out_shape=[jax.ShapeDtypeStruct((128, 640), F32)] * 4,
        compiler_params=pltpu.CompilerParams(vmem_limit_bytes=VMEM_LIMIT),
        cost_estimate=pl.CostEstimate(flops=400_000, bytes_accessed=3_900_000, transcendentals=0),
        name="cut_x",
    )(sc, a, b)


def cut_z_kernel(sc, a0, a1, a2, a3, o0, o1, o2, o3):
    for dz, o in enumerate((o0, o1, o2, o3)):
        z = lax.rem(sc[3] + dz, 4)
        rows = pl.ds(pl.multiple_of(z * 32, 32), 32)
        o[...] = (a0[rows, :] + a1[rows, :]) + (a2[rows, :] + a3[rows, :])


def cut_z(sc, parts):
    v = pl.BlockSpec(memory_space=pltpu.VMEM)
    return pl.pallas_call(
        cut_z_kernel,
        in_specs=[pl.BlockSpec(memory_space=pltpu.SMEM)] + [v] * 4,
        out_specs=[v] * 4,
        out_shape=[jax.ShapeDtypeStruct((32, 640), F32)] * 4,
        compiler_params=pltpu.CompilerParams(vmem_limit_bytes=VMEM_LIMIT),
        cost_estimate=pl.CostEstimate(flops=400_000, bytes_accessed=1_700_000, transcendentals=0),
        name="cut_z",
    )(sc, *parts)


def final_kernel(sc, a0, a1, a2, a3, o_ref):
    s = (a0[...] + a1[...]) + (a2[...] + a3[...])
    odd = sc[2] == 1
    left = lax.broadcasted_iota(jnp.int32, (32, 128), 1) < R
    tile = [s[:, 128 * t : 128 * t + 128] for t in range(5)]
    held = jnp.where(odd, tile[0], tile[4])
    turned = pltpu.roll(held, R, 1)
    weight = jnp.where(jnp.logical_xor(left, odd), turned, held)
    tile = [t / (weight + TAU) for t in tile]
    rolled = [pltpu.roll(t, R, 1) for t in tile]
    later = [jnp.where(left, rolled[t], rolled[t + 1]) for t in range(4)] + [rolled[4]]
    for t in range(4):
        o_ref[:, 128 * t : 128 * t + 128] = jnp.where(odd, later[t], tile[t])[0:25]
    o_ref[:, 512:576] = jnp.where(odd, later[4], tile[4])[0:25, 0:R]


def final(sc, parts):
    v = pl.BlockSpec(memory_space=pltpu.VMEM)
    return pl.pallas_call(
        final_kernel,
        in_specs=[pl.BlockSpec(memory_space=pltpu.SMEM)] + [v] * 4,
        out_specs=v,
        out_shape=jax.ShapeDtypeStruct((25, 576), F32),
        name="final",
    )(sc, *parts)


def place(y, x, z, core):
    return ((y % 4) * 4 + (x % 4) // 2 * 2 + core % 2) * 8 + (x % 2) * 4 + z % 4


def permutation(move):
    return [
        (place(y, x, z, c), place(*move(y, x, z, c)))
        for y in range(4)
        for x in range(4)
        for z in range(4)
        for c in range(2)
    ]


CORE = permutation(lambda y, x, z, c: (y, x, z, c + 1))
HIGH = permutation(lambda y, x, z, c: (y, x + 2, z, c))
LOW = permutation(lambda y, x, z, c: (y, x ^ 1, z, c))
Y_NEAR = permutation(lambda y, x, z, c: (y ^ 1, x, z, c))
Y_FAR = permutation(lambda y, x, z, c: (y + 2, x, z, c))
YS = [permutation(lambda y, x, z, c, d=d: (y + d, x, z, c)) for d in range(4)]
XS = [permutation(lambda y, x, z, c, d=d: (y, x + d, z, c)) for d in range(4)]
ZS = [permutation(lambda y, x, z, c, d=d: (y, x, z + d, c)) for d in range(4)]


def move(value, pairs):
    return lax.ppermute(value, AXES, pairs)


def join(own, other, upper):
    lower = upper == 0
    return jnp.stack([jnp.where(lower, own, other), jnp.where(lower, other, own)])


def per_device(particles, references, owner, class_offset, rotation, shifts, ctf_group, ctf_table):
    fwd_np, inv_np = tables()
    fwd_k, inv_k = jnp.asarray(fwd_np), jnp.asarray(inv_np)
    fx, fy = (jnp.asarray(t) for t in freq_tables())
    dom, cls = lax.axis_index("dom"), lax.axis_index("cls")
    y, xh, core = dom // 4, dom // 2 % 2, dom % 2
    xl, z = cls // 4, cls % 4
    sc = jnp.stack([y, xh * 2 + xl, core, z]).astype(jnp.int32)

    low, high = references[0:16], references[9:25]
    first = core == 0
    keep = jnp.where(first, low, high)
    give = jnp.where(first, high, low)
    got = move(give, CORE)
    block = jnp.where(
        first, jnp.concatenate([keep, got], axis=1), jnp.concatenate([got, keep], axis=1)
    )
    rows = [shifts.T, rotation[None], owner.T, class_offset[None], ctf_group[None]]
    table = ctf_table.T
    block, rows[1] = lax.optimization_barrier((block, rows[1]))
    held = prep(particles, rows, table, fx, fy, 0, 4)
    far = move(block, HIGH)
    far, *held = lax.optimization_barrier((far, *held))
    pair = join(block, far, xh)
    pair, rows[1] = lax.optimization_barrier((pair, rows[1]))
    weighted, *sent = prep(particles, rows, table, fx, fy, 4, 4, held)
    near = move(pair, Y_NEAR)
    near, weighted, *sent = lax.optimization_barrier((near, weighted, *sent))
    quad = join(pair, near, y % 2)
    octet = join(quad, move(quad, Y_FAR), y // 2).reshape(4, 2, 16, 1152)

    held = [sent[0]] + [move(sent[d], YS[d]) for d in (1, 2, 3)]
    part = spectra(weighted, fwd_k)

    own = ref_spectra(octet, fwd_k)
    up, down = move(own, ZS[1]), move(own, ZS[3])
    side = move(own, LOW)
    *held, up, down, side, part = lax.optimization_barrier((*held, up, down, side, part))
    side_up, side_down = move(side, ZS[1]), move(side, ZS[3])
    line = [own, side, up, down, side_up, side_down, move(up, ZS[1]), move(side_down, ZS[3])]
    line = line + [move(b, CORE) for b in line]
    scores = scores_of(part, line, inv_k)[0]

    mine, other = class_sums(sc, held, table)
    cut = cut_x(sc, mine, move(other, CORE))
    cut = [cut[0]] + [move(cut[d], XS[d]) for d in (1, 2, 3)]
    cut = cut_z(sc, cut)
    cut = [cut[0]] + [move(cut[d], ZS[d]) for d in (1, 2, 3)]
    return scores, final(sc, cut)


def solution(mesh):
    return jax.shard_map(
        per_device,
        mesh=mesh,
        in_specs=(
            P(("dom", "cls"), None),
            P("cls", "dom"),
            P(("dom", "cls"), None),
            P(("dom", "cls")),
            P(("dom", "cls")),
            P(("dom", "cls"), None),
            P(("dom", "cls")),
            P(),
        ),
        out_specs=(P(("dom", "cls")), P("cls", "dom")),
        check_vma=False,
    )
```

```python
import jax
import jax.numpy as jnp
import numpy as np
from jax import lax
from jax.experimental import pallas as pl
from jax.experimental.pallas import tpu as pltpu
from jax.sharding import PartitionSpec as P

A = 72
M = 37
R = 64
BOX = 128
TAU = 1.0
AXES = ("dom", "cls")
BF = jnp.bfloat16
F32 = jnp.float32
MIB = 1024 * 1024
VMEM_LIMIT = 16 * MIB
PREP_MIB = 56
K_INV = 640


def tables():
    m = np.arange(M)[:, None]
    a = np.arange(A)[None, :]
    turn = 2.0 * np.pi * ((m * a) % A) / A
    fwd = np.stack([np.cos(turn), -np.sin(turn)], axis=1).reshape(2 * M, A)
    gain = np.where((np.arange(M) == 0) | (np.arange(M) == A // 2), 1.0, 2.0)[:, None]
    inv = np.stack([np.cos(turn) / A, -np.sin(turn) / A], axis=1).astype(BF).astype(np.float32)
    inv = (inv * gain[:, None, :]).reshape(2 * M, A).T
    eye = np.eye(8, dtype=np.float32)
    fwd_k = np.kron(fwd.astype(np.float32), eye).astype(BF)
    inv_k = np.zeros((A * 8, K_INV), np.float32)
    inv_k[:, : 2 * M * 8] = np.kron(inv, eye)
    return fwd_k, inv_k.astype(BF)


def freq_tables():
    angle = 2.0 * np.pi * np.arange(A // 2) / A
    radius = np.tile(np.arange(1, R + 1), 2)
    fx = np.cos(angle)[:, None] * radius[None, :] / BOX
    fy = np.sin(angle)[:, None] * radius[None, :] / BOX
    return fx.astype(np.float32), fy.astype(np.float32)


def cos_poly():
    n = 7
    nodes = (np.cos((np.arange(64) + 0.5) * np.pi / 64) + 1.0) / 8.0
    return [float(c) for c in np.polynomial.chebyshev.Chebyshev.fit(
        nodes, np.cos(2.0 * np.pi * np.sqrt(nodes)), n - 1, domain=[0.0, 0.25]
    ).convert(kind=np.polynomial.Polynomial).coef]


COEF = cos_poly()


def prep_kernel(
    x_ref, shift_ref, rot_ref, own_ref, off_ref, grp_ref, tab_ref, fx_ref, fy_ref,
    w_ref, c0, c1, c2, c3, ws, us, aux, tab,
):
    dom, cls = lax.axis_index("dom"), lax.axis_index("cls")
    mine = 2 * (dom * 8 + cls)
    step = pl.program_id(0)

    @pl.when(step == 0)
    def _():
        shift_rows = shift_ref[...].astype(F32)
        group = grp_ref[...]
        rows = [
            shift_rows,
            rot_ref[...].astype(F32),
            (group - mine).astype(F32),
            (own_ref[...] * 32 + off_ref[...]).astype(F32),
            group.astype(F32),
            jnp.zeros((122, 128), F32),
        ]
        aux[...] = jnp.concatenate(rows, axis=0).T
        flipped = tab_ref[...].T
        tab[...] = jnp.concatenate([flipped, flipped], axis=1)

    here = aux[pl.ds(pl.multiple_of(step * 16, 16), 16), :]
    lane = lax.broadcasted_iota(jnp.int32, (16, 128), 1)
    left = lane < R
    shift = jnp.where(left, 0.0, -0.25).astype(F32)
    sxb = jnp.broadcast_to(here[:, 0:1], (16, 128))
    syb = jnp.broadcast_to(here[:, 1:2], (16, 128))
    ctf = jnp.where(here[:, 3:4] > 0.5, tab[pl.ds(mine + 1, 1), :], tab[pl.ds(mine, 1), :])
    ctf_s = jnp.where(left, -ctf, ctf)
    for b in range(A // 4):
        done = []
        for a in (2 * b, 2 * b + 1):
            v = (sxb * fx_ref[a : a + 1, :] + syb * fy_ref[a : a + 1, :]) + shift
            v = v - jnp.round(v)
            q = v * v
            e = jnp.full_like(q, COEF[-1])
            for k in COEF[-2::-1]:
                e = e * q + k
            er = pltpu.roll(e, R, 1)
            cc = jnp.where(left, e, er) * ctf
            ss = jnp.where(left, er, e) * ctf_s
            x0 = x_ref[:, a * 128 : (a + 1) * 128].astype(F32)
            h = a + A // 2
            x1 = x_ref[:, h * 128 : (h + 1) * 128].astype(F32)
            w0 = x0 * cc + pltpu.roll(x0, R, 1) * ss
            w1 = x1 * cc - pltpu.roll(x1, R, 1) * ss
            ws[:, a * 128 : (a + 1) * 128] = w0
            ws[:, h * 128 : (h + 1) * 128] = w1
            done.append((w0, w1))
        for half in (0, 1):
            row = (2 * b + half * (A // 2)) * 8
            for g in (0, 1):
                w_ref[g, row : row + 16, :] = jnp.concatenate(
                    [done[0][half][8 * g : 8 * g + 8], done[1][half][8 * g : 8 * g + 8]], axis=0
                ).astype(BF)
    rotb = jnp.broadcast_to(here[:, 2:3], (16, 128)).astype(jnp.int32)
    bit = [(rotb & (1 << k)) != 0 for k in range(7)]
    for r in range(8):
        t = [ws[:, (r + 8 * n) * 128 : (r + 8 * n + 1) * 128] for n in range(9)]
        for k in range(4):
            t = [jnp.where(bit[3 + k], t[(n + (1 << k)) % 9], t[n]) for n in range(9)]
        for n in range(9):
            us[:, (r + 8 * n) * 128 : (r + 8 * n + 1) * 128] = t[n]
    for j0 in range(0, A, 8):
        t = [us[:, ((j0 + i) % A) * 128 : ((j0 + i) % A + 1) * 128] for i in range(15)]
        t = [jnp.where(bit[0], t[i + 1], t[i]) for i in range(14)]
        t = [jnp.where(bit[1], t[i + 2], t[i]) for i in range(12)]
        for i in range(8):
            ws[:, (j0 + i) * 128 : (j0 + i + 1) * 128] = jnp.where(bit[2], t[i + 4], t[i])
    meta = jnp.where(lane == 0, here[:, 4:5], jnp.where(lane == 1, here[:, 5:6], 0.0)).astype(BF)
    width = 18 * 128
    for dy, c_ref in enumerate((c0, c1, c2, c3)):
        dest = lax.rem(dom // 4 + dy, 4)
        start = pl.multiple_of(dest * width, 128)
        c_ref[:, 0:width] = ws[:, pl.ds(start, width)].astype(BF)
        c_ref[:, width : width + 128] = meta


def prep(particles, rows, table, fx, fy):
    n = particles.shape[0]
    whole = lambda a: pl.BlockSpec(a.shape, lambda i: (0,) * a.ndim)
    block = lambda i: (i, 0)
    args = [particles, *rows, table, fx, fy]
    return pl.pallas_call(
        prep_kernel,
        grid=(n // 16,),
        in_specs=[pl.BlockSpec((16, A * 128), block)] + [whole(a) for a in args[1:]],
        out_specs=[pl.BlockSpec((2, A * 8, 128), lambda i: (i, 0, 0))]
        + [pl.BlockSpec((16, 19 * 128), block)] * 4,
        scratch_shapes=[
            pltpu.VMEM((16, A * 128), F32),
            pltpu.VMEM((16, A * 128), F32),
            pltpu.VMEM((128, 128), F32),
            pltpu.VMEM((256, 128), F32),
        ],
        out_shape=[jax.ShapeDtypeStruct((n // 8, A * 8, 128), BF)]
        + [jax.ShapeDtypeStruct((n, 19 * 128), BF)] * 4,
        compiler_params=pltpu.CompilerParams(vmem_limit_bytes=PREP_MIB * MIB),
        cost_estimate=pl.CostEstimate(
            flops=40_000_000, bytes_accessed=8_000_000, transcendentals=0
        ),
        name="prep",
    )(*args)


def spectra_kernel(w_ref, f_ref, p_ref, s):
    for g in range(8):
        y = jnp.concatenate([w_ref[2 * g], w_ref[2 * g + 1]], axis=1)
        s[:, 256 * g : 256 * g + 256] = jnp.dot(f_ref[...], y, preferred_element_type=F32)

    @pl.loop(0, M)
    def _(m):
        for i in range(2):
            row = pl.multiple_of(m * 16 + 8 * i, 8)
            v = jnp.concatenate([s[pl.ds(row, 8), 128 * g : 128 * g + 128] for g in range(16)], axis=0)
            p_ref[m, :, 128 * i : 128 * i + 128] = v.T.astype(BF)


def spectra(w, fwd_k):
    v = pl.BlockSpec(memory_space=pltpu.VMEM)
    return pl.pallas_call(
        spectra_kernel,
        in_specs=[v, v],
        out_specs=v,
        out_shape=jax.ShapeDtypeStruct((M, 128, 256), BF),
        scratch_shapes=[pltpu.VMEM((2 * M * 8, 2048), F32)],
        compiler_params=pltpu.CompilerParams(vmem_limit_bytes=16 * MIB),
        cost_estimate=pl.CostEstimate(flops=1000, bytes_accessed=1000, transcendentals=0),
        name="spectra",
    )(w, fwd_k)


def ref_kernel(b_ref, f_ref, r_ref, s):
    for y in range(4):
        for xh in range(2):
            for t in range(9):
                v = b_ref[y, xh, :, t * 128 : (t + 1) * 128].astype(F32)
                row = (y * 2 + xh) * 72 + 8 * t
                s[row : row + 8, 0:128] = v[0:8]
                s[row : row + 8, 128:256] = v[8:16]
    out = jnp.dot(f_ref[...], s[...].astype(BF), preferred_element_type=F32)
    for m in range(M):
        for i in range(2):
            r = 16 * m + 8 * i
            r_ref[m, :, 128 * i : 128 * i + 128] = jnp.concatenate(
                [out[r : r + 8, 0:128], out[r : r + 8, 128:256]], axis=0
            ).astype(BF)


def ref_spectra(blocks, fwd_k):
    v = pl.BlockSpec(memory_space=pltpu.VMEM)
    return pl.pallas_call(
        ref_kernel,
        in_specs=[v, v],
        out_specs=v,
        out_shape=jax.ShapeDtypeStruct((M, 16, 256), BF),
        scratch_shapes=[pltpu.VMEM((A * 8, 256), F32)],
        compiler_params=pltpu.CompilerParams(vmem_limit_bytes=8 * MIB),
        cost_estimate=pl.CostEstimate(flops=1000, bytes_accessed=1000, transcendentals=0),
        name="ref_spectra",
    )(blocks, fwd_k)


def score_kernel(*refs):
    p_ref, blocks, inv_ref, o_ref, xs = refs[0], refs[1:5], refs[5], refs[6], refs[7]
    xs[:, 2 * M * 8 :, :] = jnp.zeros((16, K_INV - 2 * M * 8, 256), BF)

    @pl.loop(0, M)
    def _(m):
        upper = p_ref[m]
        re, im = upper[:, 0:128], upper[:, 128:256]
        rhs = jnp.concatenate([upper, jnp.concatenate([im, -re], axis=1)], axis=0)
        lhs = jnp.concatenate([b[i, m] for b in blocks for i in range(4)], axis=0)
        x = jnp.dot(lhs, rhs, preferred_element_type=F32)
        row = pl.multiple_of(m * 16, 16)
        for g in range(16):
            for h in range(2):
                k = 16 * g + 8 * h
                xs[g, pl.ds(row, 16), 128 * h : 128 * h + 128] = jnp.concatenate(
                    [x[k : k + 8, 0:128], x[k : k + 8, 128:256]], axis=0
                ).astype(BF)

    def one(g, best):
        y = jnp.dot(inv_ref[...], xs[g], preferred_element_type=F32)
        for t in range(A):
            best = jnp.maximum(best, y[8 * t : 8 * t + 8])
        return best

    best = lax.fori_loop(0, 16, one, jnp.full((8, 256), -jnp.inf, F32))
    best = jnp.max(best, axis=0, keepdims=True)
    o_ref[...] = jnp.maximum(best[:, 0:128], best[:, 128:256])


def scores_of(p, blocks, inv_k):
    v = pl.BlockSpec(memory_space=pltpu.VMEM)
    return pl.pallas_call(
        score_kernel,
        in_specs=[v] * 6,
        out_specs=v,
        out_shape=jax.ShapeDtypeStruct((1, 128), F32),
        scratch_shapes=[pltpu.VMEM((16, K_INV, 256), BF)],
        compiler_params=pltpu.CompilerParams(vmem_limit_bytes=20 * MIB),
        cost_estimate=pl.CostEstimate(flops=6_000_000_000, bytes_accessed=8_000_000, transcendentals=0),
        name="scores",
    )(p, *blocks, inv_k)


def sums_kernel(sc, c0, c1, c2, c3, tab_ref, mine, other, acc):
    width = 18 * 128
    lane = lax.broadcasted_iota(jnp.int32, (128, 256), 1).astype(F32)
    picks, groups = [], []
    for c in (c0, c1, c2, c3):
        meta = c[:, width : width + 128].astype(F32)
        picks.append(jnp.where(lane == meta[:, 0:1], 1.0, 0.0).astype(F32).T.astype(BF))
        groups.append(jnp.where(lane == meta[:, 1:2], 1.0, 0.0).astype(BF))
    pick = jnp.concatenate(picks, axis=1)
    group = jnp.concatenate(groups, axis=0)
    count = jnp.dot(pick, group, preferred_element_type=F32)
    flipped = tab_ref[...].T
    tab = jnp.concatenate([flipped, flipped], axis=1)
    wsum = jnp.dot(count, tab * tab, precision=lax.Precision.HIGHEST, preferred_element_type=F32)
    for t in range(9):
        cols = slice(256 * t, 256 * t + 256)
        x = jnp.concatenate([c[:, cols] for c in (c0, c1, c2, c3)], axis=0)
        acc[:, cols] = jnp.dot(pick, x, preferred_element_type=F32)
    left = lax.broadcasted_iota(jnp.int32, (256, 128), 1) < R
    for ref, core in ((mine, sc[2]), (other, 1 - sc[2])):
        for xh in range(2):
            start = pl.multiple_of((9 * xh + 4 * core) * 128, 128)
            ref[xh] = acc[:, pl.ds(start, 640)]
            mid = acc[:, (9 * xh + 4) * 128 : (9 * xh + 5) * 128]
            keep = jnp.logical_xor(left, core == 1)
            ref[xh, :, pl.ds(pl.multiple_of((1 - core) * 512, 128), 128)] = jnp.where(keep, mid, wsum)


def class_sums(sc, cs, tab):
    v = pl.BlockSpec(memory_space=pltpu.VMEM)
    shape = jax.ShapeDtypeStruct((2, 256, 640), F32)
    return pl.pallas_call(
        sums_kernel,
        in_specs=[pl.BlockSpec(memory_space=pltpu.SMEM)] + [v] * 5,
        out_specs=[v, v],
        out_shape=[shape, shape],
        scratch_shapes=[pltpu.VMEM((256, 18 * 128), F32)],
        compiler_params=pltpu.CompilerParams(vmem_limit_bytes=VMEM_LIMIT),
        cost_estimate=pl.CostEstimate(flops=700_000_000, bytes_accessed=5_000_000, transcendentals=0),
        name="class_sums",
    )(sc, *cs, tab)


def cut_x_kernel(sc, a_ref, b_ref, o0, o1, o2, o3):
    for dx, o in enumerate((o0, o1, o2, o3)):
        x = lax.rem(sc[1] + dx, 4)
        xh, xl = x // 2, lax.rem(x, 2)
        rows = pl.ds(pl.multiple_of(xl * 128, 128), 128)
        o[...] = a_ref[xh, rows, :] + b_ref[xh, rows, :]


def cut_x(sc, a, b):
    v = pl.BlockSpec(memory_space=pltpu.VMEM)
    return pl.pallas_call(
        cut_x_kernel,
        in_specs=[pl.BlockSpec(memory_space=pltpu.SMEM), v, v],
        out_specs=[v] * 4,
        out_shape=[jax.ShapeDtypeStruct((128, 640), F32)] * 4,
        compiler_params=pltpu.CompilerParams(vmem_limit_bytes=VMEM_LIMIT),
        cost_estimate=pl.CostEstimate(flops=400_000, bytes_accessed=3_900_000, transcendentals=0),
        name="cut_x",
    )(sc, a, b)


def cut_z_kernel(sc, a0, a1, a2, a3, o0, o1, o2, o3):
    for dz, o in enumerate((o0, o1, o2, o3)):
        z = lax.rem(sc[3] + dz, 4)
        rows = pl.ds(pl.multiple_of(z * 32, 32), 32)
        o[...] = (a0[rows, :] + a1[rows, :]) + (a2[rows, :] + a3[rows, :])


def cut_z(sc, parts):
    v = pl.BlockSpec(memory_space=pltpu.VMEM)
    return pl.pallas_call(
        cut_z_kernel,
        in_specs=[pl.BlockSpec(memory_space=pltpu.SMEM)] + [v] * 4,
        out_specs=[v] * 4,
        out_shape=[jax.ShapeDtypeStruct((32, 640), F32)] * 4,
        compiler_params=pltpu.CompilerParams(vmem_limit_bytes=VMEM_LIMIT),
        cost_estimate=pl.CostEstimate(flops=400_000, bytes_accessed=1_700_000, transcendentals=0),
        name="cut_z",
    )(sc, *parts)


def final_kernel(sc, a0, a1, a2, a3, o_ref):
    s = (a0[...] + a1[...]) + (a2[...] + a3[...])
    odd = sc[2] == 1
    left = lax.broadcasted_iota(jnp.int32, (32, 128), 1) < R
    tile = [s[:, 128 * t : 128 * t + 128] for t in range(5)]
    held = jnp.where(odd, tile[0], tile[4])
    turned = pltpu.roll(held, R, 1)
    weight = jnp.where(jnp.logical_xor(left, odd), turned, held)
    tile = [t / (weight + TAU) for t in tile]
    rolled = [pltpu.roll(t, R, 1) for t in tile]
    later = [jnp.where(left, rolled[t], rolled[t + 1]) for t in range(4)] + [rolled[4]]
    for t in range(4):
        o_ref[:, 128 * t : 128 * t + 128] = jnp.where(odd, later[t], tile[t])[0:25]
    o_ref[:, 512:576] = jnp.where(odd, later[4], tile[4])[0:25, 0:R]


def final(sc, parts):
    v = pl.BlockSpec(memory_space=pltpu.VMEM)
    return pl.pallas_call(
        final_kernel,
        in_specs=[pl.BlockSpec(memory_space=pltpu.SMEM)] + [v] * 4,
        out_specs=v,
        out_shape=jax.ShapeDtypeStruct((25, 576), F32),
        name="final",
    )(sc, *parts)


def place(y, x, z, core):
    return ((y % 4) * 4 + (x % 4) // 2 * 2 + core % 2) * 8 + (x % 2) * 4 + z % 4


def permutation(move):
    return [
        (place(y, x, z, c), place(*move(y, x, z, c)))
        for y in range(4)
        for x in range(4)
        for z in range(4)
        for c in range(2)
    ]


CORE = permutation(lambda y, x, z, c: (y, x, z, c + 1))
HIGH = permutation(lambda y, x, z, c: (y, x + 2, z, c))
LOW = permutation(lambda y, x, z, c: (y, x ^ 1, z, c))
Y_NEAR = permutation(lambda y, x, z, c: (y ^ 1, x, z, c))
Y_FAR = permutation(lambda y, x, z, c: (y + 2, x, z, c))
YS = [permutation(lambda y, x, z, c, d=d: (y + d, x, z, c)) for d in range(4)]
XS = [permutation(lambda y, x, z, c, d=d: (y, x + d, z, c)) for d in range(4)]
ZS = [permutation(lambda y, x, z, c, d=d: (y, x, z + d, c)) for d in range(4)]


def move(value, pairs):
    return lax.ppermute(value, AXES, pairs)


def join(own, other, upper):
    lower = upper == 0
    return jnp.stack([jnp.where(lower, own, other), jnp.where(lower, other, own)])


def per_device(particles, references, owner, class_offset, rotation, shifts, ctf_group, ctf_table):
    fwd_np, inv_np = tables()
    fwd_k, inv_k = jnp.asarray(fwd_np), jnp.asarray(inv_np)
    fx, fy = (jnp.asarray(t) for t in freq_tables())
    dom, cls = lax.axis_index("dom"), lax.axis_index("cls")
    y, xh, core = dom // 4, dom // 2 % 2, dom % 2
    xl, z = cls // 4, cls % 4
    sc = jnp.stack([y, xh * 2 + xl, core, z]).astype(jnp.int32)

    low, high = references[0:16], references[9:25]
    first = core == 0
    keep = jnp.where(first, low, high)
    give = jnp.where(first, high, low)
    got = move(give, CORE)
    block = jnp.where(
        first, jnp.concatenate([keep, got], axis=1), jnp.concatenate([got, keep], axis=1)
    )
    rows = [shifts.T, rotation[None], owner.T, class_offset[None], ctf_group[None]]
    table = ctf_table.T
    block, rows[1] = lax.optimization_barrier((block, rows[1]))
    weighted, *sent = prep(particles, rows, table, fx, fy)
    far = move(block, HIGH)
    far, weighted, *sent = lax.optimization_barrier((far, weighted, *sent))
    pair = join(block, far, xh)
    near = move(pair, Y_NEAR)
    quad = join(pair, near, y % 2)
    octet = join(quad, move(quad, Y_FAR), y // 2).reshape(4, 2, 16, 1152)

    held = [sent[0]] + [move(sent[d], YS[d]) for d in (1, 2, 3)]
    part = spectra(weighted, fwd_k)

    own = ref_spectra(octet, fwd_k)
    up, down = move(own, ZS[1]), move(own, ZS[3])
    side = move(own, LOW)
    side_up, side_down = move(side, ZS[1]), move(side, ZS[3])
    *held, side, up, down, part = lax.optimization_barrier((*held, side, up, down, part))
    on_up, on_down = move(up, ZS[1]), move(side_down, ZS[3])
    early, late = jnp.stack([own, side, up, down]), jnp.stack([side_up, side_down, on_up, on_down])
    early_twin, late_twin = move(early, CORE), move(late, CORE)
    *held, late_twin, early_twin = lax.optimization_barrier((*held, late_twin, early_twin))
    mine, other = class_sums(sc, held, table)
    other = move(other, CORE)
    cut = cut_x(sc, mine, other)
    cut = [cut[0]] + [move(cut[d], XS[d]) for d in (1, 2, 3)]
    scores = scores_of(part, [early, early_twin, late, late_twin], inv_k)
    *cut, scores = lax.optimization_barrier((*cut, scores))
    cut = cut_z(sc, cut)
    cut = [cut[0]] + [move(cut[d], ZS[d]) for d in (1, 2, 3)]
    return scores[0], final(sc, cut)


def solution(mesh):
    return jax.shard_map(
        per_device,
        mesh=mesh,
        in_specs=(
            P(("dom", "cls"), None),
            P("cls", "dom"),
            P(("dom", "cls"), None),
            P(("dom", "cls")),
            P(("dom", "cls")),
            P(("dom", "cls"), None),
            P(("dom", "cls")),
            P(),
        ),
        out_specs=(P(("dom", "cls")), P("cls", "dom")),
        check_vma=False,
    )
```

```python
import functools

import jax
import jax.numpy as jnp
import numpy as np
from jax import lax
from jax.experimental import pallas as pl
from jax.experimental.pallas import tpu as pltpu
from jax.sharding import PartitionSpec as P

A = 72
M = 37
R = 64
BOX = 128
TAU = 1.0
AXES = ("dom", "cls")
BF = jnp.bfloat16
F32 = jnp.float32
MIB = 1024 * 1024
VMEM_LIMIT = 16 * MIB
PREP_MIB = 56
K_INV = 640


def tables():
    m = np.arange(M)[:, None]
    a = np.arange(A)[None, :]
    turn = 2.0 * np.pi * ((m * a) % A) / A
    fwd = np.stack([np.cos(turn), -np.sin(turn)], axis=1).reshape(2 * M, A)
    gain = np.where((np.arange(M) == 0) | (np.arange(M) == A // 2), 1.0, 2.0)[:, None]
    inv = np.stack([np.cos(turn) / A, -np.sin(turn) / A], axis=1).astype(BF).astype(np.float32)
    inv = (inv * gain[:, None, :]).reshape(2 * M, A).T
    eye = np.eye(8, dtype=np.float32)
    fwd_k = np.kron(fwd.astype(np.float32), eye).astype(BF)
    inv_k = np.zeros((A * 8, K_INV), np.float32)
    inv_k[:, : 2 * M * 8] = np.kron(inv, eye)
    return fwd_k, inv_k.astype(BF)


def freq_tables():
    angle = 2.0 * np.pi * np.arange(A // 2) / A
    radius = np.tile(np.arange(1, R + 1), 2)
    fx = np.cos(angle)[:, None] * radius[None, :] / BOX
    fy = np.sin(angle)[:, None] * radius[None, :] / BOX
    return fx.astype(np.float32), fy.astype(np.float32)


def cos_poly():
    n = 7
    nodes = (np.cos((np.arange(64) + 0.5) * np.pi / 64) + 1.0) / 8.0
    return [float(c) for c in np.polynomial.chebyshev.Chebyshev.fit(
        nodes, np.cos(2.0 * np.pi * np.sqrt(nodes)), n - 1, domain=[0.0, 0.25]
    ).convert(kind=np.polynomial.Polynomial).coef]


COEF = cos_poly()


def prep_kernel(first, x_ref, shift_ref, rot_ref, own_ref, off_ref, grp_ref, tab_ref, fx_ref, fy_ref, *refs):
    w_ref, c0, c1, c2, c3, ws, us, aux, tab = refs[-9:]
    dom, cls = lax.axis_index("dom"), lax.axis_index("cls")
    mine = 2 * (dom * 8 + cls)
    step = pl.program_id(0)

    @pl.when(step == 0)
    def _():
        shift_rows = shift_ref[...].astype(F32)
        group = grp_ref[...]
        rows = [
            shift_rows,
            rot_ref[...].astype(F32),
            (group - mine).astype(F32),
            (own_ref[...] * 32 + off_ref[...]).astype(F32),
            group.astype(F32),
            jnp.zeros((122, 128), F32),
        ]
        aux[...] = jnp.concatenate(rows, axis=0).T
        flipped = tab_ref[...].T
        tab[...] = jnp.concatenate([flipped, flipped], axis=1)

    here = aux[pl.ds(pl.multiple_of((step + first) * 16, 16), 16), :]
    lane = lax.broadcasted_iota(jnp.int32, (16, 128), 1)
    left = lane < R
    shift = jnp.where(left, 0.0, -0.25).astype(F32)
    sxb = jnp.broadcast_to(here[:, 0:1], (16, 128))
    syb = jnp.broadcast_to(here[:, 1:2], (16, 128))
    ctf = jnp.where(here[:, 3:4] > 0.5, tab[pl.ds(mine + 1, 1), :], tab[pl.ds(mine, 1), :])
    ctf_s = jnp.where(left, -ctf, ctf)
    for b in range(A // 4):
        done = []
        for a in (2 * b, 2 * b + 1):
            v = (sxb * fx_ref[a : a + 1, :] + syb * fy_ref[a : a + 1, :]) + shift
            v = v - jnp.round(v)
            q = v * v
            e = jnp.full_like(q, COEF[-1])
            for k in COEF[-2::-1]:
                e = e * q + k
            er = pltpu.roll(e, R, 1)
            cc = jnp.where(left, e, er) * ctf
            ss = jnp.where(left, er, e) * ctf_s
            x0 = x_ref[:, a * 128 : (a + 1) * 128].astype(F32)
            h = a + A // 2
            x1 = x_ref[:, h * 128 : (h + 1) * 128].astype(F32)
            w0 = x0 * cc + pltpu.roll(x0, R, 1) * ss
            w1 = x1 * cc - pltpu.roll(x1, R, 1) * ss
            ws[:, a * 128 : (a + 1) * 128] = w0
            ws[:, h * 128 : (h + 1) * 128] = w1
            done.append((w0, w1))
        for half in (0, 1):
            row = (2 * b + half * (A // 2)) * 8
            for g in (0, 1):
                w_ref[g, row : row + 16, :] = jnp.concatenate(
                    [done[0][half][8 * g : 8 * g + 8], done[1][half][8 * g : 8 * g + 8]], axis=0
                ).astype(BF)
    rotb = jnp.broadcast_to(here[:, 2:3], (16, 128)).astype(jnp.int32)
    bit = [(rotb & (1 << k)) != 0 for k in range(7)]
    for r in range(8):
        t = [ws[:, (r + 8 * n) * 128 : (r + 8 * n + 1) * 128] for n in range(9)]
        for k in range(4):
            t = [jnp.where(bit[3 + k], t[(n + (1 << k)) % 9], t[n]) for n in range(9)]
        for n in range(9):
            us[:, (r + 8 * n) * 128 : (r + 8 * n + 1) * 128] = t[n]
    for j0 in range(0, A, 8):
        t = [us[:, ((j0 + i) % A) * 128 : ((j0 + i) % A + 1) * 128] for i in range(15)]
        t = [jnp.where(bit[0], t[i + 1], t[i]) for i in range(14)]
        t = [jnp.where(bit[1], t[i + 2], t[i]) for i in range(12)]
        for i in range(8):
            ws[:, (j0 + i) * 128 : (j0 + i + 1) * 128] = jnp.where(bit[2], t[i + 4], t[i])
    meta = jnp.where(lane == 0, here[:, 4:5], jnp.where(lane == 1, here[:, 5:6], 0.0)).astype(BF)
    width = 18 * 128
    for dy, c_ref in enumerate((c0, c1, c2, c3)):
        dest = lax.rem(dom // 4 + dy, 4)
        start = pl.multiple_of(dest * width, 128)
        c_ref[:, 0:width] = ws[:, pl.ds(start, width)].astype(BF)
        c_ref[:, width : width + 128] = meta


def prep(particles, rows, table, fx, fy, first, held=()):
    n = particles.shape[0]
    whole = lambda a: pl.BlockSpec(a.shape, lambda i: (0,) * a.ndim)
    block = lambda i: (i + first, 0)
    args = [particles, *rows, table, fx, fy]
    given = len(args)
    return pl.pallas_call(
        functools.partial(prep_kernel, first),
        grid=(n // 32,),
        in_specs=[pl.BlockSpec((16, A * 128), block)]
        + [whole(a) for a in args[1:]]
        + [pl.BlockSpec(memory_space=pltpu.HBM)] * len(held),
        out_specs=[pl.BlockSpec((2, A * 8, 128), lambda i: (i + first, 0, 0))]
        + [pl.BlockSpec((16, 19 * 128), block)] * 4,
        scratch_shapes=[
            pltpu.VMEM((16, A * 128), F32),
            pltpu.VMEM((16, A * 128), F32),
            pltpu.VMEM((128, 128), F32),
            pltpu.VMEM((256, 128), F32),
        ],
        out_shape=[jax.ShapeDtypeStruct((n // 8, A * 8, 128), BF)]
        + [jax.ShapeDtypeStruct((n, 19 * 128), BF)] * 4,
        input_output_aliases={given + i: i for i in range(len(held))},
        compiler_params=pltpu.CompilerParams(vmem_limit_bytes=PREP_MIB * MIB),
        cost_estimate=pl.CostEstimate(
            flops=20_000_000, bytes_accessed=4_000_000, transcendentals=0
        ),
        name="prep",
    )(*args, *held)


def repeat(step):
    @pl.loop(0, M // 4)
    def _(i):
        for u in range(4):
            step(4 * i + u)

    step(M - 1)


def spectra_kernel(w_ref, f_ref, p_ref, s):
    for g in range(8):
        y = jnp.concatenate([w_ref[2 * g], w_ref[2 * g + 1]], axis=1)
        s[:, 256 * g : 256 * g + 256] = jnp.dot(f_ref[...], y, preferred_element_type=F32)

    def turn(m):
        for i in range(2):
            row = pl.multiple_of(m * 16 + 8 * i, 8)
            v = jnp.concatenate([s[pl.ds(row, 8), 128 * g : 128 * g + 128] for g in range(16)], axis=0)
            p_ref[m, :, 128 * i : 128 * i + 128] = v.T.astype(BF)

    repeat(turn)


def spectra(w, fwd_k):
    v = pl.BlockSpec(memory_space=pltpu.VMEM)
    return pl.pallas_call(
        spectra_kernel,
        in_specs=[v, v],
        out_specs=v,
        out_shape=jax.ShapeDtypeStruct((M, 128, 256), BF),
        scratch_shapes=[pltpu.VMEM((2 * M * 8, 2048), F32)],
        compiler_params=pltpu.CompilerParams(vmem_limit_bytes=16 * MIB),
        cost_estimate=pl.CostEstimate(flops=1000, bytes_accessed=1000, transcendentals=0),
        name="spectra",
    )(w, fwd_k)


def ref_kernel(b_ref, f_ref, r_ref, s):
    for y in range(4):
        for xh in range(2):
            for t in range(9):
                v = b_ref[y, xh, :, t * 128 : (t + 1) * 128].astype(F32)
                row = (y * 2 + xh) * 72 + 8 * t
                s[row : row + 8, 0:128] = v[0:8]
                s[row : row + 8, 128:256] = v[8:16]
    out = jnp.dot(f_ref[...], s[...].astype(BF), preferred_element_type=F32)
    for m in range(M):
        for i in range(2):
            r = 16 * m + 8 * i
            r_ref[m, :, 128 * i : 128 * i + 128] = jnp.concatenate(
                [out[r : r + 8, 0:128], out[r : r + 8, 128:256]], axis=0
            ).astype(BF)


def ref_spectra(blocks, fwd_k):
    v = pl.BlockSpec(memory_space=pltpu.VMEM)
    return pl.pallas_call(
        ref_kernel,
        in_specs=[v, v],
        out_specs=v,
        out_shape=jax.ShapeDtypeStruct((M, 16, 256), BF),
        scratch_shapes=[pltpu.VMEM((A * 8, 256), F32)],
        compiler_params=pltpu.CompilerParams(vmem_limit_bytes=8 * MIB),
        cost_estimate=pl.CostEstimate(flops=1000, bytes_accessed=1000, transcendentals=0),
        name="ref_spectra",
    )(blocks, fwd_k)


def score_kernel(*refs):
    p_ref, blocks, inv_ref, o_ref, xs = refs[0], refs[1:5], refs[5], refs[6], refs[7]
    xs[:, 2 * M * 8 :, :] = jnp.zeros((16, K_INV - 2 * M * 8, 256), BF)

    def cross(m):
        upper = p_ref[m]
        re, im = upper[:, 0:128], upper[:, 128:256]
        rhs = jnp.concatenate([upper, jnp.concatenate([im, -re], axis=1)], axis=0)
        lhs = jnp.concatenate([b[i, m] for b in blocks for i in range(4)], axis=0)
        x = jnp.dot(lhs, rhs, preferred_element_type=F32)
        row = pl.multiple_of(m * 16, 16)
        for g in range(16):
            for h in range(2):
                k = 16 * g + 8 * h
                xs[g, pl.ds(row, 16), 128 * h : 128 * h + 128] = jnp.concatenate(
                    [x[k : k + 8, 0:128], x[k : k + 8, 128:256]], axis=0
                ).astype(BF)

    repeat(cross)

    def four(i, best):
        for u in range(4):
            y = jnp.dot(inv_ref[...], xs[4 * i + u], preferred_element_type=F32)
            for t in range(A):
                best = jnp.maximum(best, y[8 * t : 8 * t + 8])
        return best

    best = lax.fori_loop(0, 4, four, jnp.full((8, 256), -jnp.inf, F32))
    best = jnp.max(best, axis=0, keepdims=True)
    o_ref[...] = jnp.maximum(best[:, 0:128], best[:, 128:256])


def scores_of(p, blocks, inv_k):
    v = pl.BlockSpec(memory_space=pltpu.VMEM)
    return pl.pallas_call(
        score_kernel,
        in_specs=[v] * 6,
        out_specs=v,
        out_shape=jax.ShapeDtypeStruct((1, 128), F32),
        scratch_shapes=[pltpu.VMEM((16, K_INV, 256), BF)],
        compiler_params=pltpu.CompilerParams(vmem_limit_bytes=20 * MIB),
        cost_estimate=pl.CostEstimate(flops=6_000_000_000, bytes_accessed=8_000_000, transcendentals=0),
        name="scores",
    )(p, *blocks, inv_k)


def sums_kernel(sc, h0, h1, h2, h3, tab_ref, mine, other, acc, rows, sems):
    copies = [
        pltpu.make_async_copy(h, rows.at[pl.ds(128 * i, 128)], sems.at[i])
        for i, h in enumerate((h0, h1, h2, h3))
    ]
    for c in copies:
        c.start()
    for c in copies:
        c.wait()
    width = 18 * 128
    lane = lax.broadcasted_iota(jnp.int32, (128, 256), 1).astype(F32)
    picks, groups = [], []
    for i in range(4):
        meta = rows[128 * i : 128 * i + 128, width : width + 128].astype(F32)
        picks.append(jnp.where(lane == meta[:, 0:1], 1.0, 0.0).astype(F32).T.astype(BF))
        groups.append(jnp.where(lane == meta[:, 1:2], 1.0, 0.0).astype(BF))
    pick = jnp.concatenate(picks, axis=1)
    group = jnp.concatenate(groups, axis=0)
    count = jnp.dot(pick, group, preferred_element_type=F32)
    flipped = tab_ref[...].T
    tab = jnp.concatenate([flipped, flipped], axis=1)
    wsum = jnp.dot(count, tab * tab, precision=lax.Precision.HIGHEST, preferred_element_type=F32)
    for t in range(9):
        cols = slice(256 * t, 256 * t + 256)
        acc[:, cols] = jnp.dot(pick, rows[:, cols], preferred_element_type=F32)
    left = lax.broadcasted_iota(jnp.int32, (256, 128), 1) < R
    for ref, core in ((mine, sc[2]), (other, 1 - sc[2])):
        for xh in range(2):
            start = pl.multiple_of((9 * xh + 4 * core) * 128, 128)
            ref[xh] = acc[:, pl.ds(start, 640)]
            mid = acc[:, (9 * xh + 4) * 128 : (9 * xh + 5) * 128]
            keep = jnp.logical_xor(left, core == 1)
            ref[xh, :, pl.ds(pl.multiple_of((1 - core) * 512, 128), 128)] = jnp.where(keep, mid, wsum)


def class_sums(sc, cs, tab):
    v = pl.BlockSpec(memory_space=pltpu.VMEM)
    hbm = pl.BlockSpec(memory_space=pltpu.HBM)
    shape = jax.ShapeDtypeStruct((2, 256, 640), F32)
    return pl.pallas_call(
        sums_kernel,
        in_specs=[pl.BlockSpec(memory_space=pltpu.SMEM)] + [hbm] * 4 + [v],
        out_specs=[v, v],
        out_shape=[shape, shape],
        scratch_shapes=[
            pltpu.VMEM((256, 18 * 128), F32),
            pltpu.VMEM((512, 19 * 128), BF),
            pltpu.SemaphoreType.DMA((4,)),
        ],
        compiler_params=pltpu.CompilerParams(vmem_limit_bytes=56 * MIB),
        cost_estimate=pl.CostEstimate(flops=700_000_000, bytes_accessed=5_000_000, transcendentals=0),
        name="class_sums",
    )(sc, *cs, tab)


def cut_x_kernel(sc, a_ref, b_ref, o0, o1, o2, o3):
    for dx, o in enumerate((o0, o1, o2, o3)):
        x = lax.rem(sc[1] + dx, 4)
        xh, xl = x // 2, lax.rem(x, 2)
        rows = pl.ds(pl.multiple_of(xl * 128, 128), 128)
        o[...] = a_ref[xh, rows, :] + b_ref[xh, rows, :]


def cut_x(sc, a, b):
    v = pl.BlockSpec(memory_space=pltpu.VMEM)
    return pl.pallas_call(
        cut_x_kernel,
        in_specs=[pl.BlockSpec(memory_space=pltpu.SMEM), v, v],
        out_specs=[v] * 4,
        out_shape=[jax.ShapeDtypeStruct((128, 640), F32)] * 4,
        compiler_params=pltpu.CompilerParams(vmem_limit_bytes=VMEM_LIMIT),
        cost_estimate=pl.CostEstimate(flops=400_000, bytes_accessed=3_900_000, transcendentals=0),
        name="cut_x",
    )(sc, a, b)


def cut_z_kernel(sc, a0, a1, a2, a3, o0, o1, o2, o3):
    for dz, o in enumerate((o0, o1, o2, o3)):
        z = lax.rem(sc[3] + dz, 4)
        rows = pl.ds(pl.multiple_of(z * 32, 32), 32)
        o[...] = (a0[rows, :] + a1[rows, :]) + (a2[rows, :] + a3[rows, :])


def cut_z(sc, parts):
    v = pl.BlockSpec(memory_space=pltpu.VMEM)
    return pl.pallas_call(
        cut_z_kernel,
        in_specs=[pl.BlockSpec(memory_space=pltpu.SMEM)] + [v] * 4,
        out_specs=[v] * 4,
        out_shape=[jax.ShapeDtypeStruct((32, 640), F32)] * 4,
        compiler_params=pltpu.CompilerParams(vmem_limit_bytes=VMEM_LIMIT),
        cost_estimate=pl.CostEstimate(flops=400_000, bytes_accessed=1_700_000, transcendentals=0),
        name="cut_z",
    )(sc, *parts)


def final_kernel(sc, a0, a1, a2, a3, o_ref):
    s = (a0[...] + a1[...]) + (a2[...] + a3[...])
    odd = sc[2] == 1
    left = lax.broadcasted_iota(jnp.int32, (32, 128), 1) < R
    tile = [s[:, 128 * t : 128 * t + 128] for t in range(5)]
    held = jnp.where(odd, tile[0], tile[4])
    turned = pltpu.roll(held, R, 1)
    weight = jnp.where(jnp.logical_xor(left, odd), turned, held)
    tile = [t / (weight + TAU) for t in tile]
    rolled = [pltpu.roll(t, R, 1) for t in tile]
    later = [jnp.where(left, rolled[t], rolled[t + 1]) for t in range(4)] + [rolled[4]]
    for t in range(4):
        o_ref[:, 128 * t : 128 * t + 128] = jnp.where(odd, later[t], tile[t])[0:25]
    o_ref[:, 512:576] = jnp.where(odd, later[4], tile[4])[0:25, 0:R]


def final(sc, parts):
    v = pl.BlockSpec(memory_space=pltpu.VMEM)
    return pl.pallas_call(
        final_kernel,
        in_specs=[pl.BlockSpec(memory_space=pltpu.SMEM)] + [v] * 4,
        out_specs=v,
        out_shape=jax.ShapeDtypeStruct((25, 576), F32),
        name="final",
    )(sc, *parts)


def place(y, x, z, core):
    return ((y % 4) * 4 + (x % 4) // 2 * 2 + core % 2) * 8 + (x % 2) * 4 + z % 4


def permutation(move):
    return [
        (place(y, x, z, c), place(*move(y, x, z, c)))
        for y in range(4)
        for x in range(4)
        for z in range(4)
        for c in range(2)
    ]


CORE = permutation(lambda y, x, z, c: (y, x, z, c + 1))
HIGH = permutation(lambda y, x, z, c: (y, x + 2, z, c))
LOW = permutation(lambda y, x, z, c: (y, x ^ 1, z, c))
Y_NEAR = permutation(lambda y, x, z, c: (y ^ 1, x, z, c))
Y_FAR = permutation(lambda y, x, z, c: (y + 2, x, z, c))
YS = [permutation(lambda y, x, z, c, d=d: (y + d, x, z, c)) for d in range(4)]
XS = [permutation(lambda y, x, z, c, d=d: (y, x + d, z, c)) for d in range(4)]
ZS = [permutation(lambda y, x, z, c, d=d: (y, x, z + d, c)) for d in range(4)]


def move(value, pairs):
    return lax.ppermute(value, AXES, pairs)


def join(own, other, upper):
    lower = upper == 0
    return jnp.stack([jnp.where(lower, own, other), jnp.where(lower, other, own)])


def per_device(particles, references, owner, class_offset, rotation, shifts, ctf_group, ctf_table):
    fwd_np, inv_np = tables()
    fwd_k, inv_k = jnp.asarray(fwd_np), jnp.asarray(inv_np)
    fx, fy = (jnp.asarray(t) for t in freq_tables())
    dom, cls = lax.axis_index("dom"), lax.axis_index("cls")
    y, xh, core = dom // 4, dom // 2 % 2, dom % 2
    xl, z = cls // 4, cls % 4
    sc = jnp.stack([y, xh * 2 + xl, core, z]).astype(jnp.int32)

    low, high = references[0:16], references[9:25]
    first = core == 0
    keep = jnp.where(first, low, high)
    give = jnp.where(first, high, low)
    got = move(give, CORE)
    block = jnp.where(
        first, jnp.concatenate([keep, got], axis=1), jnp.concatenate([got, keep], axis=1)
    )
    rows = [shifts.T, rotation[None], owner.T, class_offset[None], ctf_group[None]]
    table = ctf_table.T
    block, rows[1] = lax.optimization_barrier((block, rows[1]))
    half = prep(particles, rows, table, fx, fy, 0)
    far = move(block, HIGH)
    far, *half = lax.optimization_barrier((far, *half))
    pair = join(block, far, xh)
    pair, rows[1] = lax.optimization_barrier((pair, rows[1]))
    weighted, *sent = prep(particles, rows, table, fx, fy, 4, half)
    near = move(pair, Y_NEAR)
    near, weighted, *sent = lax.optimization_barrier((near, weighted, *sent))
    quad = join(pair, near, y % 2)
    octet = join(quad, move(quad, Y_FAR), y // 2).reshape(4, 2, 16, 1152)

    held = [sent[0]] + [move(sent[d], YS[d]) for d in (1, 2, 3)]
    part = spectra(weighted, fwd_k)

    own = ref_spectra(octet, fwd_k)
    up, down = move(own, ZS[1]), move(own, ZS[3])
    side = move(own, LOW)
    side_up, side_down = move(side, ZS[1]), move(side, ZS[3])
    *held, side, up, down, part = lax.optimization_barrier((*held, side, up, down, part))
    on_up, on_down = move(up, ZS[1]), move(side_down, ZS[3])
    early, late = jnp.stack([own, side, up, down]), jnp.stack([side_up, side_down, on_up, on_down])
    early_twin, late_twin = move(early, CORE), move(late, CORE)
    *held, side_up, side_down, early_twin = lax.optimization_barrier((*held, side_up, side_down, early_twin))
    mine, other = class_sums(sc, held, table)
    other = move(other, CORE)
    cut = cut_x(sc, mine, other)
    cut = [cut[0]] + [move(cut[d], XS[d]) for d in (1, 2, 3)]
    scores = scores_of(part, [early, early_twin, late, late_twin], inv_k)
    *cut, scores = lax.optimization_barrier((*cut, scores))
    cut = cut_z(sc, cut)
    cut = [cut[0]] + [move(cut[d], ZS[d]) for d in (1, 2, 3)]
    return scores[0], final(sc, cut)


def solution(mesh):
    return jax.shard_map(
        per_device,
        mesh=mesh,
        in_specs=(
            P(("dom", "cls"), None),
            P("cls", "dom"),
            P(("dom", "cls"), None),
            P(("dom", "cls")),
            P(("dom", "cls")),
            P(("dom", "cls"), None),
            P(("dom", "cls")),
            P(),
        ),
        out_specs=(P(("dom", "cls")), P("cls", "dom")),
        check_vma=False,
    )
```

```python
import functools

import jax
import jax.numpy as jnp
import numpy as np
from jax import lax
from jax.experimental import pallas as pl
from jax.experimental.pallas import tpu as pltpu
from jax.sharding import PartitionSpec as P

A = 72
M = 37
R = 64
BOX = 128
TAU = 1.0
AXES = ("dom", "cls")
BF = jnp.bfloat16
F32 = jnp.float32
MIB = 1024 * 1024
VMEM_LIMIT = 8 * MIB
PREP_MIB = 56
K_INV = 640


def tables():
    m = np.arange(M)[:, None]
    a = np.arange(A)[None, :]
    turn = 2.0 * np.pi * ((m * a) % A) / A
    fwd = np.stack([np.cos(turn), -np.sin(turn)], axis=1).reshape(2 * M, A)
    gain = np.where((np.arange(M) == 0) | (np.arange(M) == A // 2), 1.0, 2.0)[:, None]
    inv = np.stack([np.cos(turn) / A, -np.sin(turn) / A], axis=1).astype(BF).astype(np.float32)
    inv = (inv * gain[:, None, :]).reshape(2 * M, A).T
    eye = np.eye(8, dtype=np.float32)
    fwd_k = np.kron(fwd.astype(np.float32), eye).astype(BF)
    inv_k = np.zeros((A * 8, K_INV), np.float32)
    inv_k[:, : 2 * M * 8] = np.kron(inv, eye)
    return fwd_k, inv_k.astype(BF)


def freq_tables():
    angle = 2.0 * np.pi * np.arange(A // 2) / A
    radius = np.tile(np.arange(1, R + 1), 2)
    fx = np.cos(angle)[:, None] * radius[None, :] / BOX
    fy = np.sin(angle)[:, None] * radius[None, :] / BOX
    return fx.astype(np.float32), fy.astype(np.float32)


def cos_poly():
    n = 7
    nodes = (np.cos((np.arange(64) + 0.5) * np.pi / 64) + 1.0) / 8.0
    return [float(c) for c in np.polynomial.chebyshev.Chebyshev.fit(
        nodes, np.cos(2.0 * np.pi * np.sqrt(nodes)), n - 1, domain=[0.0, 0.25]
    ).convert(kind=np.polynomial.Polynomial).coef]


COEF = cos_poly()


def prep_kernel(first, x_ref, shift_ref, rot_ref, own_ref, off_ref, grp_ref, tab_ref, fx_ref, fy_ref, *refs):
    w_ref, c0, c1, c2, c3, ws, us, aux, tab = refs[-9:]
    dom, cls = lax.axis_index("dom"), lax.axis_index("cls")
    mine = 2 * (dom * 8 + cls)
    step = pl.program_id(0)

    @pl.when(step == 0)
    def _():
        shift_rows = shift_ref[...].astype(F32)
        group = grp_ref[...]
        rows = [
            shift_rows,
            rot_ref[...].astype(F32),
            (group - mine).astype(F32),
            (own_ref[...] * 32 + off_ref[...]).astype(F32),
            group.astype(F32),
            jnp.zeros((122, 128), F32),
        ]
        aux[...] = jnp.concatenate(rows, axis=0).T
        flipped = tab_ref[...].T
        tab[...] = jnp.concatenate([flipped, flipped], axis=1)

    here = aux[pl.ds(pl.multiple_of((step + first) * 16, 16), 16), :]
    lane = lax.broadcasted_iota(jnp.int32, (16, 128), 1)
    left = lane < R
    shift = jnp.where(left, 0.0, -0.25).astype(F32)
    sxb = jnp.broadcast_to(here[:, 0:1], (16, 128))
    syb = jnp.broadcast_to(here[:, 1:2], (16, 128))
    ctf = jnp.where(here[:, 3:4] > 0.5, tab[pl.ds(mine + 1, 1), :], tab[pl.ds(mine, 1), :])
    ctf_s = jnp.where(left, -ctf, ctf)
    for b in range(A // 4):
        done = []
        for a in (2 * b, 2 * b + 1):
            v = (sxb * fx_ref[a : a + 1, :] + syb * fy_ref[a : a + 1, :]) + shift
            v = v - jnp.round(v)
            q = v * v
            e = jnp.full_like(q, COEF[-1])
            for k in COEF[-2::-1]:
                e = e * q + k
            er = pltpu.roll(e, R, 1)
            cc = jnp.where(left, e, er) * ctf
            ss = jnp.where(left, er, e) * ctf_s
            x0 = x_ref[:, a * 128 : (a + 1) * 128].astype(F32)
            h = a + A // 2
            x1 = x_ref[:, h * 128 : (h + 1) * 128].astype(F32)
            w0 = x0 * cc + pltpu.roll(x0, R, 1) * ss
            w1 = x1 * cc - pltpu.roll(x1, R, 1) * ss
            ws[:, a * 128 : (a + 1) * 128] = w0
            ws[:, h * 128 : (h + 1) * 128] = w1
            done.append((w0, w1))
        for half in (0, 1):
            row = (2 * b + half * (A // 2)) * 8
            for g in (0, 1):
                w_ref[g, row : row + 16, :] = jnp.concatenate(
                    [done[0][half][8 * g : 8 * g + 8], done[1][half][8 * g : 8 * g + 8]], axis=0
                ).astype(BF)
    rotb = jnp.broadcast_to(here[:, 2:3], (16, 128)).astype(jnp.int32)
    bit = [(rotb & (1 << k)) != 0 for k in range(7)]
    for r in range(8):
        t = [ws[:, (r + 8 * n) * 128 : (r + 8 * n + 1) * 128] for n in range(9)]
        for k in range(4):
            t = [jnp.where(bit[3 + k], t[(n + (1 << k)) % 9], t[n]) for n in range(9)]
        for n in range(9):
            us[:, (r + 8 * n) * 128 : (r + 8 * n + 1) * 128] = t[n]
    for j0 in range(0, A, 8):
        t = [us[:, ((j0 + i) % A) * 128 : ((j0 + i) % A + 1) * 128] for i in range(15)]
        t = [jnp.where(bit[0], t[i + 1], t[i]) for i in range(14)]
        t = [jnp.where(bit[1], t[i + 2], t[i]) for i in range(12)]
        for i in range(8):
            ws[:, (j0 + i) * 128 : (j0 + i + 1) * 128] = jnp.where(bit[2], t[i + 4], t[i])
    meta = jnp.where(lane == 0, here[:, 4:5], jnp.where(lane == 1, here[:, 5:6], 0.0)).astype(BF)
    width = 18 * 128
    for dy, c_ref in enumerate((c0, c1, c2, c3)):
        dest = lax.rem(dom // 4 + dy, 4)
        start = pl.multiple_of(dest * width, 128)
        c_ref[:, 0:width] = ws[:, pl.ds(start, width)].astype(BF)
        c_ref[:, width : width + 128] = meta


def prep(particles, rows, table, fx, fy, first, held=()):
    n = particles.shape[0]
    whole = lambda a: pl.BlockSpec(a.shape, lambda i: (0,) * a.ndim)
    block = lambda i: (i + first, 0)
    args = [particles, *rows, table, fx, fy]
    given = len(args)
    return pl.pallas_call(
        functools.partial(prep_kernel, first),
        grid=(n // 32,),
        in_specs=[pl.BlockSpec((16, A * 128), block)]
        + [whole(a) for a in args[1:]]
        + [pl.BlockSpec(memory_space=pltpu.HBM)] * len(held),
        out_specs=[pl.BlockSpec((2, A * 8, 128), lambda i: (i + first, 0, 0))]
        + [pl.BlockSpec((16, 19 * 128), block)] * 4,
        scratch_shapes=[
            pltpu.VMEM((16, A * 128), F32),
            pltpu.VMEM((16, A * 128), F32),
            pltpu.VMEM((128, 128), F32),
            pltpu.VMEM((256, 128), F32),
        ],
        out_shape=[jax.ShapeDtypeStruct((n // 8, A * 8, 128), BF)]
        + [jax.ShapeDtypeStruct((n, 19 * 128), BF)] * 4,
        input_output_aliases={given + i: i for i in range(len(held))},
        compiler_params=pltpu.CompilerParams(vmem_limit_bytes=PREP_MIB * MIB),
        cost_estimate=pl.CostEstimate(
            flops=20_000_000, bytes_accessed=4_000_000, transcendentals=0
        ),
        name="prep",
    )(*args, *held)


def repeat(step):
    @pl.loop(0, M // 4)
    def _(i):
        for u in range(4):
            step(4 * i + u)

    step(M - 1)


def spectra_kernel(w_ref, f_ref, p_ref, s):
    for g in range(8):
        y = jnp.concatenate([w_ref[2 * g], w_ref[2 * g + 1]], axis=1)
        s[:, 256 * g : 256 * g + 256] = jnp.dot(f_ref[...], y, preferred_element_type=F32)

    def turn(m):
        for i in range(2):
            row = pl.multiple_of(m * 16 + 8 * i, 8)
            v = jnp.concatenate([s[pl.ds(row, 8), 128 * g : 128 * g + 128] for g in range(16)], axis=0)
            p_ref[m, :, 128 * i : 128 * i + 128] = v.T.astype(BF)

    repeat(turn)


def spectra(w, fwd_k):
    v = pl.BlockSpec(memory_space=pltpu.VMEM)
    return pl.pallas_call(
        spectra_kernel,
        in_specs=[v, v],
        out_specs=v,
        out_shape=jax.ShapeDtypeStruct((M, 128, 256), BF),
        scratch_shapes=[pltpu.VMEM((2 * M * 8, 2048), F32)],
        compiler_params=pltpu.CompilerParams(vmem_limit_bytes=16 * MIB),
        cost_estimate=pl.CostEstimate(flops=1000, bytes_accessed=1000, transcendentals=0),
        name="spectra",
    )(w, fwd_k)


def ref_kernel(b_ref, f_ref, r_ref, s):
    for y in range(4):
        for xh in range(2):
            for t in range(9):
                v = b_ref[y, xh, :, t * 128 : (t + 1) * 128].astype(F32)
                row = (y * 2 + xh) * 72 + 8 * t
                s[row : row + 8, 0:128] = v[0:8]
                s[row : row + 8, 128:256] = v[8:16]
    out = jnp.dot(f_ref[...], s[...].astype(BF), preferred_element_type=F32)
    for m in range(M):
        for i in range(2):
            r = 16 * m + 8 * i
            r_ref[m, :, 128 * i : 128 * i + 128] = jnp.concatenate(
                [out[r : r + 8, 0:128], out[r : r + 8, 128:256]], axis=0
            ).astype(BF)


def ref_spectra(blocks, fwd_k):
    v = pl.BlockSpec(memory_space=pltpu.VMEM)
    return pl.pallas_call(
        ref_kernel,
        in_specs=[v, v],
        out_specs=v,
        out_shape=jax.ShapeDtypeStruct((M, 16, 256), BF),
        scratch_shapes=[pltpu.VMEM((A * 8, 256), F32)],
        compiler_params=pltpu.CompilerParams(vmem_limit_bytes=8 * MIB),
        cost_estimate=pl.CostEstimate(flops=1000, bytes_accessed=1000, transcendentals=0),
        name="ref_spectra",
    )(blocks, fwd_k)


def score_kernel(*refs):
    p_ref, blocks, inv_ref, o_ref, xs = refs[0], refs[1:5], refs[5], refs[6], refs[7]
    xs[:, 2 * M * 8 :, :] = jnp.zeros((16, K_INV - 2 * M * 8, 256), BF)

    def cross(m):
        upper = p_ref[m]
        re, im = upper[:, 0:128], upper[:, 128:256]
        rhs = jnp.concatenate([upper, jnp.concatenate([im, -re], axis=1)], axis=0)
        lhs = jnp.concatenate([b[i, m] for b in blocks for i in range(4)], axis=0)
        x = jnp.dot(lhs, rhs, preferred_element_type=F32)
        row = pl.multiple_of(m * 16, 16)
        for g in range(16):
            for h in range(2):
                k = 16 * g + 8 * h
                xs[g, pl.ds(row, 16), 128 * h : 128 * h + 128] = jnp.concatenate(
                    [x[k : k + 8, 0:128], x[k : k + 8, 128:256]], axis=0
                ).astype(BF)

    repeat(cross)

    def four(i, best):
        for u in range(4):
            y = jnp.dot(inv_ref[...], xs[4 * i + u], preferred_element_type=F32)
            for t in range(A):
                best = jnp.maximum(best, y[8 * t : 8 * t + 8])
        return best

    best = lax.fori_loop(0, 4, four, jnp.full((8, 256), -jnp.inf, F32))
    best = jnp.max(best, axis=0, keepdims=True)
    o_ref[...] = jnp.maximum(best[:, 0:128], best[:, 128:256])


def scores_of(p, blocks, inv_k):
    v = pl.BlockSpec(memory_space=pltpu.VMEM)
    return pl.pallas_call(
        score_kernel,
        in_specs=[v] * 6,
        out_specs=v,
        out_shape=jax.ShapeDtypeStruct((1, 128), F32),
        scratch_shapes=[pltpu.VMEM((16, K_INV, 256), BF)],
        compiler_params=pltpu.CompilerParams(vmem_limit_bytes=20 * MIB),
        cost_estimate=pl.CostEstimate(flops=6_000_000_000, bytes_accessed=8_000_000, transcendentals=0),
        name="scores",
    )(p, *blocks, inv_k)


def sums_kernel(sc, c0, c1, c2, c3, tab_ref, mine, other, acc):
    width = 18 * 128
    lane = lax.broadcasted_iota(jnp.int32, (128, 256), 1).astype(F32)
    picks, groups = [], []
    for c in (c0, c1, c2, c3):
        meta = c[:, width : width + 128].astype(F32)
        picks.append(jnp.where(lane == meta[:, 0:1], 1.0, 0.0).astype(F32).T.astype(BF))
        groups.append(jnp.where(lane == meta[:, 1:2], 1.0, 0.0).astype(BF))
    pick = jnp.concatenate(picks, axis=1)
    group = jnp.concatenate(groups, axis=0)
    count = jnp.dot(pick, group, preferred_element_type=F32)
    flipped = tab_ref[...].T
    tab = jnp.concatenate([flipped, flipped], axis=1)
    wsum = jnp.dot(count, tab * tab, precision=lax.Precision.HIGHEST, preferred_element_type=F32)
    for t in range(9):
        cols = slice(256 * t, 256 * t + 256)
        x = jnp.concatenate([c[:, cols] for c in (c0, c1, c2, c3)], axis=0)
        acc[:, cols] = jnp.dot(pick, x, preferred_element_type=F32)
    left = lax.broadcasted_iota(jnp.int32, (256, 128), 1) < R
    for ref, core in ((mine, sc[2]), (other, 1 - sc[2])):
        for xh in range(2):
            start = pl.multiple_of((9 * xh + 4 * core) * 128, 128)
            ref[xh] = acc[:, pl.ds(start, 640)]
            mid = acc[:, (9 * xh + 4) * 128 : (9 * xh + 5) * 128]
            keep = jnp.logical_xor(left, core == 1)
            ref[xh, :, pl.ds(pl.multiple_of((1 - core) * 512, 128), 128)] = jnp.where(keep, mid, wsum)


def class_sums(sc, cs, tab):
    v = pl.BlockSpec(memory_space=pltpu.VMEM)
    shape = jax.ShapeDtypeStruct((2, 256, 640), F32)
    return pl.pallas_call(
        sums_kernel,
        in_specs=[pl.BlockSpec(memory_space=pltpu.SMEM)] + [v] * 5,
        out_specs=[v, v],
        out_shape=[shape, shape],
        scratch_shapes=[pltpu.VMEM((256, 18 * 128), F32)],
        compiler_params=pltpu.CompilerParams(vmem_limit_bytes=VMEM_LIMIT),
        cost_estimate=pl.CostEstimate(flops=700_000_000, bytes_accessed=5_000_000, transcendentals=0),
        name="class_sums",
    )(sc, *cs, tab)


def cut_x_kernel(sc, a_ref, b_ref, o0, o1, o2, o3):
    for dx, o in enumerate((o0, o1, o2, o3)):
        x = lax.rem(sc[1] + dx, 4)
        xh, xl = x // 2, lax.rem(x, 2)
        rows = pl.ds(pl.multiple_of(xl * 128, 128), 128)
        o[...] = a_ref[xh, rows, :] + b_ref[xh, rows, :]


def cut_x(sc, a, b):
    v = pl.BlockSpec(memory_space=pltpu.VMEM)
    return pl.pallas_call(
        cut_x_kernel,
        in_specs=[pl.BlockSpec(memory_space=pltpu.SMEM), v, v],
        out_specs=[v] * 4,
        out_shape=[jax.ShapeDtypeStruct((128, 640), F32)] * 4,
        compiler_params=pltpu.CompilerParams(vmem_limit_bytes=VMEM_LIMIT),
        cost_estimate=pl.CostEstimate(flops=400_000, bytes_accessed=3_900_000, transcendentals=0),
        name="cut_x",
    )(sc, a, b)


def cut_z_kernel(sc, a0, a1, a2, a3, o0, o1, o2, o3):
    for dz, o in enumerate((o0, o1, o2, o3)):
        z = lax.rem(sc[3] + dz, 4)
        rows = pl.ds(pl.multiple_of(z * 32, 32), 32)
        o[...] = (a0[rows, :] + a1[rows, :]) + (a2[rows, :] + a3[rows, :])


def cut_z(sc, parts):
    v = pl.BlockSpec(memory_space=pltpu.VMEM)
    return pl.pallas_call(
        cut_z_kernel,
        in_specs=[pl.BlockSpec(memory_space=pltpu.SMEM)] + [v] * 4,
        out_specs=[v] * 4,
        out_shape=[jax.ShapeDtypeStruct((32, 640), F32)] * 4,
        compiler_params=pltpu.CompilerParams(vmem_limit_bytes=VMEM_LIMIT),
        cost_estimate=pl.CostEstimate(flops=400_000, bytes_accessed=1_700_000, transcendentals=0),
        name="cut_z",
    )(sc, *parts)


def final_kernel(sc, a0, a1, a2, a3, o_ref):
    s = (a0[...] + a1[...]) + (a2[...] + a3[...])
    odd = sc[2] == 1
    left = lax.broadcasted_iota(jnp.int32, (32, 128), 1) < R
    tile = [s[:, 128 * t : 128 * t + 128] for t in range(5)]
    held = jnp.where(odd, tile[0], tile[4])
    turned = pltpu.roll(held, R, 1)
    weight = jnp.where(jnp.logical_xor(left, odd), turned, held)
    tile = [t / (weight + TAU) for t in tile]
    rolled = [pltpu.roll(t, R, 1) for t in tile]
    later = [jnp.where(left, rolled[t], rolled[t + 1]) for t in range(4)] + [rolled[4]]
    for t in range(4):
        o_ref[:, 128 * t : 128 * t + 128] = jnp.where(odd, later[t], tile[t])[0:25]
    o_ref[:, 512:576] = jnp.where(odd, later[4], tile[4])[0:25, 0:R]


def final(sc, parts):
    v = pl.BlockSpec(memory_space=pltpu.VMEM)
    return pl.pallas_call(
        final_kernel,
        in_specs=[pl.BlockSpec(memory_space=pltpu.SMEM)] + [v] * 4,
        out_specs=v,
        out_shape=jax.ShapeDtypeStruct((25, 576), F32),
        compiler_params=pltpu.CompilerParams(vmem_limit_bytes=2 * MIB),
        name="final",
    )(sc, *parts)


def place(y, x, z, core):
    return ((y % 4) * 4 + (x % 4) // 2 * 2 + core % 2) * 8 + (x % 2) * 4 + z % 4


def permutation(move):
    return [
        (place(y, x, z, c), place(*move(y, x, z, c)))
        for y in range(4)
        for x in range(4)
        for z in range(4)
        for c in range(2)
    ]


CORE = permutation(lambda y, x, z, c: (y, x, z, c + 1))
HIGH = permutation(lambda y, x, z, c: (y, x + 2, z, c))
LOW = permutation(lambda y, x, z, c: (y, x ^ 1, z, c))
Y_NEAR = permutation(lambda y, x, z, c: (y ^ 1, x, z, c))
Y_FAR = permutation(lambda y, x, z, c: (y + 2, x, z, c))
YS = [permutation(lambda y, x, z, c, d=d: (y + d, x, z, c)) for d in range(4)]
XS = [permutation(lambda y, x, z, c, d=d: (y, x + d, z, c)) for d in range(4)]
ZS = [permutation(lambda y, x, z, c, d=d: (y, x, z + d, c)) for d in range(4)]


def move(value, pairs):
    return lax.ppermute(value, AXES, pairs)


def after(values, *others):
    return lax.optimization_barrier((*values, *others))[: len(values)]


def join(own, other, upper):
    lower = upper == 0
    return jnp.stack([jnp.where(lower, own, other), jnp.where(lower, other, own)])


def per_device(particles, references, owner, class_offset, rotation, shifts, ctf_group, ctf_table):
    fwd_np, inv_np = tables()
    fwd_k, inv_k = jnp.asarray(fwd_np), jnp.asarray(inv_np)
    fx, fy = (jnp.asarray(t) for t in freq_tables())
    dom, cls = lax.axis_index("dom"), lax.axis_index("cls")
    y, xh, core = dom // 4, dom // 2 % 2, dom % 2
    xl, z = cls // 4, cls % 4
    sc = jnp.stack([y, xh * 2 + xl, core, z]).astype(jnp.int32)

    low, high = references[0:16], references[9:25]
    first = core == 0
    keep = jnp.where(first, low, high)
    give = jnp.where(first, high, low)
    got = move(give, CORE)
    block = jnp.where(
        first, jnp.concatenate([keep, got], axis=1), jnp.concatenate([got, keep], axis=1)
    )
    rows = [shifts.T, rotation[None], owner.T, class_offset[None], ctf_group[None]]
    table = ctf_table.T
    block, rows[1] = lax.optimization_barrier((block, rows[1]))
    half = prep(particles, rows, table, fx, fy, 0)
    far = move(block, HIGH)
    far, *half = lax.optimization_barrier((far, *half))
    pair = join(block, far, xh)
    pair, rows[1] = lax.optimization_barrier((pair, rows[1]))
    weighted, *sent = prep(particles, rows, table, fx, fy, 4, half)
    near = move(pair, Y_NEAR)
    near, weighted, *sent = lax.optimization_barrier((near, weighted, *sent))
    quad = join(pair, near, y % 2)
    octet = join(quad, move(quad, Y_FAR), y // 2).reshape(4, 2, 16, 1152)

    held = [sent[0]] + [move(sent[d], YS[d]) for d in (1, 2, 3)]
    part = spectra(weighted, fwd_k)

    own = ref_spectra(octet, fwd_k)
    up, down = move(own, ZS[1]), move(own, ZS[3])
    side = move(own, LOW)
    side_up, side_down = move(side, ZS[1]), move(side, ZS[3])
    on_up, on_down = move(up, ZS[1]), move(side_down, ZS[3])
    early = jnp.stack([own, side, up, down])
    early_twin = move(early, CORE)
    held = after(held, side, up, down, side_up, side_down, part)
    held = after(held, on_up, on_down)
    mine, other = class_sums(sc, held, table)
    cut = cut_x(sc, mine, move(other, CORE))
    late = jnp.stack([side_up, side_down, on_up, on_down])
    late_twin = move(late, CORE)
    cut = [cut[0]] + [move(cut[d], XS[d]) for d in (1, 2, 3)]
    scores = scores_of(part, [early, early_twin, late, late_twin], inv_k)
    *cut, scores = lax.optimization_barrier((*cut, scores))
    cut = cut_z(sc, cut)
    cut = [cut[0]] + [move(cut[d], ZS[d]) for d in (1, 2, 3)]
    return scores[0], final(sc, cut)


def solution(mesh):
    return jax.shard_map(
        per_device,
        mesh=mesh,
        in_specs=(
            P(("dom", "cls"), None),
            P("cls", "dom"),
            P(("dom", "cls"), None),
            P(("dom", "cls")),
            P(("dom", "cls")),
            P(("dom", "cls"), None),
            P(("dom", "cls")),
            P(),
        ),
        out_specs=(P(("dom", "cls")), P("cls", "dom")),
        check_vma=False,
    )
```

```python
import functools

import jax
import jax.numpy as jnp
import numpy as np
from jax import lax
from jax.experimental import pallas as pl
from jax.experimental.pallas import tpu as pltpu
from jax.sharding import PartitionSpec as P

A = 72
M = 37
R = 64
BOX = 128
TAU = 1.0
AXES = ("dom", "cls")
BF = jnp.bfloat16
F32 = jnp.float32
MIB = 1024 * 1024
VMEM_LIMIT = 8 * MIB
PREP_MIB = 56
K_INV = 640


def tables():
    m = np.arange(M)[:, None]
    a = np.arange(A)[None, :]
    turn = 2.0 * np.pi * ((m * a) % A) / A
    fwd = np.stack([np.cos(turn), -np.sin(turn)], axis=1).reshape(2 * M, A)
    gain = np.where((np.arange(M) == 0) | (np.arange(M) == A // 2), 1.0, 2.0)[:, None]
    inv = np.stack([np.cos(turn) / A, -np.sin(turn) / A], axis=1).astype(BF).astype(np.float32)
    inv = (inv * gain[:, None, :]).reshape(2 * M, A).T
    eye = np.eye(8, dtype=np.float32)
    fwd_k = np.kron(fwd.astype(np.float32), eye).astype(BF)
    inv_k = np.zeros((A * 8, K_INV), np.float32)
    inv_k[:, : 2 * M * 8] = np.kron(inv, eye)
    return fwd_k, inv_k.astype(BF)


def freq_tables():
    angle = 2.0 * np.pi * np.arange(A // 2) / A
    radius = np.tile(np.arange(1, R + 1), 2)
    fx = np.cos(angle)[:, None] * radius[None, :] / BOX
    fy = np.sin(angle)[:, None] * radius[None, :] / BOX
    return fx.astype(np.float32), fy.astype(np.float32)


def cos_poly():
    n = 7
    nodes = (np.cos((np.arange(64) + 0.5) * np.pi / 64) + 1.0) / 8.0
    return [float(c) for c in np.polynomial.chebyshev.Chebyshev.fit(
        nodes, np.cos(2.0 * np.pi * np.sqrt(nodes)), n - 1, domain=[0.0, 0.25]
    ).convert(kind=np.polynomial.Polynomial).coef]


COEF = cos_poly()


def prep_kernel(first, x_ref, shift_ref, rot_ref, own_ref, off_ref, grp_ref, tab_ref, fx_ref, fy_ref, *refs):
    w_ref, c0, c1, c2, c3, ws, us, aux, tab = refs[-9:]
    dom, cls = lax.axis_index("dom"), lax.axis_index("cls")
    mine = 2 * (dom * 8 + cls)
    step = pl.program_id(0)

    @pl.when(step == 0)
    def _():
        shift_rows = shift_ref[...].astype(F32)
        group = grp_ref[...]
        rows = [
            shift_rows,
            rot_ref[...].astype(F32),
            (group - mine).astype(F32),
            (own_ref[...] * 32 + off_ref[...]).astype(F32),
            group.astype(F32),
            jnp.zeros((122, 128), F32),
        ]
        aux[...] = jnp.concatenate(rows, axis=0).T
        flipped = tab_ref[...].T
        tab[...] = jnp.concatenate([flipped, flipped], axis=1)

    here = aux[pl.ds(pl.multiple_of((step + first) * 16, 16), 16), :]
    lane = lax.broadcasted_iota(jnp.int32, (16, 128), 1)
    left = lane < R
    shift = jnp.where(left, 0.0, -0.25).astype(F32)
    sxb = jnp.broadcast_to(here[:, 0:1], (16, 128))
    syb = jnp.broadcast_to(here[:, 1:2], (16, 128))
    ctf = jnp.where(here[:, 3:4] > 0.5, tab[pl.ds(mine + 1, 1), :], tab[pl.ds(mine, 1), :])
    ctf_s = jnp.where(left, -ctf, ctf)
    for b in range(A // 4):
        done = []
        for a in (2 * b, 2 * b + 1):
            v = (sxb * fx_ref[a : a + 1, :] + syb * fy_ref[a : a + 1, :]) + shift
            v = v - jnp.round(v)
            q = v * v
            e = jnp.full_like(q, COEF[-1])
            for k in COEF[-2::-1]:
                e = e * q + k
            er = pltpu.roll(e, R, 1)
            cc = jnp.where(left, e, er) * ctf
            ss = jnp.where(left, er, e) * ctf_s
            x0 = x_ref[:, a * 128 : (a + 1) * 128].astype(F32)
            h = a + A // 2
            x1 = x_ref[:, h * 128 : (h + 1) * 128].astype(F32)
            w0 = x0 * cc + pltpu.roll(x0, R, 1) * ss
            w1 = x1 * cc - pltpu.roll(x1, R, 1) * ss
            ws[:, a * 128 : (a + 1) * 128] = w0
            ws[:, h * 128 : (h + 1) * 128] = w1
            done.append((w0, w1))
        for half in (0, 1):
            row = (2 * b + half * (A // 2)) * 8
            for g in (0, 1):
                w_ref[g, row : row + 16, :] = jnp.concatenate(
                    [done[0][half][8 * g : 8 * g + 8], done[1][half][8 * g : 8 * g + 8]], axis=0
                ).astype(BF)
    rotb = jnp.broadcast_to(here[:, 2:3], (16, 128)).astype(jnp.int32)
    bit = [(rotb & (1 << k)) != 0 for k in range(7)]
    for r in range(8):
        t = [ws[:, (r + 8 * n) * 128 : (r + 8 * n + 1) * 128] for n in range(9)]
        for k in range(4):
            t = [jnp.where(bit[3 + k], t[(n + (1 << k)) % 9], t[n]) for n in range(9)]
        for n in range(9):
            us[:, (r + 8 * n) * 128 : (r + 8 * n + 1) * 128] = t[n]
    for j0 in range(0, A, 8):
        t = [us[:, ((j0 + i) % A) * 128 : ((j0 + i) % A + 1) * 128] for i in range(15)]
        t = [jnp.where(bit[0], t[i + 1], t[i]) for i in range(14)]
        t = [jnp.where(bit[1], t[i + 2], t[i]) for i in range(12)]
        for i in range(8):
            ws[:, (j0 + i) * 128 : (j0 + i + 1) * 128] = jnp.where(bit[2], t[i + 4], t[i])
    meta = jnp.where(lane == 0, here[:, 4:5], jnp.where(lane == 1, here[:, 5:6], 0.0)).astype(BF)
    width = 18 * 128
    for dy, c_ref in enumerate((c0, c1, c2, c3)):
        dest = lax.rem(dom // 4 + dy, 4)
        start = pl.multiple_of(dest * width, 128)
        c_ref[:, 0:width] = ws[:, pl.ds(start, width)].astype(BF)
        c_ref[:, width : width + 128] = meta


def prep(particles, rows, table, fx, fy, first, held=()):
    n = particles.shape[0]
    whole = lambda a: pl.BlockSpec(a.shape, lambda i: (0,) * a.ndim)
    block = lambda i: (i + first, 0)
    args = [particles, *rows, table, fx, fy]
    given = len(args)
    return pl.pallas_call(
        functools.partial(prep_kernel, first),
        grid=(n // 32,),
        in_specs=[pl.BlockSpec((16, A * 128), block)]
        + [whole(a) for a in args[1:]]
        + [pl.BlockSpec(memory_space=pltpu.HBM)] * len(held),
        out_specs=[pl.BlockSpec((2, A * 8, 128), lambda i: (i + first, 0, 0))]
        + [pl.BlockSpec((16, 19 * 128), block)] * 4,
        scratch_shapes=[
            pltpu.VMEM((16, A * 128), F32),
            pltpu.VMEM((16, A * 128), F32),
            pltpu.VMEM((128, 128), F32),
            pltpu.VMEM((256, 128), F32),
        ],
        out_shape=[jax.ShapeDtypeStruct((n // 8, A * 8, 128), BF)]
        + [jax.ShapeDtypeStruct((n, 19 * 128), BF)] * 4,
        input_output_aliases={given + i: i for i in range(len(held))},
        compiler_params=pltpu.CompilerParams(vmem_limit_bytes=PREP_MIB * MIB),
        cost_estimate=pl.CostEstimate(
            flops=20_000_000, bytes_accessed=4_000_000, transcendentals=0
        ),
        name="prep",
    )(*args, *held)


def repeat(step):
    @pl.loop(0, M // 4)
    def _(i):
        for u in range(4):
            step(4 * i + u)

    step(M - 1)


def spectra_kernel(w_ref, f_ref, p_ref, s):
    for g in range(8):
        y = jnp.concatenate([w_ref[2 * g], w_ref[2 * g + 1]], axis=1)
        s[:, 256 * g : 256 * g + 256] = jnp.dot(f_ref[...], y, preferred_element_type=F32)

    def turn(m):
        for i in range(2):
            row = pl.multiple_of(m * 16 + 8 * i, 8)
            v = jnp.concatenate([s[pl.ds(row, 8), 128 * g : 128 * g + 128] for g in range(16)], axis=0)
            p_ref[m, :, 128 * i : 128 * i + 128] = v.T.astype(BF)

    repeat(turn)


def spectra(w, fwd_k):
    v = pl.BlockSpec(memory_space=pltpu.VMEM)
    return pl.pallas_call(
        spectra_kernel,
        in_specs=[v, v],
        out_specs=v,
        out_shape=jax.ShapeDtypeStruct((M, 128, 256), BF),
        scratch_shapes=[pltpu.VMEM((2 * M * 8, 2048), F32)],
        compiler_params=pltpu.CompilerParams(vmem_limit_bytes=16 * MIB),
        cost_estimate=pl.CostEstimate(flops=1000, bytes_accessed=1000, transcendentals=0),
        name="spectra",
    )(w, fwd_k)


def ref_kernel(b_ref, f_ref, r_ref, s):
    for y in range(4):
        for xh in range(2):
            for t in range(9):
                v = b_ref[y, xh, :, t * 128 : (t + 1) * 128].astype(F32)
                row = (y * 2 + xh) * 72 + 8 * t
                s[row : row + 8, 0:128] = v[0:8]
                s[row : row + 8, 128:256] = v[8:16]
    out = jnp.dot(f_ref[...], s[...].astype(BF), preferred_element_type=F32)
    for m in range(M):
        for i in range(2):
            r = 16 * m + 8 * i
            r_ref[m, :, 128 * i : 128 * i + 128] = jnp.concatenate(
                [out[r : r + 8, 0:128], out[r : r + 8, 128:256]], axis=0
            ).astype(BF)


def ref_spectra(blocks, fwd_k):
    v = pl.BlockSpec(memory_space=pltpu.VMEM)
    return pl.pallas_call(
        ref_kernel,
        in_specs=[v, v],
        out_specs=v,
        out_shape=jax.ShapeDtypeStruct((M, 16, 256), BF),
        scratch_shapes=[pltpu.VMEM((A * 8, 256), F32)],
        compiler_params=pltpu.CompilerParams(vmem_limit_bytes=8 * MIB),
        cost_estimate=pl.CostEstimate(flops=1000, bytes_accessed=1000, transcendentals=0),
        name="ref_spectra",
    )(blocks, fwd_k)


def score_kernel(*refs):
    p_ref, blocks, inv_ref, o_ref, xs = refs[0], refs[1:5], refs[5], refs[6], refs[7]
    xs[:, 2 * M * 8 :, :] = jnp.zeros((16, K_INV - 2 * M * 8, 256), BF)

    def cross(m):
        upper = p_ref[m]
        re, im = upper[:, 0:128], upper[:, 128:256]
        rhs = jnp.concatenate([upper, jnp.concatenate([im, -re], axis=1)], axis=0)
        lhs = jnp.concatenate([b[i, m] for b in blocks for i in range(4)], axis=0)
        x = jnp.dot(lhs, rhs, preferred_element_type=F32)
        row = pl.multiple_of(m * 16, 16)
        for g in range(16):
            for h in range(2):
                k = 16 * g + 8 * h
                xs[g, pl.ds(row, 16), 128 * h : 128 * h + 128] = jnp.concatenate(
                    [x[k : k + 8, 0:128], x[k : k + 8, 128:256]], axis=0
                ).astype(BF)

    repeat(cross)

    def four(i, best):
        for u in range(4):
            y = jnp.dot(inv_ref[...], xs[4 * i + u], preferred_element_type=F32)
            for t in range(A):
                best = jnp.maximum(best, y[8 * t : 8 * t + 8])
        return best

    best = lax.fori_loop(0, 4, four, jnp.full((8, 256), -jnp.inf, F32))
    best = jnp.max(best, axis=0, keepdims=True)
    o_ref[...] = jnp.maximum(best[:, 0:128], best[:, 128:256])


def scores_of(p, blocks, inv_k):
    v = pl.BlockSpec(memory_space=pltpu.VMEM)
    return pl.pallas_call(
        score_kernel,
        in_specs=[v] * 6,
        out_specs=v,
        out_shape=jax.ShapeDtypeStruct((1, 128), F32),
        scratch_shapes=[pltpu.VMEM((16, K_INV, 256), BF)],
        compiler_params=pltpu.CompilerParams(vmem_limit_bytes=20 * MIB),
        cost_estimate=pl.CostEstimate(flops=6_000_000_000, bytes_accessed=8_000_000, transcendentals=0),
        name="scores",
    )(p, *blocks, inv_k)


def sums_kernel(sc, c0, c1, c2, c3, tab_ref, mine, other, acc):
    width = 18 * 128
    lane = lax.broadcasted_iota(jnp.int32, (128, 256), 1).astype(F32)
    picks, groups = [], []
    for c in (c0, c1, c2, c3):
        meta = c[:, width : width + 128].astype(F32)
        picks.append(jnp.where(lane == meta[:, 0:1], 1.0, 0.0).astype(F32).T.astype(BF))
        groups.append(jnp.where(lane == meta[:, 1:2], 1.0, 0.0).astype(BF))
    pick = jnp.concatenate(picks, axis=1)
    group = jnp.concatenate(groups, axis=0)
    count = jnp.dot(pick, group, preferred_element_type=F32)
    flipped = tab_ref[...].T
    tab = jnp.concatenate([flipped, flipped], axis=1)
    wsum = jnp.dot(count, tab * tab, precision=lax.Precision.HIGHEST, preferred_element_type=F32)
    for t in range(9):
        cols = slice(256 * t, 256 * t + 256)
        x = jnp.concatenate([c[:, cols] for c in (c0, c1, c2, c3)], axis=0)
        acc[:, cols] = jnp.dot(pick, x, preferred_element_type=F32)
    left = lax.broadcasted_iota(jnp.int32, (256, 128), 1) < R
    for ref, core in ((mine, sc[2]), (other, 1 - sc[2])):
        for xh in range(2):
            start = pl.multiple_of((9 * xh + 4 * core) * 128, 128)
            ref[xh] = acc[:, pl.ds(start, 640)]
            mid = acc[:, (9 * xh + 4) * 128 : (9 * xh + 5) * 128]
            keep = jnp.logical_xor(left, core == 1)
            ref[xh, :, pl.ds(pl.multiple_of((1 - core) * 512, 128), 128)] = jnp.where(keep, mid, wsum)


def class_sums(sc, cs, tab):
    v = pl.BlockSpec(memory_space=pltpu.VMEM)
    shape = jax.ShapeDtypeStruct((2, 256, 640), F32)
    return pl.pallas_call(
        sums_kernel,
        in_specs=[pl.BlockSpec(memory_space=pltpu.SMEM)] + [v] * 5,
        out_specs=[v, v],
        out_shape=[shape, shape],
        scratch_shapes=[pltpu.VMEM((256, 18 * 128), F32)],
        compiler_params=pltpu.CompilerParams(vmem_limit_bytes=VMEM_LIMIT),
        cost_estimate=pl.CostEstimate(flops=700_000_000, bytes_accessed=5_000_000, transcendentals=0),
        name="class_sums",
    )(sc, *cs, tab)


def cut_x_kernel(sc, a_ref, b_ref, o0, o1, o2, o3):
    for dx, o in enumerate((o0, o1, o2, o3)):
        x = lax.rem(sc[1] + dx, 4)
        xh, xl = x // 2, lax.rem(x, 2)
        rows = pl.ds(pl.multiple_of(xl * 128, 128), 128)
        o[...] = (a_ref[xh, rows, :] + b_ref[xh, rows, :]).astype(o.dtype)


def cut_x(sc, a, b):
    v = pl.BlockSpec(memory_space=pltpu.VMEM)
    return pl.pallas_call(
        cut_x_kernel,
        in_specs=[pl.BlockSpec(memory_space=pltpu.SMEM), v, v],
        out_specs=[v] * 4,
        out_shape=[jax.ShapeDtypeStruct((128, 640), F32)] + [jax.ShapeDtypeStruct((128, 640), BF)] * 3,
        compiler_params=pltpu.CompilerParams(vmem_limit_bytes=VMEM_LIMIT),
        cost_estimate=pl.CostEstimate(flops=400_000, bytes_accessed=3_900_000, transcendentals=0),
        name="cut_x",
    )(sc, a, b)


def cut_z_kernel(sc, a0, a1, a2, a3, o0, o1, o2, o3):
    for dz, o in enumerate((o0, o1, o2, o3)):
        z = lax.rem(sc[3] + dz, 4)
        rows = pl.ds(pl.multiple_of(z * 32, 32), 32)
        far = a1[rows, :].astype(F32) + a2[rows, :].astype(F32) + a3[rows, :].astype(F32)
        o[...] = a0[rows, :] + far


def cut_z(sc, parts):
    v = pl.BlockSpec(memory_space=pltpu.VMEM)
    return pl.pallas_call(
        cut_z_kernel,
        in_specs=[pl.BlockSpec(memory_space=pltpu.SMEM)] + [v] * 4,
        out_specs=[v] * 4,
        out_shape=[jax.ShapeDtypeStruct((32, 640), F32)] * 4,
        compiler_params=pltpu.CompilerParams(vmem_limit_bytes=VMEM_LIMIT),
        cost_estimate=pl.CostEstimate(flops=400_000, bytes_accessed=1_700_000, transcendentals=0),
        name="cut_z",
    )(sc, *parts)


def final_kernel(sc, a0, a1, a2, a3, o_ref):
    s = (a0[...] + a1[...]) + (a2[...] + a3[...])
    odd = sc[2] == 1
    left = lax.broadcasted_iota(jnp.int32, (32, 128), 1) < R
    tile = [s[:, 128 * t : 128 * t + 128] for t in range(5)]
    held = jnp.where(odd, tile[0], tile[4])
    turned = pltpu.roll(held, R, 1)
    weight = jnp.where(jnp.logical_xor(left, odd), turned, held)
    tile = [t / (weight + TAU) for t in tile]
    rolled = [pltpu.roll(t, R, 1) for t in tile]
    later = [jnp.where(left, rolled[t], rolled[t + 1]) for t in range(4)] + [rolled[4]]
    for t in range(4):
        o_ref[:, 128 * t : 128 * t + 128] = jnp.where(odd, later[t], tile[t])[0:25]
    o_ref[:, 512:576] = jnp.where(odd, later[4], tile[4])[0:25, 0:R]


def final(sc, parts):
    v = pl.BlockSpec(memory_space=pltpu.VMEM)
    return pl.pallas_call(
        final_kernel,
        in_specs=[pl.BlockSpec(memory_space=pltpu.SMEM)] + [v] * 4,
        out_specs=v,
        out_shape=jax.ShapeDtypeStruct((25, 576), F32),
        compiler_params=pltpu.CompilerParams(vmem_limit_bytes=2 * MIB),
        name="final",
    )(sc, *parts)


def place(y, x, z, core):
    return ((y % 4) * 4 + (x % 4) // 2 * 2 + core % 2) * 8 + (x % 2) * 4 + z % 4


def permutation(move):
    return [
        (place(y, x, z, c), place(*move(y, x, z, c)))
        for y in range(4)
        for x in range(4)
        for z in range(4)
        for c in range(2)
    ]


CORE = permutation(lambda y, x, z, c: (y, x, z, c + 1))
HIGH = permutation(lambda y, x, z, c: (y, x + 2, z, c))
LOW = permutation(lambda y, x, z, c: (y, x ^ 1, z, c))
Y_NEAR = permutation(lambda y, x, z, c: (y ^ 1, x, z, c))
Y_FAR = permutation(lambda y, x, z, c: (y + 2, x, z, c))
YS = [permutation(lambda y, x, z, c, d=d: (y + d, x, z, c)) for d in range(4)]
XS = [permutation(lambda y, x, z, c, d=d: (y, x + d, z, c)) for d in range(4)]
ZS = [permutation(lambda y, x, z, c, d=d: (y, x, z + d, c)) for d in range(4)]


def move(value, pairs):
    return lax.ppermute(value, AXES, pairs)


def after(values, *others):
    return lax.optimization_barrier((*values, *others))[: len(values)]


def join(own, other, upper):
    lower = upper == 0
    return jnp.stack([jnp.where(lower, own, other), jnp.where(lower, other, own)])


def per_device(particles, references, owner, class_offset, rotation, shifts, ctf_group, ctf_table):
    fwd_np, inv_np = tables()
    fwd_k, inv_k = jnp.asarray(fwd_np), jnp.asarray(inv_np)
    fx, fy = (jnp.asarray(t) for t in freq_tables())
    dom, cls = lax.axis_index("dom"), lax.axis_index("cls")
    y, xh, core = dom // 4, dom // 2 % 2, dom % 2
    xl, z = cls // 4, cls % 4
    sc = jnp.stack([y, xh * 2 + xl, core, z]).astype(jnp.int32)

    low, high = references[0:16], references[9:25]
    first = core == 0
    keep = jnp.where(first, low, high)
    give = jnp.where(first, high, low)
    got = move(give, CORE)
    block = jnp.where(
        first, jnp.concatenate([keep, got], axis=1), jnp.concatenate([got, keep], axis=1)
    )
    rows = [shifts.T, rotation[None], owner.T, class_offset[None], ctf_group[None]]
    table = ctf_table.T
    block, rows[1] = lax.optimization_barrier((block, rows[1]))
    half = prep(particles, rows, table, fx, fy, 0)
    far = move(block, HIGH)
    far, *half = lax.optimization_barrier((far, *half))
    pair = join(block, far, xh)
    pair, rows[1] = lax.optimization_barrier((pair, rows[1]))
    weighted, *sent = prep(particles, rows, table, fx, fy, 4, half)
    near = move(pair, Y_NEAR)
    near, weighted, *sent = lax.optimization_barrier((near, weighted, *sent))
    quad = join(pair, near, y % 2)
    octet = join(quad, move(quad, Y_FAR), y // 2).reshape(4, 2, 16, 1152)

    held = [sent[0]] + [move(sent[d], YS[d]) for d in (1, 2, 3)]
    part = spectra(weighted, fwd_k)

    own = ref_spectra(octet, fwd_k)
    up, down = move(own, ZS[1]), move(own, ZS[3])
    side = move(own, LOW)
    side_up, side_down = move(side, ZS[1]), move(side, ZS[3])
    on_up, on_down = move(up, ZS[1]), move(side_down, ZS[3])
    early = jnp.stack([own, side, up, down])
    early_twin = move(early, CORE)
    held = after(held, side, up, down, side_up, side_down, part)
    held = after(held, on_up, on_down)
    mine, other = class_sums(sc, held, table)
    cut = cut_x(sc, mine, move(other, CORE))
    late = jnp.stack([side_up, side_down, on_up, on_down])
    late_twin = move(late, CORE)
    cut = [cut[0]] + [move(cut[d], XS[d]) for d in (1, 2, 3)]
    scores = scores_of(part, [early, early_twin, late, late_twin], inv_k)
    *cut, scores = lax.optimization_barrier((*cut, scores))
    cut = cut_z(sc, cut)
    cut = [cut[0]] + [move(cut[d], ZS[d]) for d in (1, 2, 3)]
    return scores[0], final(sc, cut)


def solution(mesh):
    return jax.shard_map(
        per_device,
        mesh=mesh,
        in_specs=(
            P(("dom", "cls"), None),
            P("cls", "dom"),
            P(("dom", "cls"), None),
            P(("dom", "cls")),
            P(("dom", "cls")),
            P(("dom", "cls"), None),
            P(("dom", "cls")),
            P(),
        ),
        out_specs=(P(("dom", "cls")), P("cls", "dom")),
        check_vma=False,
    )
```

```python
import functools

import jax
import jax.numpy as jnp
import numpy as np
from jax import lax
from jax.experimental import pallas as pl
from jax.experimental.pallas import tpu as pltpu
from jax.sharding import PartitionSpec as P

A = 72
M = 37
R = 64
BOX = 128
TAU = 1.0
AXES = ("dom", "cls")
BF = jnp.bfloat16
F32 = jnp.float32
MIB = 1024 * 1024
VMEM_LIMIT = 8 * MIB
PREP_MIB = 56
K_INV = 640


def tables():
    m = np.arange(M)[:, None]
    a = np.arange(A)[None, :]
    turn = 2.0 * np.pi * ((m * a) % A) / A
    fwd = np.stack([np.cos(turn), -np.sin(turn)], axis=1).reshape(2 * M, A)
    gain = np.where((np.arange(M) == 0) | (np.arange(M) == A // 2), 1.0, 2.0)[:, None]
    inv = np.stack([np.cos(turn) / A, -np.sin(turn) / A], axis=1).astype(BF).astype(np.float32)
    inv = (inv * gain[:, None, :]).reshape(2 * M, A).T
    eye = np.eye(8, dtype=np.float32)
    fwd_k = np.kron(fwd.astype(np.float32), eye).astype(BF)
    inv_k = np.zeros((A * 8, K_INV), np.float32)
    inv_k[:, : 2 * M * 8] = np.kron(inv, eye)
    return fwd_k, inv_k.astype(BF)


def freq_tables():
    angle = 2.0 * np.pi * np.arange(A // 2) / A
    radius = np.tile(np.arange(1, R + 1), 2)
    fx = np.cos(angle)[:, None] * radius[None, :] / BOX
    fy = np.sin(angle)[:, None] * radius[None, :] / BOX
    return fx.astype(np.float32), fy.astype(np.float32)


def cos_poly():
    n = 7
    nodes = (np.cos((np.arange(64) + 0.5) * np.pi / 64) + 1.0) / 8.0
    return [float(c) for c in np.polynomial.chebyshev.Chebyshev.fit(
        nodes, np.cos(2.0 * np.pi * np.sqrt(nodes)), n - 1, domain=[0.0, 0.25]
    ).convert(kind=np.polynomial.Polynomial).coef]


COEF = cos_poly()


def prep_kernel(first, x_ref, shift_ref, rot_ref, own_ref, off_ref, grp_ref, tab_ref, fx_ref, fy_ref, *refs):
    w_ref, c0, c1, c2, c3, ws, us, aux, tab = refs[-9:]
    dom, cls = lax.axis_index("dom"), lax.axis_index("cls")
    mine = 2 * (dom * 8 + cls)
    step = pl.program_id(0)

    @pl.when(step == 0)
    def _():
        shift_rows = shift_ref[...].astype(F32)
        group = grp_ref[...]
        rows = [
            shift_rows,
            rot_ref[...].astype(F32),
            (group - mine).astype(F32),
            (own_ref[...] * 32 + off_ref[...]).astype(F32),
            group.astype(F32),
            jnp.zeros((122, 128), F32),
        ]
        aux[...] = jnp.concatenate(rows, axis=0).T
        flipped = tab_ref[...].T
        tab[...] = jnp.concatenate([flipped, flipped], axis=1)

    here = aux[pl.ds(pl.multiple_of((step + first) * 16, 16), 16), :]
    lane = lax.broadcasted_iota(jnp.int32, (16, 128), 1)
    left = lane < R
    shift = jnp.where(left, 0.0, -0.25).astype(F32)
    sxb = jnp.broadcast_to(here[:, 0:1], (16, 128))
    syb = jnp.broadcast_to(here[:, 1:2], (16, 128))
    ctf = jnp.where(here[:, 3:4] > 0.5, tab[pl.ds(mine + 1, 1), :], tab[pl.ds(mine, 1), :])
    ctf_s = jnp.where(left, -ctf, ctf)
    for b in range(A // 4):
        done = []
        for a in (2 * b, 2 * b + 1):
            v = (sxb * fx_ref[a : a + 1, :] + syb * fy_ref[a : a + 1, :]) + shift
            v = v - jnp.round(v)
            q = v * v
            e = jnp.full_like(q, COEF[-1])
            for k in COEF[-2::-1]:
                e = e * q + k
            er = pltpu.roll(e, R, 1)
            cc = jnp.where(left, e, er) * ctf
            ss = jnp.where(left, er, e) * ctf_s
            x0 = x_ref[:, a * 128 : (a + 1) * 128].astype(F32)
            h = a + A // 2
            x1 = x_ref[:, h * 128 : (h + 1) * 128].astype(F32)
            w0 = x0 * cc + pltpu.roll(x0, R, 1) * ss
            w1 = x1 * cc - pltpu.roll(x1, R, 1) * ss
            ws[:, a * 128 : (a + 1) * 128] = w0
            ws[:, h * 128 : (h + 1) * 128] = w1
            done.append((w0, w1))
        for half in (0, 1):
            row = (2 * b + half * (A // 2)) * 8
            for g in (0, 1):
                w_ref[g, row : row + 16, :] = jnp.concatenate(
                    [done[0][half][8 * g : 8 * g + 8], done[1][half][8 * g : 8 * g + 8]], axis=0
                ).astype(BF)
    rotb = jnp.broadcast_to(here[:, 2:3], (16, 128)).astype(jnp.int32)
    bit = [(rotb & (1 << k)) != 0 for k in range(7)]
    for r in range(8):
        t = [ws[:, (r + 8 * n) * 128 : (r + 8 * n + 1) * 128] for n in range(9)]
        for k in range(4):
            t = [jnp.where(bit[3 + k], t[(n + (1 << k)) % 9], t[n]) for n in range(9)]
        for n in range(9):
            us[:, (r + 8 * n) * 128 : (r + 8 * n + 1) * 128] = t[n]
    for j0 in range(0, A, 8):
        t = [us[:, ((j0 + i) % A) * 128 : ((j0 + i) % A + 1) * 128] for i in range(15)]
        t = [jnp.where(bit[0], t[i + 1], t[i]) for i in range(14)]
        t = [jnp.where(bit[1], t[i + 2], t[i]) for i in range(12)]
        for i in range(8):
            ws[:, (j0 + i) * 128 : (j0 + i + 1) * 128] = jnp.where(bit[2], t[i + 4], t[i])
    meta = jnp.where(lane == 0, here[:, 4:5], jnp.where(lane == 1, here[:, 5:6], 0.0)).astype(BF)
    width = 18 * 128
    for dy, c_ref in enumerate((c0, c1, c2, c3)):
        dest = lax.rem(dom // 4 + dy, 4)
        start = pl.multiple_of(dest * width, 128)
        c_ref[:, 0:width] = ws[:, pl.ds(start, width)].astype(BF)
        c_ref[:, width : width + 128] = meta


def prep(particles, rows, table, fx, fy, first, held=()):
    n = particles.shape[0]
    whole = lambda a: pl.BlockSpec(a.shape, lambda i: (0,) * a.ndim)
    block = lambda i: (i + first, 0)
    args = [particles, *rows, table, fx, fy]
    given = len(args)
    return pl.pallas_call(
        functools.partial(prep_kernel, first),
        grid=(n // 32,),
        in_specs=[pl.BlockSpec((16, A * 128), block)]
        + [whole(a) for a in args[1:]]
        + [pl.BlockSpec(memory_space=pltpu.HBM)] * len(held),
        out_specs=[pl.BlockSpec((2, A * 8, 128), lambda i: (i + first, 0, 0))]
        + [pl.BlockSpec((16, 19 * 128), block)] * 4,
        scratch_shapes=[
            pltpu.VMEM((16, A * 128), F32),
            pltpu.VMEM((16, A * 128), F32),
            pltpu.VMEM((128, 128), F32),
            pltpu.VMEM((256, 128), F32),
        ],
        out_shape=[jax.ShapeDtypeStruct((n // 8, A * 8, 128), BF)]
        + [jax.ShapeDtypeStruct((n, 19 * 128), BF)] * 4,
        input_output_aliases={given + i: i for i in range(len(held))},
        compiler_params=pltpu.CompilerParams(vmem_limit_bytes=PREP_MIB * MIB),
        cost_estimate=pl.CostEstimate(
            flops=20_000_000, bytes_accessed=4_000_000, transcendentals=0
        ),
        name="prep",
    )(*args, *held)


def repeat(step):
    @pl.loop(0, M // 4)
    def _(i):
        for u in range(4):
            step(4 * i + u)

    step(M - 1)


def spectra_kernel(w_ref, f_ref, p_ref, s):
    for g in range(8):
        y = jnp.concatenate([w_ref[2 * g], w_ref[2 * g + 1]], axis=1)
        s[:, 256 * g : 256 * g + 256] = jnp.dot(f_ref[...], y, preferred_element_type=F32)

    def turn(m):
        for i in range(2):
            row = pl.multiple_of(m * 16 + 8 * i, 8)
            v = jnp.concatenate([s[pl.ds(row, 8), 128 * g : 128 * g + 128] for g in range(16)], axis=0)
            p_ref[m, :, 128 * i : 128 * i + 128] = v.T.astype(BF)

    repeat(turn)


def spectra(w, fwd_k):
    v = pl.BlockSpec(memory_space=pltpu.VMEM)
    return pl.pallas_call(
        spectra_kernel,
        in_specs=[v, v],
        out_specs=v,
        out_shape=jax.ShapeDtypeStruct((M, 128, 256), BF),
        scratch_shapes=[pltpu.VMEM((2 * M * 8, 2048), F32)],
        compiler_params=pltpu.CompilerParams(vmem_limit_bytes=16 * MIB),
        cost_estimate=pl.CostEstimate(flops=1000, bytes_accessed=1000, transcendentals=0),
        name="spectra",
    )(w, fwd_k)


def ref_kernel(b_ref, f_ref, r_ref, s):
    for y in range(4):
        for xh in range(2):
            for t in range(9):
                v = b_ref[y, xh, :, t * 128 : (t + 1) * 128].astype(F32)
                row = (y * 2 + xh) * 72 + 8 * t
                s[row : row + 8, 0:128] = v[0:8]
                s[row : row + 8, 128:256] = v[8:16]
    out = jnp.dot(f_ref[...], s[...].astype(BF), preferred_element_type=F32)
    for m in range(M):
        for i in range(2):
            r = 16 * m + 8 * i
            r_ref[m, :, 128 * i : 128 * i + 128] = jnp.concatenate(
                [out[r : r + 8, 0:128], out[r : r + 8, 128:256]], axis=0
            ).astype(BF)


def ref_spectra(blocks, fwd_k):
    v = pl.BlockSpec(memory_space=pltpu.VMEM)
    return pl.pallas_call(
        ref_kernel,
        in_specs=[v, v],
        out_specs=v,
        out_shape=jax.ShapeDtypeStruct((M, 16, 256), BF),
        scratch_shapes=[pltpu.VMEM((A * 8, 256), F32)],
        compiler_params=pltpu.CompilerParams(vmem_limit_bytes=8 * MIB),
        cost_estimate=pl.CostEstimate(flops=1000, bytes_accessed=1000, transcendentals=0),
        name="ref_spectra",
    )(blocks, fwd_k)


def score_kernel(*refs):
    p_ref, blocks, inv_ref, o_ref, xs = refs[0], refs[1:5], refs[5], refs[6], refs[7]
    xs[:, 2 * M * 8 :, :] = jnp.zeros((16, K_INV - 2 * M * 8, 256), BF)

    def cross(m):
        upper = p_ref[m]
        re, im = upper[:, 0:128], upper[:, 128:256]
        rhs = jnp.concatenate([upper, jnp.concatenate([im, -re], axis=1)], axis=0)
        lhs = jnp.concatenate([b[i, m] for b in blocks for i in range(4)], axis=0)
        x = jnp.dot(lhs, rhs, preferred_element_type=F32)
        row = pl.multiple_of(m * 16, 16)
        for g in range(16):
            for h in range(2):
                k = 16 * g + 8 * h
                xs[g, pl.ds(row, 16), 128 * h : 128 * h + 128] = jnp.concatenate(
                    [x[k : k + 8, 0:128], x[k : k + 8, 128:256]], axis=0
                ).astype(BF)

    repeat(cross)

    def four(i, best):
        for u in range(4):
            y = jnp.dot(inv_ref[...], xs[4 * i + u], preferred_element_type=F32)
            for t in range(A):
                best = jnp.maximum(best, y[8 * t : 8 * t + 8])
        return best

    best = lax.fori_loop(0, 4, four, jnp.full((8, 256), -jnp.inf, F32))
    best = jnp.max(best, axis=0, keepdims=True)
    o_ref[...] = jnp.maximum(best[:, 0:128], best[:, 128:256])


def scores_of(p, blocks, inv_k):
    v = pl.BlockSpec(memory_space=pltpu.VMEM)
    return pl.pallas_call(
        score_kernel,
        in_specs=[v] * 6,
        out_specs=v,
        out_shape=jax.ShapeDtypeStruct((1, 128), F32),
        scratch_shapes=[pltpu.VMEM((16, K_INV, 256), BF)],
        compiler_params=pltpu.CompilerParams(vmem_limit_bytes=20 * MIB),
        cost_estimate=pl.CostEstimate(flops=6_000_000_000, bytes_accessed=8_000_000, transcendentals=0),
        name="scores",
    )(p, *blocks, inv_k)


def sums_kernel(sc, c0, c1, c2, c3, tab_ref, mine, other, acc):
    width = 18 * 128
    lane = lax.broadcasted_iota(jnp.int32, (128, 256), 1).astype(F32)
    picks, groups = [], []
    for c in (c0, c1, c2, c3):
        meta = c[:, width : width + 128].astype(F32)
        picks.append(jnp.where(lane == meta[:, 0:1], 1.0, 0.0).astype(F32).T.astype(BF))
        groups.append(jnp.where(lane == meta[:, 1:2], 1.0, 0.0).astype(BF))
    pick = jnp.concatenate(picks, axis=1)
    group = jnp.concatenate(groups, axis=0)
    count = jnp.dot(pick, group, preferred_element_type=F32)
    flipped = tab_ref[...].T
    tab = jnp.concatenate([flipped, flipped], axis=1)
    wsum = jnp.dot(count, tab * tab, precision=lax.Precision.HIGHEST, preferred_element_type=F32)
    for t in range(9):
        cols = slice(256 * t, 256 * t + 256)
        x = jnp.concatenate([c[:, cols] for c in (c0, c1, c2, c3)], axis=0)
        acc[:, cols] = jnp.dot(pick, x, preferred_element_type=F32)
    left = lax.broadcasted_iota(jnp.int32, (256, 128), 1) < R
    for ref, core in ((mine, sc[2]), (other, 1 - sc[2])):
        for xh in range(2):
            start = pl.multiple_of((9 * xh + 4 * core) * 128, 128)
            ref[xh] = acc[:, pl.ds(start, 640)]
            mid = acc[:, (9 * xh + 4) * 128 : (9 * xh + 5) * 128]
            keep = jnp.logical_xor(left, core == 1)
            ref[xh, :, pl.ds(pl.multiple_of((1 - core) * 512, 128), 128)] = jnp.where(keep, mid, wsum)


def class_sums(sc, cs, tab):
    v = pl.BlockSpec(memory_space=pltpu.VMEM)
    shape = jax.ShapeDtypeStruct((2, 256, 640), F32)
    return pl.pallas_call(
        sums_kernel,
        in_specs=[pl.BlockSpec(memory_space=pltpu.SMEM)] + [v] * 5,
        out_specs=[v, v],
        out_shape=[shape, shape],
        scratch_shapes=[pltpu.VMEM((256, 18 * 128), F32)],
        compiler_params=pltpu.CompilerParams(vmem_limit_bytes=VMEM_LIMIT),
        cost_estimate=pl.CostEstimate(flops=700_000_000, bytes_accessed=5_000_000, transcendentals=0),
        name="class_sums",
    )(sc, *cs, tab)


def cut_x_kernel(sc, a_ref, b_ref, o0, o1, o2, o3):
    for dx, o in enumerate((o0, o1, o2, o3)):
        x = lax.rem(sc[1] + dx, 4)
        xh, xl = x // 2, lax.rem(x, 2)
        rows = pl.ds(pl.multiple_of(xl * 128, 128), 128)
        o[...] = (a_ref[xh, rows, :] + b_ref[xh, rows, :]).astype(o.dtype)


def cut_x(sc, a, b):
    v = pl.BlockSpec(memory_space=pltpu.VMEM)
    return pl.pallas_call(
        cut_x_kernel,
        in_specs=[pl.BlockSpec(memory_space=pltpu.SMEM), v, v],
        out_specs=[v] * 4,
        out_shape=[jax.ShapeDtypeStruct((128, 640), F32)] + [jax.ShapeDtypeStruct((128, 640), BF)] * 3,
        compiler_params=pltpu.CompilerParams(vmem_limit_bytes=VMEM_LIMIT),
        cost_estimate=pl.CostEstimate(flops=400_000, bytes_accessed=3_900_000, transcendentals=0),
        name="cut_x",
    )(sc, a, b)


def cut_z_kernel(sc, a0, a1, a2, a3, o0, o1, o2, o3):
    for dz, o in enumerate((o0, o1, o2, o3)):
        z = lax.rem(sc[3] + dz, 4)
        rows = pl.ds(pl.multiple_of(z * 32, 32), 32)
        far = a1[rows, :].astype(F32) + a2[rows, :].astype(F32) + a3[rows, :].astype(F32)
        o[...] = a0[rows, :] + far


def cut_z(sc, parts):
    v = pl.BlockSpec(memory_space=pltpu.VMEM)
    return pl.pallas_call(
        cut_z_kernel,
        in_specs=[pl.BlockSpec(memory_space=pltpu.SMEM)] + [v] * 4,
        out_specs=[v] * 4,
        out_shape=[jax.ShapeDtypeStruct((32, 640), F32)] * 4,
        compiler_params=pltpu.CompilerParams(vmem_limit_bytes=VMEM_LIMIT),
        cost_estimate=pl.CostEstimate(flops=400_000, bytes_accessed=1_700_000, transcendentals=0),
        name="cut_z",
    )(sc, *parts)


def final_kernel(sc, a0, a1, a2, a3, o_ref):
    s = (a0[...] + a1[...]) + (a2[...] + a3[...])
    odd = sc[2] == 1
    left = lax.broadcasted_iota(jnp.int32, (32, 128), 1) < R
    tile = [s[:, 128 * t : 128 * t + 128] for t in range(5)]
    held = jnp.where(odd, tile[0], tile[4])
    turned = pltpu.roll(held, R, 1)
    weight = jnp.where(jnp.logical_xor(left, odd), turned, held)
    tile = [t / (weight + TAU) for t in tile]
    rolled = [pltpu.roll(t, R, 1) for t in tile]
    later = [jnp.where(left, rolled[t], rolled[t + 1]) for t in range(4)] + [rolled[4]]
    for t in range(4):
        o_ref[:, 128 * t : 128 * t + 128] = jnp.where(odd, later[t], tile[t])[0:25]
    o_ref[:, 512:576] = jnp.where(odd, later[4], tile[4])[0:25, 0:R]


def final(sc, parts):
    v = pl.BlockSpec(memory_space=pltpu.VMEM)
    return pl.pallas_call(
        final_kernel,
        in_specs=[pl.BlockSpec(memory_space=pltpu.SMEM)] + [v] * 4,
        out_specs=v,
        out_shape=jax.ShapeDtypeStruct((25, 576), F32),
        compiler_params=pltpu.CompilerParams(vmem_limit_bytes=2 * MIB),
        name="final",
    )(sc, *parts)


def place(y, x, z, core):
    return ((y % 4) * 4 + (x % 4) // 2 * 2 + core % 2) * 8 + (x % 2) * 4 + z % 4


def permutation(move):
    return [
        (place(y, x, z, c), place(*move(y, x, z, c)))
        for y in range(4)
        for x in range(4)
        for z in range(4)
        for c in range(2)
    ]


CORE = permutation(lambda y, x, z, c: (y, x, z, c + 1))
HIGH = permutation(lambda y, x, z, c: (y, x + 2, z, c))
LOW = permutation(lambda y, x, z, c: (y, x ^ 1, z, c))
Y_NEAR = permutation(lambda y, x, z, c: (y ^ 1, x, z, c))
Y_FAR = permutation(lambda y, x, z, c: (y + 2, x, z, c))
YS = [permutation(lambda y, x, z, c, d=d: (y + d, x, z, c)) for d in range(4)]
XS = [permutation(lambda y, x, z, c, d=d: (y, x + d, z, c)) for d in range(4)]
ZS = [permutation(lambda y, x, z, c, d=d: (y, x, z + d, c)) for d in range(4)]


def move(value, pairs):
    return lax.ppermute(value, AXES, pairs)


def after(values, *others):
    return lax.optimization_barrier((*values, *others))[: len(values)]


def join(own, other, upper):
    lower = upper == 0
    return jnp.stack([jnp.where(lower, own, other), jnp.where(lower, other, own)])


def per_device(particles, references, owner, class_offset, rotation, shifts, ctf_group, ctf_table):
    fwd_np, inv_np = tables()
    fwd_k, inv_k = jnp.asarray(fwd_np), jnp.asarray(inv_np)
    fx, fy = (jnp.asarray(t) for t in freq_tables())
    dom, cls = lax.axis_index("dom"), lax.axis_index("cls")
    y, xh, core = dom // 4, dom // 2 % 2, dom % 2
    xl, z = cls // 4, cls % 4
    sc = jnp.stack([y, xh * 2 + xl, core, z]).astype(jnp.int32)

    low, high = references[0:16], references[9:25]
    first = core == 0
    keep = jnp.where(first, low, high)
    give = jnp.where(first, high, low)
    got = move(give, CORE)
    block = jnp.where(
        first, jnp.concatenate([keep, got], axis=1), jnp.concatenate([got, keep], axis=1)
    )
    rows = [shifts.T, rotation[None], owner.T, class_offset[None], ctf_group[None]]
    table = ctf_table.T
    block, rows[1] = lax.optimization_barrier((block, rows[1]))
    half = prep(particles, rows, table, fx, fy, 0)
    far = move(block, HIGH)
    far, *half = lax.optimization_barrier((far, *half))
    pair = join(block, far, xh)
    pair, rows[1] = lax.optimization_barrier((pair, rows[1]))
    weighted, *sent = prep(particles, rows, table, fx, fy, 4, half)
    near = move(pair, Y_NEAR)
    near, weighted, *sent = lax.optimization_barrier((near, weighted, *sent))
    quad = join(pair, near, y % 2)
    octet = join(quad, move(quad, Y_FAR), y // 2).reshape(4, 2, 16, 1152)

    across = move(sent[2], YS[2])
    part = spectra(weighted, fwd_k)
    one, three = after([sent[1], sent[3]], across, part)
    held = [sent[0], move(one, YS[1]), across, move(three, YS[3])]
    own = ref_spectra(octet, fwd_k)
    up, down = move(own, ZS[1]), move(own, ZS[3])
    side = move(own, LOW)
    side_up, side_down = move(side, ZS[1]), move(side, ZS[3])
    on_up, on_down = move(up, ZS[1]), move(side_down, ZS[3])
    early = jnp.stack([own, side, up, down])
    early_twin = move(early, CORE)
    held = after(held, side, up, down, side_up, side_down)
    mine, other = class_sums(sc, held, table)
    cut = cut_x(sc, mine, move(other, CORE))
    late = jnp.stack([side_up, side_down, on_up, on_down])
    late_twin = move(late, CORE)
    cut = [cut[0]] + [move(cut[d], XS[d]) for d in (1, 2, 3)]
    scores = scores_of(part, [early, early_twin, late, late_twin], inv_k)
    *cut, scores = lax.optimization_barrier((*cut, scores))
    cut = cut_z(sc, cut)
    cut = [cut[0]] + [move(cut[d], ZS[d]) for d in (1, 2, 3)]
    return scores[0], final(sc, cut)


def solution(mesh):
    return jax.shard_map(
        per_device,
        mesh=mesh,
        in_specs=(
            P(("dom", "cls"), None),
            P("cls", "dom"),
            P(("dom", "cls"), None),
            P(("dom", "cls")),
            P(("dom", "cls")),
            P(("dom", "cls"), None),
            P(("dom", "cls")),
            P(),
        ),
        out_specs=(P(("dom", "cls")), P("cls", "dom")),
        check_vma=False,
    )
```

```python
import functools

import jax
import jax.numpy as jnp
import numpy as np
from jax import lax
from jax.experimental import pallas as pl
from jax.experimental.pallas import tpu as pltpu
from jax.sharding import PartitionSpec as P

A = 72
M = 37
R = 64
BOX = 128
TAU = 1.0
AXES = ("dom", "cls")
BF = jnp.bfloat16
F32 = jnp.float32
MIB = 1024 * 1024
VMEM_LIMIT = 8 * MIB
PREP_MIB = 56
K_INV = 640


def tables():
    m = np.arange(M)[:, None]
    a = np.arange(A)[None, :]
    turn = 2.0 * np.pi * ((m * a) % A) / A
    fwd = np.stack([np.cos(turn), -np.sin(turn)], axis=1).reshape(2 * M, A)
    gain = np.where((np.arange(M) == 0) | (np.arange(M) == A // 2), 1.0, 2.0)[:, None]
    inv = np.stack([np.cos(turn) / A, -np.sin(turn) / A], axis=1).astype(BF).astype(np.float32)
    inv = (inv * gain[:, None, :]).reshape(2 * M, A).T
    eye = np.eye(8, dtype=np.float32)
    fwd_k = np.kron(fwd.astype(np.float32), eye).astype(BF)
    inv_k = np.zeros((A * 8, K_INV), np.float32)
    inv_k[:, : 2 * M * 8] = np.kron(inv, eye)
    return fwd_k, inv_k.astype(BF)


def freq_tables():
    angle = 2.0 * np.pi * np.arange(A // 2) / A
    radius = np.tile(np.arange(1, R + 1), 2)
    fx = np.cos(angle)[:, None] * radius[None, :] / BOX
    fy = np.sin(angle)[:, None] * radius[None, :] / BOX
    return fx.astype(np.float32), fy.astype(np.float32)


def cos_poly():
    n = 7
    nodes = (np.cos((np.arange(64) + 0.5) * np.pi / 64) + 1.0) / 8.0
    return [float(c) for c in np.polynomial.chebyshev.Chebyshev.fit(
        nodes, np.cos(2.0 * np.pi * np.sqrt(nodes)), n - 1, domain=[0.0, 0.25]
    ).convert(kind=np.polynomial.Polynomial).coef]


COEF = cos_poly()


def prep_kernel(first, x_ref, shift_ref, rot_ref, own_ref, off_ref, grp_ref, tab_ref, fx_ref, fy_ref, *refs):
    w_ref, c0, c1, c2, c3, ws, us, aux, tab = refs[-9:]
    dom, cls = lax.axis_index("dom"), lax.axis_index("cls")
    mine = 2 * (dom * 8 + cls)
    step = pl.program_id(0)

    @pl.when(step == 0)
    def _():
        shift_rows = shift_ref[...].astype(F32)
        group = grp_ref[...]
        rows = [
            shift_rows,
            rot_ref[...].astype(F32),
            (group - mine).astype(F32),
            (own_ref[...] * 32 + off_ref[...]).astype(F32),
            group.astype(F32),
            jnp.zeros((122, 128), F32),
        ]
        aux[...] = jnp.concatenate(rows, axis=0).T
        flipped = tab_ref[...].T
        tab[...] = jnp.concatenate([flipped, flipped], axis=1)

    here = aux[pl.ds(pl.multiple_of((step + first) * 16, 16), 16), :]
    lane = lax.broadcasted_iota(jnp.int32, (16, 128), 1)
    left = lane < R
    shift = jnp.where(left, 0.0, -0.25).astype(F32)
    sxb = jnp.broadcast_to(here[:, 0:1], (16, 128))
    syb = jnp.broadcast_to(here[:, 1:2], (16, 128))
    ctf = jnp.where(here[:, 3:4] > 0.5, tab[pl.ds(mine + 1, 1), :], tab[pl.ds(mine, 1), :])
    ctf_s = jnp.where(left, -ctf, ctf)
    for b in range(A // 4):
        done = []
        for a in (2 * b, 2 * b + 1):
            v = (sxb * fx_ref[a : a + 1, :] + syb * fy_ref[a : a + 1, :]) + shift
            v = v - jnp.round(v)
            q = v * v
            e = jnp.full_like(q, COEF[-1])
            for k in COEF[-2::-1]:
                e = e * q + k
            er = pltpu.roll(e, R, 1)
            cc = jnp.where(left, e, er) * ctf
            ss = jnp.where(left, er, e) * ctf_s
            x0 = x_ref[:, a * 128 : (a + 1) * 128].astype(F32)
            h = a + A // 2
            x1 = x_ref[:, h * 128 : (h + 1) * 128].astype(F32)
            w0 = x0 * cc + pltpu.roll(x0, R, 1) * ss
            w1 = x1 * cc - pltpu.roll(x1, R, 1) * ss
            ws[:, a * 128 : (a + 1) * 128] = w0
            ws[:, h * 128 : (h + 1) * 128] = w1
            done.append((w0, w1))
        for half in (0, 1):
            row = (2 * b + half * (A // 2)) * 8
            for g in (0, 1):
                w_ref[g, row : row + 16, :] = jnp.concatenate(
                    [done[0][half][8 * g : 8 * g + 8], done[1][half][8 * g : 8 * g + 8]], axis=0
                ).astype(BF)
    rotb = jnp.broadcast_to(here[:, 2:3], (16, 128)).astype(jnp.int32)
    bit = [(rotb & (1 << k)) != 0 for k in range(7)]
    for r in range(8):
        t = [ws[:, (r + 8 * n) * 128 : (r + 8 * n + 1) * 128] for n in range(9)]
        for k in range(4):
            t = [jnp.where(bit[3 + k], t[(n + (1 << k)) % 9], t[n]) for n in range(9)]
        for n in range(9):
            us[:, (r + 8 * n) * 128 : (r + 8 * n + 1) * 128] = t[n]
    for j0 in range(0, A, 8):
        t = [us[:, ((j0 + i) % A) * 128 : ((j0 + i) % A + 1) * 128] for i in range(15)]
        t = [jnp.where(bit[0], t[i + 1], t[i]) for i in range(14)]
        t = [jnp.where(bit[1], t[i + 2], t[i]) for i in range(12)]
        for i in range(8):
            ws[:, (j0 + i) * 128 : (j0 + i + 1) * 128] = jnp.where(bit[2], t[i + 4], t[i])
    meta = jnp.where(lane == 0, here[:, 4:5], jnp.where(lane == 1, here[:, 5:6], 0.0)).astype(BF)
    width = 18 * 128
    for dy, c_ref in enumerate((c0, c1, c2, c3)):
        dest = lax.rem(dom // 4 + dy, 4)
        start = pl.multiple_of(dest * width, 128)
        c_ref[:, 0:width] = ws[:, pl.ds(start, width)].astype(BF)
        c_ref[:, width : width + 128] = meta


def prep(particles, rows, table, fx, fy, first, held=()):
    n = particles.shape[0]
    whole = lambda a: pl.BlockSpec(a.shape, lambda i: (0,) * a.ndim)
    block = lambda i: (i + first, 0)
    args = [particles, *rows, table, fx, fy]
    given = len(args)
    return pl.pallas_call(
        functools.partial(prep_kernel, first),
        grid=(n // 32,),
        in_specs=[pl.BlockSpec((16, A * 128), block)]
        + [whole(a) for a in args[1:]]
        + [pl.BlockSpec(memory_space=pltpu.HBM)] * len(held),
        out_specs=[pl.BlockSpec((2, A * 8, 128), lambda i: (i + first, 0, 0))]
        + [pl.BlockSpec((16, 19 * 128), block)] * 4,
        scratch_shapes=[
            pltpu.VMEM((16, A * 128), F32),
            pltpu.VMEM((16, A * 128), F32),
            pltpu.VMEM((128, 128), F32),
            pltpu.VMEM((256, 128), F32),
        ],
        out_shape=[jax.ShapeDtypeStruct((n // 8, A * 8, 128), BF)]
        + [jax.ShapeDtypeStruct((n, 19 * 128), BF)] * 4,
        input_output_aliases={given + i: i for i in range(len(held))},
        compiler_params=pltpu.CompilerParams(vmem_limit_bytes=PREP_MIB * MIB),
        cost_estimate=pl.CostEstimate(
            flops=20_000_000, bytes_accessed=4_000_000, transcendentals=0
        ),
        name="prep",
    )(*args, *held)


def repeat(step):
    @pl.loop(0, M // 4)
    def _(i):
        for u in range(4):
            step(4 * i + u)

    step(M - 1)


def spectra_kernel(w_ref, f_ref, p_ref, s):
    for g in range(8):
        y = jnp.concatenate([w_ref[2 * g], w_ref[2 * g + 1]], axis=1)
        s[:, 256 * g : 256 * g + 256] = jnp.dot(f_ref[...], y, preferred_element_type=F32)

    def turn(m):
        for i in range(2):
            row = pl.multiple_of(m * 16 + 8 * i, 8)
            v = jnp.concatenate([s[pl.ds(row, 8), 128 * g : 128 * g + 128] for g in range(16)], axis=0)
            p_ref[m, :, 128 * i : 128 * i + 128] = v.T.astype(BF)

    repeat(turn)


def spectra(w, fwd_k):
    v = pl.BlockSpec(memory_space=pltpu.VMEM)
    return pl.pallas_call(
        spectra_kernel,
        in_specs=[v, v],
        out_specs=v,
        out_shape=jax.ShapeDtypeStruct((M, 128, 256), BF),
        scratch_shapes=[pltpu.VMEM((2 * M * 8, 2048), F32)],
        compiler_params=pltpu.CompilerParams(vmem_limit_bytes=16 * MIB),
        cost_estimate=pl.CostEstimate(flops=1000, bytes_accessed=1000, transcendentals=0),
        name="spectra",
    )(w, fwd_k)


def ref_kernel(b_ref, f_ref, r_ref, s):
    for y in range(4):
        for xh in range(2):
            for t in range(9):
                v = b_ref[y, xh, :, t * 128 : (t + 1) * 128].astype(F32)
                row = (y * 2 + xh) * 72 + 8 * t
                s[row : row + 8, 0:128] = v[0:8]
                s[row : row + 8, 128:256] = v[8:16]
    out = jnp.dot(f_ref[...], s[...].astype(BF), preferred_element_type=F32)
    for m in range(M):
        for i in range(2):
            r = 16 * m + 8 * i
            r_ref[m, :, 128 * i : 128 * i + 128] = jnp.concatenate(
                [out[r : r + 8, 0:128], out[r : r + 8, 128:256]], axis=0
            ).astype(BF)


def ref_spectra(blocks, fwd_k):
    v = pl.BlockSpec(memory_space=pltpu.VMEM)
    return pl.pallas_call(
        ref_kernel,
        in_specs=[v, v],
        out_specs=v,
        out_shape=jax.ShapeDtypeStruct((M, 16, 256), BF),
        scratch_shapes=[pltpu.VMEM((A * 8, 256), F32)],
        compiler_params=pltpu.CompilerParams(vmem_limit_bytes=8 * MIB),
        cost_estimate=pl.CostEstimate(flops=1000, bytes_accessed=1000, transcendentals=0),
        name="ref_spectra",
    )(blocks, fwd_k)


def score_kernel(*refs):
    p_ref, blocks, inv_ref, o_ref, xs = refs[0], refs[1:5], refs[5], refs[6], refs[7]
    xs[:, 2 * M * 8 :, :] = jnp.zeros((16, K_INV - 2 * M * 8, 256), BF)

    def cross(m):
        upper = p_ref[m]
        re, im = upper[:, 0:128], upper[:, 128:256]
        rhs = jnp.concatenate([upper, jnp.concatenate([im, -re], axis=1)], axis=0)
        lhs = jnp.concatenate([b[i, m] for b in blocks for i in range(4)], axis=0)
        x = jnp.dot(lhs, rhs, preferred_element_type=F32)
        row = pl.multiple_of(m * 16, 16)
        for g in range(16):
            for h in range(2):
                k = 16 * g + 8 * h
                xs[g, pl.ds(row, 16), 128 * h : 128 * h + 128] = jnp.concatenate(
                    [x[k : k + 8, 0:128], x[k : k + 8, 128:256]], axis=0
                ).astype(BF)

    repeat(cross)

    def four(i, best):
        for u in range(4):
            y = jnp.dot(inv_ref[...], xs[4 * i + u], preferred_element_type=F32)
            for t in range(A):
                best = jnp.maximum(best, y[8 * t : 8 * t + 8])
        return best

    best = lax.fori_loop(0, 4, four, jnp.full((8, 256), -jnp.inf, F32))
    best = jnp.max(best, axis=0, keepdims=True)
    o_ref[...] = jnp.maximum(best[:, 0:128], best[:, 128:256])


def scores_of(p, blocks, inv_k):
    v = pl.BlockSpec(memory_space=pltpu.VMEM)
    return pl.pallas_call(
        score_kernel,
        in_specs=[v] * 6,
        out_specs=v,
        out_shape=jax.ShapeDtypeStruct((1, 128), F32),
        scratch_shapes=[pltpu.VMEM((16, K_INV, 256), BF)],
        compiler_params=pltpu.CompilerParams(vmem_limit_bytes=20 * MIB),
        cost_estimate=pl.CostEstimate(flops=6_000_000_000, bytes_accessed=8_000_000, transcendentals=0),
        name="scores",
    )(p, *blocks, inv_k)


def sums_kernel(sc, c0, c1, c2, c3, tab_ref, mine, other, acc):
    width = 18 * 128
    lane = lax.broadcasted_iota(jnp.int32, (128, 256), 1).astype(F32)
    picks, groups = [], []
    for c in (c0, c1, c2, c3):
        meta = c[:, width : width + 128].astype(F32)
        picks.append(jnp.where(lane == meta[:, 0:1], 1.0, 0.0).astype(F32).T.astype(BF))
        groups.append(jnp.where(lane == meta[:, 1:2], 1.0, 0.0).astype(BF))
    pick = jnp.concatenate(picks, axis=1)
    group = jnp.concatenate(groups, axis=0)
    count = jnp.dot(pick, group, preferred_element_type=F32)
    flipped = tab_ref[...].T
    tab = jnp.concatenate([flipped, flipped], axis=1)
    wsum = jnp.dot(count, tab * tab, precision=lax.Precision.HIGHEST, preferred_element_type=F32)
    for t in range(9):
        cols = slice(256 * t, 256 * t + 256)
        x = jnp.concatenate([c[:, cols] for c in (c0, c1, c2, c3)], axis=0)
        acc[:, cols] = jnp.dot(pick, x, preferred_element_type=F32)
    left = lax.broadcasted_iota(jnp.int32, (256, 128), 1) < R
    for ref, core in ((mine, sc[2]), (other, 1 - sc[2])):
        for xh in range(2):
            start = pl.multiple_of((9 * xh + 4 * core) * 128, 128)
            ref[xh] = acc[:, pl.ds(start, 640)]
            mid = acc[:, (9 * xh + 4) * 128 : (9 * xh + 5) * 128]
            keep = jnp.logical_xor(left, core == 1)
            ref[xh, :, pl.ds(pl.multiple_of((1 - core) * 512, 128), 128)] = jnp.where(keep, mid, wsum)


def class_sums(sc, cs, tab):
    v = pl.BlockSpec(memory_space=pltpu.VMEM)
    shape = jax.ShapeDtypeStruct((2, 256, 640), F32)
    return pl.pallas_call(
        sums_kernel,
        in_specs=[pl.BlockSpec(memory_space=pltpu.SMEM)] + [v] * 5,
        out_specs=[v, v],
        out_shape=[shape, shape],
        scratch_shapes=[pltpu.VMEM((256, 18 * 128), F32)],
        compiler_params=pltpu.CompilerParams(vmem_limit_bytes=VMEM_LIMIT),
        cost_estimate=pl.CostEstimate(flops=700_000_000, bytes_accessed=5_000_000, transcendentals=0),
        name="class_sums",
    )(sc, *cs, tab)


def cut_x_kernel(sc, a_ref, b_ref, o0, o1, o2, o3):
    for dx, o in enumerate((o0, o1, o2, o3)):
        x = lax.rem(sc[1] + dx, 4)
        xh, xl = x // 2, lax.rem(x, 2)
        rows = pl.ds(pl.multiple_of(xl * 128, 128), 128)
        o[...] = (a_ref[xh, rows, :] + b_ref[xh, rows, :]).astype(o.dtype)


def cut_x(sc, a, b):
    v = pl.BlockSpec(memory_space=pltpu.VMEM)
    return pl.pallas_call(
        cut_x_kernel,
        in_specs=[pl.BlockSpec(memory_space=pltpu.SMEM), v, v],
        out_specs=[v] * 4,
        out_shape=[jax.ShapeDtypeStruct((128, 640), F32)] + [jax.ShapeDtypeStruct((128, 640), BF)] * 3,
        compiler_params=pltpu.CompilerParams(vmem_limit_bytes=VMEM_LIMIT),
        cost_estimate=pl.CostEstimate(flops=400_000, bytes_accessed=3_900_000, transcendentals=0),
        name="cut_x",
    )(sc, a, b)


def cut_z_kernel(sc, a0, a1, a2, a3, o0, o1, o2, o3):
    for dz, o in enumerate((o0, o1, o2, o3)):
        z = lax.rem(sc[3] + dz, 4)
        rows = pl.ds(pl.multiple_of(z * 32, 32), 32)
        far = a1[rows, :].astype(F32) + a2[rows, :].astype(F32) + a3[rows, :].astype(F32)
        o[...] = a0[rows, :] + far


def cut_z(sc, parts):
    v = pl.BlockSpec(memory_space=pltpu.VMEM)
    return pl.pallas_call(
        cut_z_kernel,
        in_specs=[pl.BlockSpec(memory_space=pltpu.SMEM)] + [v] * 4,
        out_specs=[v] * 4,
        out_shape=[jax.ShapeDtypeStruct((32, 640), F32)] * 4,
        compiler_params=pltpu.CompilerParams(vmem_limit_bytes=VMEM_LIMIT),
        cost_estimate=pl.CostEstimate(flops=400_000, bytes_accessed=1_700_000, transcendentals=0),
        name="cut_z",
    )(sc, *parts)


def final_kernel(sc, a0, a1, a2, a3, o_ref):
    s = (a0[...] + a1[...]) + (a2[...] + a3[...])
    odd = sc[2] == 1
    left = lax.broadcasted_iota(jnp.int32, (32, 128), 1) < R
    tile = [s[:, 128 * t : 128 * t + 128] for t in range(5)]
    held = jnp.where(odd, tile[0], tile[4])
    turned = pltpu.roll(held, R, 1)
    weight = jnp.where(jnp.logical_xor(left, odd), turned, held)
    tile = [t / (weight + TAU) for t in tile]
    rolled = [pltpu.roll(t, R, 1) for t in tile]
    later = [jnp.where(left, rolled[t], rolled[t + 1]) for t in range(4)] + [rolled[4]]
    for t in range(4):
        o_ref[:, 128 * t : 128 * t + 128] = jnp.where(odd, later[t], tile[t])[0:25]
    o_ref[:, 512:576] = jnp.where(odd, later[4], tile[4])[0:25, 0:R]


def final(sc, parts):
    v = pl.BlockSpec(memory_space=pltpu.VMEM)
    return pl.pallas_call(
        final_kernel,
        in_specs=[pl.BlockSpec(memory_space=pltpu.SMEM)] + [v] * 4,
        out_specs=v,
        out_shape=jax.ShapeDtypeStruct((25, 576), F32),
        compiler_params=pltpu.CompilerParams(vmem_limit_bytes=2 * MIB),
        name="final",
    )(sc, *parts)


def place(y, x, z, core):
    return ((y % 4) * 4 + (x % 4) // 2 * 2 + core % 2) * 8 + (x % 2) * 4 + z % 4


def permutation(move):
    return [
        (place(y, x, z, c), place(*move(y, x, z, c)))
        for y in range(4)
        for x in range(4)
        for z in range(4)
        for c in range(2)
    ]


CORE = permutation(lambda y, x, z, c: (y, x, z, c + 1))
HIGH = permutation(lambda y, x, z, c: (y, x + 2, z, c))
LOW = permutation(lambda y, x, z, c: (y, x ^ 1, z, c))
Y_NEAR = permutation(lambda y, x, z, c: (y ^ 1, x, z, c))
Y_FAR = permutation(lambda y, x, z, c: (y + 2, x, z, c))
YS = [permutation(lambda y, x, z, c, d=d: (y + d, x, z, c)) for d in range(4)]
XS = [permutation(lambda y, x, z, c, d=d: (y, x + d, z, c)) for d in range(4)]
ZS = [permutation(lambda y, x, z, c, d=d: (y, x, z + d, c)) for d in range(4)]


def move(value, pairs):
    return lax.ppermute(value, AXES, pairs)


def after(values, *others):
    return lax.optimization_barrier((*values, *others))[: len(values)]


def join(own, other, upper):
    lower = upper == 0
    return jnp.stack([jnp.where(lower, own, other), jnp.where(lower, other, own)])


def per_device(particles, references, owner, class_offset, rotation, shifts, ctf_group, ctf_table):
    fwd_np, inv_np = tables()
    fwd_k, inv_k = jnp.asarray(fwd_np), jnp.asarray(inv_np)
    fx, fy = (jnp.asarray(t) for t in freq_tables())
    dom, cls = lax.axis_index("dom"), lax.axis_index("cls")
    y, xh, core = dom // 4, dom // 2 % 2, dom % 2
    xl, z = cls // 4, cls % 4
    sc = jnp.stack([y, xh * 2 + xl, core, z]).astype(jnp.int32)

    low, high = references[0:16], references[9:25]
    first = core == 0
    keep = jnp.where(first, low, high)
    give = jnp.where(first, high, low)
    got = move(give, CORE)
    block = jnp.where(
        first, jnp.concatenate([keep, got], axis=1), jnp.concatenate([got, keep], axis=1)
    )
    rows = [shifts.T, rotation[None], owner.T, class_offset[None], ctf_group[None]]
    table = ctf_table.T
    block, rows[1] = lax.optimization_barrier((block, rows[1]))
    half = prep(particles, rows, table, fx, fy, 0)
    far = move(block, HIGH)
    far, *half = lax.optimization_barrier((far, *half))
    pair = join(block, far, xh)
    pair, rows[1] = lax.optimization_barrier((pair, rows[1]))
    weighted, *sent = prep(particles, rows, table, fx, fy, 4, half)
    near = move(pair, Y_NEAR)
    near, weighted, *sent = lax.optimization_barrier((near, weighted, *sent))
    quad = join(pair, near, y % 2)
    octet = join(quad, move(quad, Y_FAR), y // 2).reshape(4, 2, 16, 1152)

    across = move(sent[2], YS[2])
    part = spectra(weighted, fwd_k)
    own = ref_spectra(octet, fwd_k)
    up, down = move(own, ZS[1]), move(own, ZS[3])
    side = move(own, LOW)
    side_up, side_down = move(side, ZS[1]), move(side, ZS[3])
    one, three = after([sent[1], sent[3]], across, part, up, down)
    held = [sent[0], move(one, YS[1]), across, move(three, YS[3])]
    on_up, on_down = move(up, ZS[1]), move(side_down, ZS[3])
    early = jnp.stack([own, side, up, down])
    early_twin = move(early, CORE)
    held = after(held, side_up, side_down)
    mine, other = class_sums(sc, held, table)
    cut = cut_x(sc, mine, move(other, CORE))
    late = jnp.stack([side_up, side_down, on_up, on_down])
    late_twin = move(late, CORE)
    cut = [cut[0]] + [move(cut[d], XS[d]) for d in (1, 2, 3)]
    scores = scores_of(part, [early, early_twin, late, late_twin], inv_k)
    *cut, scores = lax.optimization_barrier((*cut, scores))
    cut = cut_z(sc, cut)
    cut = [cut[0]] + [move(cut[d], ZS[d]) for d in (1, 2, 3)]
    return scores[0], final(sc, cut)


def solution(mesh):
    return jax.shard_map(
        per_device,
        mesh=mesh,
        in_specs=(
            P(("dom", "cls"), None),
            P("cls", "dom"),
            P(("dom", "cls"), None),
            P(("dom", "cls")),
            P(("dom", "cls")),
            P(("dom", "cls"), None),
            P(("dom", "cls")),
            P(),
        ),
        out_specs=(P(("dom", "cls")), P("cls", "dom")),
        check_vma=False,
    )
```

```python
import functools

import jax
import jax.numpy as jnp
import numpy as np
from jax import lax
from jax.experimental import pallas as pl
from jax.experimental.pallas import tpu as pltpu
from jax.sharding import PartitionSpec as P

A = 72
M = 37
R = 64
BOX = 128
TAU = 1.0
AXES = ("dom", "cls")
BF = jnp.bfloat16
F32 = jnp.float32
MIB = 1024 * 1024
VMEM_LIMIT = 8 * MIB
PREP_MIB = 56
K_INV = 640


def tables():
    m = np.arange(M)[:, None]
    a = np.arange(A)[None, :]
    turn = 2.0 * np.pi * ((m * a) % A) / A
    fwd = np.stack([np.cos(turn), -np.sin(turn)], axis=1).reshape(2 * M, A)
    gain = np.where((np.arange(M) == 0) | (np.arange(M) == A // 2), 1.0, 2.0)[:, None]
    inv = np.stack([np.cos(turn) / A, -np.sin(turn) / A], axis=1).astype(BF).astype(np.float32)
    inv = (inv * gain[:, None, :]).reshape(2 * M, A).T
    eye = np.eye(8, dtype=np.float32)
    fwd_k = np.kron(fwd.astype(np.float32), eye).astype(BF)
    inv_k = np.zeros((A * 8, K_INV), np.float32)
    inv_k[:, : 2 * M * 8] = np.kron(inv, eye)
    return fwd_k, inv_k.astype(BF)


def freq_tables():
    angle = 2.0 * np.pi * np.arange(A // 2) / A
    radius = np.tile(np.arange(1, R + 1), 2)
    fx = np.cos(angle)[:, None] * radius[None, :] / BOX
    fy = np.sin(angle)[:, None] * radius[None, :] / BOX
    return fx.astype(np.float32), fy.astype(np.float32)


def cos_poly():
    n = 7
    nodes = (np.cos((np.arange(64) + 0.5) * np.pi / 64) + 1.0) / 8.0
    return [float(c) for c in np.polynomial.chebyshev.Chebyshev.fit(
        nodes, np.cos(2.0 * np.pi * np.sqrt(nodes)), n - 1, domain=[0.0, 0.25]
    ).convert(kind=np.polynomial.Polynomial).coef]


COEF = cos_poly()


def prep_kernel(first, x_ref, shift_ref, rot_ref, own_ref, off_ref, grp_ref, tab_ref, fx_ref, fy_ref, *refs):
    w_ref, c0, c1, c2, c3, ws, us, aux, tab = refs[-9:]
    dom, cls = lax.axis_index("dom"), lax.axis_index("cls")
    mine = 2 * (dom * 8 + cls)
    step = pl.program_id(0)

    @pl.when(step == 0)
    def _():
        shift_rows = shift_ref[...].astype(F32)
        group = grp_ref[...]
        rows = [
            shift_rows,
            rot_ref[...].astype(F32),
            (group - mine).astype(F32),
            (own_ref[...] * 32 + off_ref[...]).astype(F32),
            group.astype(F32),
            jnp.zeros((122, 128), F32),
        ]
        aux[...] = jnp.concatenate(rows, axis=0).T
        flipped = tab_ref[...].T
        tab[...] = jnp.concatenate([flipped, flipped], axis=1)

    here = aux[pl.ds(pl.multiple_of((step + first) * 16, 16), 16), :]
    lane = lax.broadcasted_iota(jnp.int32, (16, 128), 1)
    left = lane < R
    shift = jnp.where(left, 0.0, -0.25).astype(F32)
    sxb = jnp.broadcast_to(here[:, 0:1], (16, 128))
    syb = jnp.broadcast_to(here[:, 1:2], (16, 128))
    ctf = jnp.where(here[:, 3:4] > 0.5, tab[pl.ds(mine + 1, 1), :], tab[pl.ds(mine, 1), :])
    ctf_s = jnp.where(left, -ctf, ctf)
    for b in range(A // 4):
        done = []
        for a in (2 * b, 2 * b + 1):
            v = (sxb * fx_ref[a : a + 1, :] + syb * fy_ref[a : a + 1, :]) + shift
            v = v - jnp.round(v)
            q = v * v
            e = jnp.full_like(q, COEF[-1])
            for k in COEF[-2::-1]:
                e = e * q + k
            er = pltpu.roll(e, R, 1)
            cc = jnp.where(left, e, er) * ctf
            ss = jnp.where(left, er, e) * ctf_s
            x0 = x_ref[:, a * 128 : (a + 1) * 128].astype(F32)
            h = a + A // 2
            x1 = x_ref[:, h * 128 : (h + 1) * 128].astype(F32)
            w0 = x0 * cc + pltpu.roll(x0, R, 1) * ss
            w1 = x1 * cc - pltpu.roll(x1, R, 1) * ss
            ws[:, a * 128 : (a + 1) * 128] = w0
            ws[:, h * 128 : (h + 1) * 128] = w1
            done.append((w0, w1))
        for half in (0, 1):
            row = (2 * b + half * (A // 2)) * 8
            for g in (0, 1):
                w_ref[g, row : row + 16, :] = jnp.concatenate(
                    [done[0][half][8 * g : 8 * g + 8], done[1][half][8 * g : 8 * g + 8]], axis=0
                ).astype(BF)
    rotb = jnp.broadcast_to(here[:, 2:3], (16, 128)).astype(jnp.int32)
    bit = [(rotb & (1 << k)) != 0 for k in range(7)]
    for r in range(8):
        t = [ws[:, (r + 8 * n) * 128 : (r + 8 * n + 1) * 128] for n in range(9)]
        for k in range(4):
            t = [jnp.where(bit[3 + k], t[(n + (1 << k)) % 9], t[n]) for n in range(9)]
        for n in range(9):
            us[:, (r + 8 * n) * 128 : (r + 8 * n + 1) * 128] = t[n]
    for j0 in range(0, A, 8):
        t = [us[:, ((j0 + i) % A) * 128 : ((j0 + i) % A + 1) * 128] for i in range(15)]
        t = [jnp.where(bit[0], t[i + 1], t[i]) for i in range(14)]
        t = [jnp.where(bit[1], t[i + 2], t[i]) for i in range(12)]
        for i in range(8):
            ws[:, (j0 + i) * 128 : (j0 + i + 1) * 128] = jnp.where(bit[2], t[i + 4], t[i])
    meta = jnp.where(lane == 0, here[:, 4:5], jnp.where(lane == 1, here[:, 5:6], 0.0)).astype(BF)
    width = 18 * 128
    for dy, c_ref in enumerate((c0, c1, c2, c3)):
        dest = lax.rem(dom // 4 + dy, 4)
        start = pl.multiple_of(dest * width, 128)
        c_ref[:, 0:width] = ws[:, pl.ds(start, width)].astype(BF)
        c_ref[:, width : width + 128] = meta


def prep(particles, rows, table, fx, fy, first, held=()):
    n = particles.shape[0]
    whole = lambda a: pl.BlockSpec(a.shape, lambda i: (0,) * a.ndim)
    block = lambda i: (i + first, 0)
    args = [particles, *rows, table, fx, fy]
    given = len(args)
    return pl.pallas_call(
        functools.partial(prep_kernel, first),
        grid=(n // 32,),
        in_specs=[pl.BlockSpec((16, A * 128), block)]
        + [whole(a) for a in args[1:]]
        + [pl.BlockSpec(memory_space=pltpu.HBM)] * len(held),
        out_specs=[pl.BlockSpec((2, A * 8, 128), lambda i: (i + first, 0, 0))]
        + [pl.BlockSpec((16, 19 * 128), block)] * 4,
        scratch_shapes=[
            pltpu.VMEM((16, A * 128), F32),
            pltpu.VMEM((16, A * 128), F32),
            pltpu.VMEM((128, 128), F32),
            pltpu.VMEM((256, 128), F32),
        ],
        out_shape=[jax.ShapeDtypeStruct((n // 8, A * 8, 128), BF)]
        + [jax.ShapeDtypeStruct((n, 19 * 128), BF)] * 4,
        input_output_aliases={given + i: i for i in range(len(held))},
        compiler_params=pltpu.CompilerParams(vmem_limit_bytes=PREP_MIB * MIB),
        cost_estimate=pl.CostEstimate(
            flops=20_000_000, bytes_accessed=4_000_000, transcendentals=0
        ),
        name="prep",
    )(*args, *held)


def repeat(step):
    @pl.loop(0, M // 4)
    def _(i):
        for u in range(4):
            step(4 * i + u)

    step(M - 1)


def spectra_kernel(w_ref, f_ref, p_ref, s):
    for g in range(8):
        y = jnp.concatenate([w_ref[2 * g], w_ref[2 * g + 1]], axis=1)
        s[:, 256 * g : 256 * g + 256] = jnp.dot(f_ref[...], y, preferred_element_type=F32)

    def turn(m):
        for i in range(2):
            row = pl.multiple_of(m * 16 + 8 * i, 8)
            v = jnp.concatenate([s[pl.ds(row, 8), 128 * g : 128 * g + 128] for g in range(16)], axis=0)
            p_ref[m, :, 128 * i : 128 * i + 128] = v.T.astype(BF)

    repeat(turn)


def spectra(w, fwd_k):
    v = pl.BlockSpec(memory_space=pltpu.VMEM)
    return pl.pallas_call(
        spectra_kernel,
        in_specs=[v, v],
        out_specs=v,
        out_shape=jax.ShapeDtypeStruct((M, 128, 256), BF),
        scratch_shapes=[pltpu.VMEM((2 * M * 8, 2048), F32)],
        compiler_params=pltpu.CompilerParams(vmem_limit_bytes=16 * MIB),
        cost_estimate=pl.CostEstimate(flops=1000, bytes_accessed=1000, transcendentals=0),
        name="spectra",
    )(w, fwd_k)


def ref_kernel(b_ref, f_ref, r_ref, s):
    for y in range(4):
        for xh in range(2):
            for t in range(9):
                v = b_ref[y, xh, :, t * 128 : (t + 1) * 128].astype(F32)
                row = (y * 2 + xh) * 72 + 8 * t
                s[row : row + 8, 0:128] = v[0:8]
                s[row : row + 8, 128:256] = v[8:16]
    out = jnp.dot(f_ref[...], s[...].astype(BF), preferred_element_type=F32)
    for m in range(M):
        for i in range(2):
            r = 16 * m + 8 * i
            r_ref[m, :, 128 * i : 128 * i + 128] = jnp.concatenate(
                [out[r : r + 8, 0:128], out[r : r + 8, 128:256]], axis=0
            ).astype(BF)


def ref_spectra(blocks, fwd_k):
    v = pl.BlockSpec(memory_space=pltpu.VMEM)
    return pl.pallas_call(
        ref_kernel,
        in_specs=[v, v],
        out_specs=v,
        out_shape=jax.ShapeDtypeStruct((M, 16, 256), BF),
        scratch_shapes=[pltpu.VMEM((A * 8, 256), F32)],
        compiler_params=pltpu.CompilerParams(vmem_limit_bytes=8 * MIB),
        cost_estimate=pl.CostEstimate(flops=1000, bytes_accessed=1000, transcendentals=0),
        name="ref_spectra",
    )(blocks, fwd_k)


def score_kernel(*refs):
    p_ref, blocks, inv_ref, o_ref, xs = refs[0], refs[1:5], refs[5], refs[6], refs[7]
    xs[:, 2 * M * 8 :, :] = jnp.zeros((16, K_INV - 2 * M * 8, 256), BF)

    def cross(m):
        upper = p_ref[m]
        re, im = upper[:, 0:128], upper[:, 128:256]
        rhs = jnp.concatenate([upper, jnp.concatenate([im, -re], axis=1)], axis=0)
        lhs = jnp.concatenate([b[i, m] for b in blocks for i in range(4)], axis=0)
        x = jnp.dot(lhs, rhs, preferred_element_type=F32)
        row = pl.multiple_of(m * 16, 16)
        for g in range(16):
            for h in range(2):
                k = 16 * g + 8 * h
                xs[g, pl.ds(row, 16), 128 * h : 128 * h + 128] = jnp.concatenate(
                    [x[k : k + 8, 0:128], x[k : k + 8, 128:256]], axis=0
                ).astype(BF)

    repeat(cross)

    def four(i, best):
        for u in range(4):
            y = jnp.dot(inv_ref[...], xs[4 * i + u], preferred_element_type=F32)
            for t in range(A):
                best = jnp.maximum(best, y[8 * t : 8 * t + 8])
        return best

    best = lax.fori_loop(0, 4, four, jnp.full((8, 256), -jnp.inf, F32))
    best = jnp.max(best, axis=0, keepdims=True)
    o_ref[...] = jnp.maximum(best[:, 0:128], best[:, 128:256])


def scores_of(p, blocks, inv_k):
    v = pl.BlockSpec(memory_space=pltpu.VMEM)
    return pl.pallas_call(
        score_kernel,
        in_specs=[v] * 6,
        out_specs=v,
        out_shape=jax.ShapeDtypeStruct((1, 128), F32),
        scratch_shapes=[pltpu.VMEM((16, K_INV, 256), BF)],
        compiler_params=pltpu.CompilerParams(vmem_limit_bytes=20 * MIB),
        cost_estimate=pl.CostEstimate(flops=6_000_000_000, bytes_accessed=8_000_000, transcendentals=0),
        name="scores",
    )(p, *blocks, inv_k)


def sums_kernel(sc, c0, c1, c2, c3, tab_ref, mine, other, acc):
    width = 18 * 128
    lane = lax.broadcasted_iota(jnp.int32, (128, 256), 1).astype(F32)
    picks, groups = [], []
    for c in (c0, c1, c2, c3):
        meta = c[:, width : width + 128].astype(F32)
        picks.append(jnp.where(lane == meta[:, 0:1], 1.0, 0.0).astype(F32).T.astype(BF))
        groups.append(jnp.where(lane == meta[:, 1:2], 1.0, 0.0).astype(BF))
    pick = jnp.concatenate(picks, axis=1)
    group = jnp.concatenate(groups, axis=0)
    count = jnp.dot(pick, group, preferred_element_type=F32)
    flipped = tab_ref[...].T
    tab = jnp.concatenate([flipped, flipped], axis=1)
    wsum = jnp.dot(count, tab * tab, precision=lax.Precision.HIGHEST, preferred_element_type=F32)
    for t in range(9):
        cols = slice(256 * t, 256 * t + 256)
        x = jnp.concatenate([c[:, cols] for c in (c0, c1, c2, c3)], axis=0)
        acc[:, cols] = jnp.dot(pick, x, preferred_element_type=F32)
    left = lax.broadcasted_iota(jnp.int32, (256, 128), 1) < R
    for ref, core in ((mine, sc[2]), (other, 1 - sc[2])):
        for xh in range(2):
            start = pl.multiple_of((9 * xh + 4 * core) * 128, 128)
            ref[xh] = acc[:, pl.ds(start, 640)]
            mid = acc[:, (9 * xh + 4) * 128 : (9 * xh + 5) * 128]
            keep = jnp.logical_xor(left, core == 1)
            ref[xh, :, pl.ds(pl.multiple_of((1 - core) * 512, 128), 128)] = jnp.where(keep, mid, wsum)


def class_sums(sc, cs, tab):
    v = pl.BlockSpec(memory_space=pltpu.VMEM)
    shape = jax.ShapeDtypeStruct((2, 256, 640), F32)
    return pl.pallas_call(
        sums_kernel,
        in_specs=[pl.BlockSpec(memory_space=pltpu.SMEM)] + [v] * 5,
        out_specs=[v, v],
        out_shape=[shape, shape],
        scratch_shapes=[pltpu.VMEM((256, 18 * 128), F32)],
        compiler_params=pltpu.CompilerParams(vmem_limit_bytes=VMEM_LIMIT),
        cost_estimate=pl.CostEstimate(flops=700_000_000, bytes_accessed=5_000_000, transcendentals=0),
        name="class_sums",
    )(sc, *cs, tab)


def cut_x_kernel(sc, a_ref, b_ref, o0, o1, o2, o3):
    for dx, o in enumerate((o0, o1, o2, o3)):
        x = lax.rem(sc[1] + dx, 4)
        xh, xl = x // 2, lax.rem(x, 2)
        rows = pl.ds(pl.multiple_of(xl * 128, 128), 128)
        o[...] = (a_ref[xh, rows, :] + b_ref[xh, rows, :]).astype(o.dtype)


def cut_x(sc, a, b):
    v = pl.BlockSpec(memory_space=pltpu.VMEM)
    return pl.pallas_call(
        cut_x_kernel,
        in_specs=[pl.BlockSpec(memory_space=pltpu.SMEM), v, v],
        out_specs=[v] * 4,
        out_shape=[jax.ShapeDtypeStruct((128, 640), F32)] + [jax.ShapeDtypeStruct((128, 640), BF)] * 3,
        compiler_params=pltpu.CompilerParams(vmem_limit_bytes=VMEM_LIMIT),
        cost_estimate=pl.CostEstimate(flops=400_000, bytes_accessed=3_900_000, transcendentals=0),
        name="cut_x",
    )(sc, a, b)


def cut_z_kernel(sc, a0, a1, a2, a3, o0, o1, o2, o3):
    for dz, o in enumerate((o0, o1, o2, o3)):
        z = lax.rem(sc[3] + dz, 4)
        rows = pl.ds(pl.multiple_of(z * 32, 32), 32)
        far = a1[rows, :].astype(F32) + a2[rows, :].astype(F32) + a3[rows, :].astype(F32)
        o[...] = (a0[rows, :] + far).astype(o.dtype)


def cut_z(sc, parts):
    v = pl.BlockSpec(memory_space=pltpu.VMEM)
    return pl.pallas_call(
        cut_z_kernel,
        in_specs=[pl.BlockSpec(memory_space=pltpu.SMEM)] + [v] * 4,
        out_specs=[v] * 4,
        out_shape=[jax.ShapeDtypeStruct((32, 640), F32)] + [jax.ShapeDtypeStruct((32, 640), BF)] * 3,
        compiler_params=pltpu.CompilerParams(vmem_limit_bytes=VMEM_LIMIT),
        cost_estimate=pl.CostEstimate(flops=400_000, bytes_accessed=1_700_000, transcendentals=0),
        name="cut_z",
    )(sc, *parts)


def final_kernel(sc, a0, a1, a2, a3, o_ref):
    s = a0[...] + (a1[...].astype(F32) + a2[...].astype(F32) + a3[...].astype(F32))
    odd = sc[2] == 1
    left = lax.broadcasted_iota(jnp.int32, (32, 128), 1) < R
    tile = [s[:, 128 * t : 128 * t + 128] for t in range(5)]
    held = jnp.where(odd, tile[0], tile[4])
    turned = pltpu.roll(held, R, 1)
    weight = jnp.where(jnp.logical_xor(left, odd), turned, held)
    tile = [t / (weight + TAU) for t in tile]
    rolled = [pltpu.roll(t, R, 1) for t in tile]
    later = [jnp.where(left, rolled[t], rolled[t + 1]) for t in range(4)] + [rolled[4]]
    for t in range(4):
        o_ref[:, 128 * t : 128 * t + 128] = jnp.where(odd, later[t], tile[t])[0:25]
    o_ref[:, 512:576] = jnp.where(odd, later[4], tile[4])[0:25, 0:R]


def final(sc, parts):
    v = pl.BlockSpec(memory_space=pltpu.VMEM)
    return pl.pallas_call(
        final_kernel,
        in_specs=[pl.BlockSpec(memory_space=pltpu.SMEM)] + [v] * 4,
        out_specs=v,
        out_shape=jax.ShapeDtypeStruct((25, 576), F32),
        compiler_params=pltpu.CompilerParams(vmem_limit_bytes=2 * MIB),
        name="final",
    )(sc, *parts)


def place(y, x, z, core):
    return ((y % 4) * 4 + (x % 4) // 2 * 2 + core % 2) * 8 + (x % 2) * 4 + z % 4


def permutation(move):
    return [
        (place(y, x, z, c), place(*move(y, x, z, c)))
        for y in range(4)
        for x in range(4)
        for z in range(4)
        for c in range(2)
    ]


CORE = permutation(lambda y, x, z, c: (y, x, z, c + 1))
HIGH = permutation(lambda y, x, z, c: (y, x + 2, z, c))
LOW = permutation(lambda y, x, z, c: (y, x ^ 1, z, c))
Y_NEAR = permutation(lambda y, x, z, c: (y ^ 1, x, z, c))
Y_FAR = permutation(lambda y, x, z, c: (y + 2, x, z, c))
YS = [permutation(lambda y, x, z, c, d=d: (y + d, x, z, c)) for d in range(4)]
XS = [permutation(lambda y, x, z, c, d=d: (y, x + d, z, c)) for d in range(4)]
ZS = [permutation(lambda y, x, z, c, d=d: (y, x, z + d, c)) for d in range(4)]


def move(value, pairs):
    return lax.ppermute(value, AXES, pairs)


def after(values, *others):
    return lax.optimization_barrier((*values, *others))[: len(values)]


def join(own, other, upper):
    lower = upper == 0
    return jnp.stack([jnp.where(lower, own, other), jnp.where(lower, other, own)])


def per_device(particles, references, owner, class_offset, rotation, shifts, ctf_group, ctf_table):
    fwd_np, inv_np = tables()
    fwd_k, inv_k = jnp.asarray(fwd_np), jnp.asarray(inv_np)
    fx, fy = (jnp.asarray(t) for t in freq_tables())
    dom, cls = lax.axis_index("dom"), lax.axis_index("cls")
    y, xh, core = dom // 4, dom // 2 % 2, dom % 2
    xl, z = cls // 4, cls % 4
    sc = jnp.stack([y, xh * 2 + xl, core, z]).astype(jnp.int32)

    low, high = references[0:16], references[9:25]
    first = core == 0
    keep = jnp.where(first, low, high)
    give = jnp.where(first, high, low)
    got = move(give, CORE)
    block = jnp.where(
        first, jnp.concatenate([keep, got], axis=1), jnp.concatenate([got, keep], axis=1)
    )
    rows = [shifts.T, rotation[None], owner.T, class_offset[None], ctf_group[None]]
    table = ctf_table.T
    block, rows[1] = lax.optimization_barrier((block, rows[1]))
    half = prep(particles, rows, table, fx, fy, 0)
    far = move(block, HIGH)
    far, *half = lax.optimization_barrier((far, *half))
    pair = join(block, far, xh)
    pair, rows[1] = lax.optimization_barrier((pair, rows[1]))
    weighted, *sent = prep(particles, rows, table, fx, fy, 4, half)
    near = move(pair, Y_NEAR)
    near, weighted, *sent = lax.optimization_barrier((near, weighted, *sent))
    quad = join(pair, near, y % 2)
    octet = join(quad, move(quad, Y_FAR), y // 2).reshape(4, 2, 16, 1152)

    across = move(sent[2], YS[2])
    part = spectra(weighted, fwd_k)
    own = ref_spectra(octet, fwd_k)
    up, down = move(own, ZS[1]), move(own, ZS[3])
    side = move(own, LOW)
    side_up, side_down = move(side, ZS[1]), move(side, ZS[3])
    one, three = after([sent[1], sent[3]], across, part, up, down)
    held = [sent[0], move(one, YS[1]), across, move(three, YS[3])]
    on_up, on_down = move(up, ZS[1]), move(side_down, ZS[3])
    early = jnp.stack([own, side, up, down])
    early_twin = move(early, CORE)
    held = after(held, side_up, side_down)
    mine, other = class_sums(sc, held, table)
    cut = cut_x(sc, mine, move(other, CORE))
    late = jnp.stack([side_up, side_down, on_up, on_down])
    late_twin = move(late, CORE)
    cut = [cut[0]] + [move(cut[d], XS[d]) for d in (1, 2, 3)]
    scores = scores_of(part, [early, early_twin, late, late_twin], inv_k)
    *cut, scores = lax.optimization_barrier((*cut, scores))
    cut = cut_z(sc, cut)
    cut = [cut[0]] + [move(cut[d], ZS[d]) for d in (1, 2, 3)]
    return scores[0], final(sc, cut)


def solution(mesh):
    return jax.shard_map(
        per_device,
        mesh=mesh,
        in_specs=(
            P(("dom", "cls"), None),
            P("cls", "dom"),
            P(("dom", "cls"), None),
            P(("dom", "cls")),
            P(("dom", "cls")),
            P(("dom", "cls"), None),
            P(("dom", "cls")),
            P(),
        ),
        out_specs=(P(("dom", "cls")), P("cls", "dom")),
        check_vma=False,
    )
```

```python
import functools

import jax
import jax.numpy as jnp
import numpy as np
from jax import lax
from jax.experimental import pallas as pl
from jax.experimental.pallas import tpu as pltpu
from jax.sharding import PartitionSpec as P

A = 72
M = 37
R = 64
BOX = 128
TAU = 1.0
AXES = ("dom", "cls")
BF = jnp.bfloat16
F32 = jnp.float32
MIB = 1024 * 1024
VMEM_LIMIT = 8 * MIB
PREP_MIB = 56
K_INV = 640


def tables():
    m = np.arange(M)[:, None]
    a = np.arange(A)[None, :]
    turn = 2.0 * np.pi * ((m * a) % A) / A
    fwd = np.stack([np.cos(turn), -np.sin(turn)], axis=1).reshape(2 * M, A)
    gain = np.where((np.arange(M) == 0) | (np.arange(M) == A // 2), 1.0, 2.0)[:, None]
    inv = np.stack([np.cos(turn) / A, -np.sin(turn) / A], axis=1).astype(BF).astype(np.float32)
    inv = (inv * gain[:, None, :]).reshape(2 * M, A).T
    eye = np.eye(8, dtype=np.float32)
    fwd_k = np.kron(fwd.astype(np.float32), eye).astype(BF)
    inv_k = np.zeros((A * 8, K_INV), np.float32)
    inv_k[:, : 2 * M * 8] = np.kron(inv, eye)
    return fwd_k, inv_k.astype(BF)


def freq_tables():
    angle = 2.0 * np.pi * np.arange(A // 2) / A
    radius = np.tile(np.arange(1, R + 1), 2)
    fx = np.cos(angle)[:, None] * radius[None, :] / BOX
    fy = np.sin(angle)[:, None] * radius[None, :] / BOX
    return fx.astype(np.float32), fy.astype(np.float32)


def cos_poly():
    n = 7
    nodes = (np.cos((np.arange(64) + 0.5) * np.pi / 64) + 1.0) / 8.0
    return [float(c) for c in np.polynomial.chebyshev.Chebyshev.fit(
        nodes, np.cos(2.0 * np.pi * np.sqrt(nodes)), n - 1, domain=[0.0, 0.25]
    ).convert(kind=np.polynomial.Polynomial).coef]


COEF = cos_poly()


def prep_kernel(first, x_ref, shift_ref, rot_ref, own_ref, off_ref, grp_ref, tab_ref, fx_ref, fy_ref, *refs):
    w_ref, c0, c1, c2, c3, ws, us, aux, tab = refs[-9:]
    dom, cls = lax.axis_index("dom"), lax.axis_index("cls")
    mine = 2 * (dom * 8 + cls)
    step = pl.program_id(0)

    @pl.when(step == 0)
    def _():
        shift_rows = shift_ref[...].astype(F32)
        group = grp_ref[...]
        rows = [
            shift_rows,
            rot_ref[...].astype(F32),
            (group - mine).astype(F32),
            (own_ref[...] * 32 + off_ref[...]).astype(F32),
            group.astype(F32),
            jnp.zeros((122, 128), F32),
        ]
        aux[...] = jnp.concatenate(rows, axis=0).T
        flipped = tab_ref[...].T
        tab[...] = jnp.concatenate([flipped, flipped], axis=1)

    @pl.loop(0, 2)
    def _(half):
        span = pl.ds(pl.multiple_of(half * 16, 16), 16)
        here = aux[pl.ds(pl.multiple_of((2 * (step + first) + half) * 16, 16), 16), :]
        lane = lax.broadcasted_iota(jnp.int32, (16, 128), 1)
        left = lane < R
        shift = jnp.where(left, 0.0, -0.25).astype(F32)
        sxb = jnp.broadcast_to(here[:, 0:1], (16, 128))
        syb = jnp.broadcast_to(here[:, 1:2], (16, 128))
        ctf = jnp.where(here[:, 3:4] > 0.5, tab[pl.ds(mine + 1, 1), :], tab[pl.ds(mine, 1), :])
        ctf_s = jnp.where(left, -ctf, ctf)
        for b in range(A // 4):
            done = []
            for a in (2 * b, 2 * b + 1):
                v = (sxb * fx_ref[a : a + 1, :] + syb * fy_ref[a : a + 1, :]) + shift
                v = v - jnp.round(v)
                q = v * v
                e = jnp.full_like(q, COEF[-1])
                for k in COEF[-2::-1]:
                    e = e * q + k
                er = pltpu.roll(e, R, 1)
                cc = jnp.where(left, e, er) * ctf
                ss = jnp.where(left, er, e) * ctf_s
                x0 = x_ref[span, a * 128 : (a + 1) * 128].astype(F32)
                h = a + A // 2
                x1 = x_ref[span, h * 128 : (h + 1) * 128].astype(F32)
                w0 = x0 * cc + pltpu.roll(x0, R, 1) * ss
                w1 = x1 * cc - pltpu.roll(x1, R, 1) * ss
                ws[:, a * 128 : (a + 1) * 128] = w0
                ws[:, h * 128 : (h + 1) * 128] = w1
                done.append((w0, w1))
            for turn in (0, 1):
                row = (2 * b + turn * (A // 2)) * 8
                for g in (0, 1):
                    w_ref[2 * half + g, row : row + 16, :] = jnp.concatenate(
                        [done[0][turn][8 * g : 8 * g + 8], done[1][turn][8 * g : 8 * g + 8]], axis=0
                    ).astype(BF)
        rotb = jnp.broadcast_to(here[:, 2:3], (16, 128)).astype(jnp.int32)
        bit = [(rotb & (1 << k)) != 0 for k in range(7)]
        for r in range(8):
            t = [ws[:, (r + 8 * n) * 128 : (r + 8 * n + 1) * 128] for n in range(9)]
            for k in range(4):
                t = [jnp.where(bit[3 + k], t[(n + (1 << k)) % 9], t[n]) for n in range(9)]
            for n in range(9):
                us[:, (r + 8 * n) * 128 : (r + 8 * n + 1) * 128] = t[n]
        for j0 in range(0, A, 8):
            t = [us[:, ((j0 + i) % A) * 128 : ((j0 + i) % A + 1) * 128] for i in range(15)]
            t = [jnp.where(bit[0], t[i + 1], t[i]) for i in range(14)]
            t = [jnp.where(bit[1], t[i + 2], t[i]) for i in range(12)]
            for i in range(8):
                ws[:, (j0 + i) * 128 : (j0 + i + 1) * 128] = jnp.where(bit[2], t[i + 4], t[i])
        meta = jnp.where(lane == 0, here[:, 4:5], jnp.where(lane == 1, here[:, 5:6], 0.0)).astype(BF)
        width = 18 * 128
        for dy, c_ref in enumerate((c0, c1, c2, c3)):
            dest = lax.rem(dom // 4 + dy, 4)
            start = pl.multiple_of(dest * width, 128)
            c_ref[span, 0:width] = ws[:, pl.ds(start, width)].astype(BF)
            c_ref[span, width : width + 128] = meta


def prep(particles, rows, table, fx, fy, first, held=()):
    n = particles.shape[0]
    whole = lambda a: pl.BlockSpec(a.shape, lambda i: (0,) * a.ndim)
    block = lambda i: (i + first, 0)
    args = [particles, *rows, table, fx, fy]
    given = len(args)
    return pl.pallas_call(
        functools.partial(prep_kernel, first),
        grid=(n // 64,),
        in_specs=[pl.BlockSpec((32, A * 128), block)]
        + [whole(a) for a in args[1:]]
        + [pl.BlockSpec(memory_space=pltpu.HBM)] * len(held),
        out_specs=[pl.BlockSpec((4, A * 8, 128), lambda i: (i + first, 0, 0))]
        + [pl.BlockSpec((32, 19 * 128), block)] * 4,
        scratch_shapes=[
            pltpu.VMEM((16, A * 128), F32),
            pltpu.VMEM((16, A * 128), F32),
            pltpu.VMEM((128, 128), F32),
            pltpu.VMEM((256, 128), F32),
        ],
        out_shape=[jax.ShapeDtypeStruct((n // 8, A * 8, 128), BF)]
        + [jax.ShapeDtypeStruct((n, 19 * 128), BF)] * 4,
        input_output_aliases={given + i: i for i in range(len(held))},
        compiler_params=pltpu.CompilerParams(vmem_limit_bytes=PREP_MIB * MIB),
        cost_estimate=pl.CostEstimate(
            flops=20_000_000, bytes_accessed=4_000_000, transcendentals=0
        ),
        name="prep",
    )(*args, *held)


def repeat(step):
    @pl.loop(0, M // 4)
    def _(i):
        for u in range(4):
            step(4 * i + u)

    step(M - 1)


def spectra_kernel(w_ref, f_ref, p_ref, s):
    for g in range(8):
        y = jnp.concatenate([w_ref[2 * g], w_ref[2 * g + 1]], axis=1)
        s[:, 256 * g : 256 * g + 256] = jnp.dot(f_ref[...], y, preferred_element_type=F32)

    def turn(m):
        for i in range(2):
            row = pl.multiple_of(m * 16 + 8 * i, 8)
            v = jnp.concatenate([s[pl.ds(row, 8), 128 * g : 128 * g + 128] for g in range(16)], axis=0)
            p_ref[m, :, 128 * i : 128 * i + 128] = v.T.astype(BF)

    repeat(turn)


def spectra(w, fwd_k):
    v = pl.BlockSpec(memory_space=pltpu.VMEM)
    return pl.pallas_call(
        spectra_kernel,
        in_specs=[v, v],
        out_specs=v,
        out_shape=jax.ShapeDtypeStruct((M, 128, 256), BF),
        scratch_shapes=[pltpu.VMEM((2 * M * 8, 2048), F32)],
        compiler_params=pltpu.CompilerParams(vmem_limit_bytes=16 * MIB),
        cost_estimate=pl.CostEstimate(flops=1000, bytes_accessed=1000, transcendentals=0),
        name="spectra",
    )(w, fwd_k)


def ref_kernel(own_ref, far_ref, f_ref, r_ref, s):
    upper = lax.rem(lax.axis_index("dom") // 8, 2)
    for ref, place_of in ((own_ref, upper), (far_ref, 1 - upper)):
        for y in range(2):
            for xh in range(2):
                for t in range(9):
                    v = ref[y, xh, :, t * 128 : (t + 1) * 128].astype(F32)
                    row = pl.multiple_of(place_of * 288 + (y * 2 + xh) * 72 + 8 * t, 8)
                    s[pl.ds(row, 8), 0:128] = v[0:8]
                    s[pl.ds(row, 8), 128:256] = v[8:16]
    out = jnp.dot(f_ref[...], s[...].astype(BF), preferred_element_type=F32)
    for m in range(M):
        for i in range(2):
            r = 16 * m + 8 * i
            r_ref[m, :, 128 * i : 128 * i + 128] = jnp.concatenate(
                [out[r : r + 8, 0:128], out[r : r + 8, 128:256]], axis=0
            ).astype(BF)


def ref_spectra(own, far, fwd_k):
    v = pl.BlockSpec(memory_space=pltpu.VMEM)
    return pl.pallas_call(
        ref_kernel,
        in_specs=[v, v, v],
        out_specs=v,
        out_shape=jax.ShapeDtypeStruct((M, 16, 256), BF),
        scratch_shapes=[pltpu.VMEM((A * 8, 256), F32)],
        compiler_params=pltpu.CompilerParams(vmem_limit_bytes=8 * MIB),
        cost_estimate=pl.CostEstimate(flops=1000, bytes_accessed=1000, transcendentals=0),
        name="ref_spectra",
    )(own, far, fwd_k)


def score_kernel(*refs):
    p_ref, blocks, inv_ref, o_ref, xs = refs[0], refs[1:5], refs[5], refs[6], refs[7]
    xs[:, 2 * M * 8 :, :] = jnp.zeros((16, K_INV - 2 * M * 8, 256), BF)

    def cross(m):
        upper = p_ref[m]
        re, im = upper[:, 0:128], upper[:, 128:256]
        rhs = jnp.concatenate([upper, jnp.concatenate([im, -re], axis=1)], axis=0)
        lhs = jnp.concatenate([b[i, m] for b in blocks for i in range(4)], axis=0)
        x = jnp.dot(lhs, rhs, preferred_element_type=F32)
        row = pl.multiple_of(m * 16, 16)
        for g in range(16):
            for h in range(2):
                k = 16 * g + 8 * h
                xs[g, pl.ds(row, 16), 128 * h : 128 * h + 128] = jnp.concatenate(
                    [x[k : k + 8, 0:128], x[k : k + 8, 128:256]], axis=0
                ).astype(BF)

    repeat(cross)

    def four(i, best):
        for u in range(4):
            y = jnp.dot(inv_ref[...], xs[4 * i + u], preferred_element_type=F32)
            for t in range(A):
                best = jnp.maximum(best, y[8 * t : 8 * t + 8])
        return best

    best = lax.fori_loop(0, 4, four, jnp.full((8, 256), -jnp.inf, F32))
    best = jnp.max(best, axis=0, keepdims=True)
    o_ref[...] = jnp.maximum(best[:, 0:128], best[:, 128:256])


def scores_of(p, blocks, inv_k):
    v = pl.BlockSpec(memory_space=pltpu.VMEM)
    return pl.pallas_call(
        score_kernel,
        in_specs=[v] * 6,
        out_specs=v,
        out_shape=jax.ShapeDtypeStruct((1, 128), F32),
        scratch_shapes=[pltpu.VMEM((16, K_INV, 256), BF)],
        compiler_params=pltpu.CompilerParams(vmem_limit_bytes=20 * MIB),
        cost_estimate=pl.CostEstimate(flops=6_000_000_000, bytes_accessed=8_000_000, transcendentals=0),
        name="scores",
    )(p, *blocks, inv_k)


def sums_kernel(sc, c0, c1, c2, c3, tab_ref, mine, other, acc):
    width = 18 * 128
    lane = lax.broadcasted_iota(jnp.int32, (128, 256), 1).astype(F32)
    picks, groups = [], []
    for c in (c0, c1, c2, c3):
        meta = c[:, width : width + 128].astype(F32)
        picks.append(jnp.where(lane == meta[:, 0:1], 1.0, 0.0).astype(F32).T.astype(BF))
        groups.append(jnp.where(lane == meta[:, 1:2], 1.0, 0.0).astype(BF))
    pick = jnp.concatenate(picks, axis=1)
    group = jnp.concatenate(groups, axis=0)
    count = jnp.dot(pick, group, preferred_element_type=F32)
    flipped = tab_ref[...].T
    tab = jnp.concatenate([flipped, flipped], axis=1)
    wsum = jnp.dot(count, tab * tab, precision=lax.Precision.HIGHEST, preferred_element_type=F32)
    for t in range(9):
        cols = slice(256 * t, 256 * t + 256)
        x = jnp.concatenate([c[:, cols] for c in (c0, c1, c2, c3)], axis=0)
        acc[:, cols] = jnp.dot(pick, x, preferred_element_type=F32)
    left = lax.broadcasted_iota(jnp.int32, (256, 128), 1) < R
    for ref, core in ((mine, sc[2]), (other, 1 - sc[2])):
        for xh in range(2):
            start = pl.multiple_of((9 * xh + 4 * core) * 128, 128)
            ref[xh] = acc[:, pl.ds(start, 640)]
            mid = acc[:, (9 * xh + 4) * 128 : (9 * xh + 5) * 128]
            keep = jnp.logical_xor(left, core == 1)
            ref[xh, :, pl.ds(pl.multiple_of((1 - core) * 512, 128), 128)] = jnp.where(keep, mid, wsum)


def class_sums(sc, cs, tab):
    v = pl.BlockSpec(memory_space=pltpu.VMEM)
    shape = jax.ShapeDtypeStruct((2, 256, 640), F32)
    return pl.pallas_call(
        sums_kernel,
        in_specs=[pl.BlockSpec(memory_space=pltpu.SMEM)] + [v] * 5,
        out_specs=[v, v],
        out_shape=[shape, shape],
        scratch_shapes=[pltpu.VMEM((256, 18 * 128), F32)],
        compiler_params=pltpu.CompilerParams(vmem_limit_bytes=VMEM_LIMIT),
        cost_estimate=pl.CostEstimate(flops=700_000_000, bytes_accessed=5_000_000, transcendentals=0),
        name="class_sums",
    )(sc, *cs, tab)


def cut_x_kernel(sc, a_ref, b_ref, o0, o1, o2, o3):
    for dx, o in enumerate((o0, o1, o2, o3)):
        x = lax.rem(sc[1] + dx, 4)
        xh, xl = x // 2, lax.rem(x, 2)
        rows = pl.ds(pl.multiple_of(xl * 128, 128), 128)
        o[...] = (a_ref[xh, rows, :] + b_ref[xh, rows, :]).astype(o.dtype)


def cut_x(sc, a, b):
    v = pl.BlockSpec(memory_space=pltpu.VMEM)
    return pl.pallas_call(
        cut_x_kernel,
        in_specs=[pl.BlockSpec(memory_space=pltpu.SMEM), v, v],
        out_specs=[v] * 4,
        out_shape=[jax.ShapeDtypeStruct((128, 640), F32)] + [jax.ShapeDtypeStruct((128, 640), BF)] * 3,
        compiler_params=pltpu.CompilerParams(vmem_limit_bytes=VMEM_LIMIT),
        cost_estimate=pl.CostEstimate(flops=400_000, bytes_accessed=3_900_000, transcendentals=0),
        name="cut_x",
    )(sc, a, b)


def cut_z_kernel(sc, a0, a1, a2, a3, o0, o1, o2, o3):
    for dz, o in enumerate((o0, o1, o2, o3)):
        z = lax.rem(sc[3] + dz, 4)
        rows = pl.ds(pl.multiple_of(z * 32, 32), 32)
        far = a1[rows, :].astype(F32) + a2[rows, :].astype(F32) + a3[rows, :].astype(F32)
        o[...] = (a0[rows, :] + far).astype(o.dtype)


def cut_z(sc, parts):
    v = pl.BlockSpec(memory_space=pltpu.VMEM)
    return pl.pallas_call(
        cut_z_kernel,
        in_specs=[pl.BlockSpec(memory_space=pltpu.SMEM)] + [v] * 4,
        out_specs=[v] * 4,
        out_shape=[jax.ShapeDtypeStruct((32, 640), F32)] + [jax.ShapeDtypeStruct((32, 640), BF)] * 3,
        compiler_params=pltpu.CompilerParams(vmem_limit_bytes=VMEM_LIMIT),
        cost_estimate=pl.CostEstimate(flops=400_000, bytes_accessed=1_700_000, transcendentals=0),
        name="cut_z",
    )(sc, *parts)


def final_kernel(sc, a0, a1, a2, a3, o_ref):
    s = a0[...] + (a1[...].astype(F32) + a2[...].astype(F32) + a3[...].astype(F32))
    odd = sc[2] == 1
    left = lax.broadcasted_iota(jnp.int32, (32, 128), 1) < R
    tile = [s[:, 128 * t : 128 * t + 128] for t in range(5)]
    held = jnp.where(odd, tile[0], tile[4])
    turned = pltpu.roll(held, R, 1)
    weight = jnp.where(jnp.logical_xor(left, odd), turned, held)
    tile = [t / (weight + TAU) for t in tile]
    rolled = [pltpu.roll(t, R, 1) for t in tile]
    later = [jnp.where(left, rolled[t], rolled[t + 1]) for t in range(4)] + [rolled[4]]
    for t in range(4):
        o_ref[:, 128 * t : 128 * t + 128] = jnp.where(odd, later[t], tile[t])[0:25]
    o_ref[:, 512:576] = jnp.where(odd, later[4], tile[4])[0:25, 0:R]


def final(sc, parts):
    v = pl.BlockSpec(memory_space=pltpu.VMEM)
    return pl.pallas_call(
        final_kernel,
        in_specs=[pl.BlockSpec(memory_space=pltpu.SMEM)] + [v] * 4,
        out_specs=v,
        out_shape=jax.ShapeDtypeStruct((25, 576), F32),
        compiler_params=pltpu.CompilerParams(vmem_limit_bytes=2 * MIB),
        name="final",
    )(sc, *parts)


def place(y, x, z, core):
    return ((y % 4) * 4 + (x % 4) // 2 * 2 + core % 2) * 8 + (x % 2) * 4 + z % 4


def permutation(move):
    return [
        (place(y, x, z, c), place(*move(y, x, z, c)))
        for y in range(4)
        for x in range(4)
        for z in range(4)
        for c in range(2)
    ]


CORE = permutation(lambda y, x, z, c: (y, x, z, c + 1))
HIGH = permutation(lambda y, x, z, c: (y, x + 2, z, c))
LOW = permutation(lambda y, x, z, c: (y, x ^ 1, z, c))
Y_NEAR = permutation(lambda y, x, z, c: (y ^ 1, x, z, c))
Y_FAR = permutation(lambda y, x, z, c: (y + 2, x, z, c))
YS = [permutation(lambda y, x, z, c, d=d: (y + d, x, z, c)) for d in range(4)]
XS = [permutation(lambda y, x, z, c, d=d: (y, x + d, z, c)) for d in range(4)]
ZS = [permutation(lambda y, x, z, c, d=d: (y, x, z + d, c)) for d in range(4)]


def move(value, pairs):
    return lax.ppermute(value, AXES, pairs)


def after(values, *others):
    return lax.optimization_barrier((*values, *others))[: len(values)]


def join(own, other, upper):
    lower = upper == 0
    return jnp.stack([jnp.where(lower, own, other), jnp.where(lower, other, own)])


def per_device(particles, references, owner, class_offset, rotation, shifts, ctf_group, ctf_table):
    fwd_np, inv_np = tables()
    fwd_k, inv_k = jnp.asarray(fwd_np), jnp.asarray(inv_np)
    fx, fy = (jnp.asarray(t) for t in freq_tables())
    dom, cls = lax.axis_index("dom"), lax.axis_index("cls")
    y, xh, core = dom // 4, dom // 2 % 2, dom % 2
    xl, z = cls // 4, cls % 4
    sc = jnp.stack([y, xh * 2 + xl, core, z]).astype(jnp.int32)

    low, high = references[0:16], references[9:25]
    first = core == 0
    keep = jnp.where(first, low, high)
    give = jnp.where(first, high, low)
    got = move(give, CORE)
    block = jnp.where(
        first, jnp.concatenate([keep, got], axis=1), jnp.concatenate([got, keep], axis=1)
    )
    rows = [shifts.T, rotation[None], owner.T, class_offset[None], ctf_group[None]]
    table = ctf_table.T
    block, rows[1] = lax.optimization_barrier((block, rows[1]))
    half = prep(particles, rows, table, fx, fy, 0)
    far = move(block, HIGH)
    far, *half = lax.optimization_barrier((far, *half))
    pair = join(block, far, xh)
    pair, rows[1] = lax.optimization_barrier((pair, rows[1]))
    weighted, *sent = prep(particles, rows, table, fx, fy, 2, half)
    near = move(pair, Y_NEAR)
    near, weighted, *sent = lax.optimization_barrier((near, weighted, *sent))
    quad = join(pair, near, y % 2)
    opposite = move(quad, Y_FAR)

    across = move(sent[2], YS[2])
    part = spectra(weighted, fwd_k)
    own = ref_spectra(quad, opposite, fwd_k)
    up, down = move(own, ZS[1]), move(own, ZS[3])
    side = move(own, LOW)
    side_up, side_down = move(side, ZS[1]), move(side, ZS[3])
    one, three = after([sent[1], sent[3]], across, part, up, down)
    held = [sent[0], move(one, YS[1]), across, move(three, YS[3])]
    on_up, on_down = move(up, ZS[1]), move(side_down, ZS[3])
    early = jnp.stack([own, side, up, down])
    early_twin = move(early, CORE)
    held = after(held, side_up, side_down)
    mine, other = class_sums(sc, held, table)
    cut = cut_x(sc, mine, move(other, CORE))
    late = jnp.stack([side_up, side_down, on_up, on_down])
    late_twin = move(late, CORE)
    cut = [cut[0]] + [move(cut[d], XS[d]) for d in (1, 2, 3)]
    scores = scores_of(part, [early, early_twin, late, late_twin], inv_k)
    *cut, scores = lax.optimization_barrier((*cut, scores))
    cut = cut_z(sc, cut)
    cut = [cut[0]] + [move(cut[d], ZS[d]) for d in (1, 2, 3)]
    return scores[0], final(sc, cut)


def solution(mesh):
    return jax.shard_map(
        per_device,
        mesh=mesh,
        in_specs=(
            P(("dom", "cls"), None),
            P("cls", "dom"),
            P(("dom", "cls"), None),
            P(("dom", "cls")),
            P(("dom", "cls")),
            P(("dom", "cls"), None),
            P(("dom", "cls")),
            P(),
        ),
        out_specs=(P(("dom", "cls")), P("cls", "dom")),
        check_vma=False,
    )
```

```python
import functools

import jax
import jax.numpy as jnp
import numpy as np
from jax import lax
from jax.experimental import pallas as pl
from jax.experimental.pallas import tpu as pltpu
from jax.sharding import PartitionSpec as P

A = 72
M = 37
R = 64
BOX = 128
TAU = 1.0
AXES = ("dom", "cls")
BF = jnp.bfloat16
F32 = jnp.float32
MIB = 1024 * 1024
VMEM_LIMIT = 8 * MIB
PREP_MIB = 56
K_INV = 640


def tables():
    m = np.arange(M)[:, None]
    a = np.arange(A)[None, :]
    turn = 2.0 * np.pi * ((m * a) % A) / A
    fwd = np.stack([np.cos(turn), -np.sin(turn)], axis=1).reshape(2 * M, A)
    gain = np.where((np.arange(M) == 0) | (np.arange(M) == A // 2), 1.0, 2.0)[:, None]
    inv = np.stack([np.cos(turn) / A, -np.sin(turn) / A], axis=1).astype(BF).astype(np.float32)
    inv = (inv * gain[:, None, :]).reshape(2 * M, A).T
    eye = np.eye(8, dtype=np.float32)
    fwd_k = np.kron(fwd.astype(np.float32), eye).astype(BF)
    inv_k = np.zeros((A * 8, K_INV), np.float32)
    inv_k[:, : 2 * M * 8] = np.kron(inv, eye)
    return fwd_k, inv_k.astype(BF)


def freq_tables():
    angle = 2.0 * np.pi * np.arange(A // 2) / A
    radius = np.tile(np.arange(1, R + 1), 2)
    fx = np.cos(angle)[:, None] * radius[None, :] / BOX
    fy = np.sin(angle)[:, None] * radius[None, :] / BOX
    return fx.astype(np.float32), fy.astype(np.float32)


def cos_poly():
    n = 7
    nodes = (np.cos((np.arange(64) + 0.5) * np.pi / 64) + 1.0) / 8.0
    return [float(c) for c in np.polynomial.chebyshev.Chebyshev.fit(
        nodes, np.cos(2.0 * np.pi * np.sqrt(nodes)), n - 1, domain=[0.0, 0.25]
    ).convert(kind=np.polynomial.Polynomial).coef]


COEF = cos_poly()


def prep_kernel(first, x_ref, shift_ref, rot_ref, own_ref, off_ref, grp_ref, tab_ref, fx_ref, fy_ref, *refs):
    w_ref, c0, c1, c2, c3, ws, us, aux, tab = refs[-9:]
    dom, cls = lax.axis_index("dom"), lax.axis_index("cls")
    mine = 2 * (dom * 8 + cls)
    step = pl.program_id(0)

    @pl.when(step == 0)
    def _():
        shift_rows = shift_ref[...].astype(F32)
        group = grp_ref[...]
        rows = [
            shift_rows,
            rot_ref[...].astype(F32),
            (group - mine).astype(F32),
            (own_ref[...] * 32 + off_ref[...]).astype(F32),
            group.astype(F32),
            jnp.zeros((122, 128), F32),
        ]
        aux[...] = jnp.concatenate(rows, axis=0).T
        flipped = tab_ref[...].T
        tab[...] = jnp.concatenate([flipped, flipped], axis=1)

    @pl.loop(0, 2)
    def _(half):
        span = pl.ds(pl.multiple_of(half * 16, 16), 16)
        here = aux[pl.ds(pl.multiple_of((2 * (step + first) + half) * 16, 16), 16), :]
        lane = lax.broadcasted_iota(jnp.int32, (16, 128), 1)
        left = lane < R
        shift = jnp.where(left, 0.0, -0.25).astype(F32)
        sxb = jnp.broadcast_to(here[:, 0:1], (16, 128))
        syb = jnp.broadcast_to(here[:, 1:2], (16, 128))
        ctf = jnp.where(here[:, 3:4] > 0.5, tab[pl.ds(mine + 1, 1), :], tab[pl.ds(mine, 1), :])
        ctf_s = jnp.where(left, -ctf, ctf)
        for b in range(A // 4):
            done = []
            for a in (2 * b, 2 * b + 1):
                v = (sxb * fx_ref[a : a + 1, :] + syb * fy_ref[a : a + 1, :]) + shift
                v = v - jnp.round(v)
                q = v * v
                e = jnp.full_like(q, COEF[-1])
                for k in COEF[-2::-1]:
                    e = e * q + k
                er = pltpu.roll(e, R, 1)
                cc = jnp.where(left, e, er) * ctf
                ss = jnp.where(left, er, e) * ctf_s
                x0 = x_ref[span, a * 128 : (a + 1) * 128].astype(F32)
                h = a + A // 2
                x1 = x_ref[span, h * 128 : (h + 1) * 128].astype(F32)
                w0 = x0 * cc + pltpu.roll(x0, R, 1) * ss
                w1 = x1 * cc - pltpu.roll(x1, R, 1) * ss
                ws[:, a * 128 : (a + 1) * 128] = w0
                ws[:, h * 128 : (h + 1) * 128] = w1
                done.append((w0, w1))
            for turn in (0, 1):
                row = (2 * b + turn * (A // 2)) * 8
                for g in (0, 1):
                    w_ref[2 * half + g, row : row + 16, :] = jnp.concatenate(
                        [done[0][turn][8 * g : 8 * g + 8], done[1][turn][8 * g : 8 * g + 8]], axis=0
                    ).astype(BF)
        rotb = jnp.broadcast_to(here[:, 2:3], (16, 128)).astype(jnp.int32)
        bit = [(rotb & (1 << k)) != 0 for k in range(7)]
        for r in range(8):
            t = [ws[:, (r + 8 * n) * 128 : (r + 8 * n + 1) * 128] for n in range(9)]
            for k in range(4):
                t = [jnp.where(bit[3 + k], t[(n + (1 << k)) % 9], t[n]) for n in range(9)]
            for n in range(9):
                us[:, (r + 8 * n) * 128 : (r + 8 * n + 1) * 128] = t[n]
        for j0 in range(0, A, 8):
            t = [us[:, ((j0 + i) % A) * 128 : ((j0 + i) % A + 1) * 128] for i in range(15)]
            t = [jnp.where(bit[0], t[i + 1], t[i]) for i in range(14)]
            t = [jnp.where(bit[1], t[i + 2], t[i]) for i in range(12)]
            for i in range(8):
                ws[:, (j0 + i) * 128 : (j0 + i + 1) * 128] = jnp.where(bit[2], t[i + 4], t[i])
        meta = jnp.where(lane == 0, here[:, 4:5], jnp.where(lane == 1, here[:, 5:6], 0.0)).astype(BF)
        width = 18 * 128
        for dy, c_ref in enumerate((c0, c1, c2, c3)):
            dest = lax.rem(dom // 4 + dy, 4)
            start = pl.multiple_of(dest * width, 128)
            c_ref[span, 0:width] = ws[:, pl.ds(start, width)].astype(BF)
            c_ref[span, width : width + 128] = meta


def prep(particles, rows, table, fx, fy, first, held=()):
    n = particles.shape[0]
    whole = lambda a: pl.BlockSpec(a.shape, lambda i: (0,) * a.ndim)
    block = lambda i: (i + first, 0)
    args = [particles, *rows, table, fx, fy]
    given = len(args)
    return pl.pallas_call(
        functools.partial(prep_kernel, first),
        grid=(n // 64,),
        in_specs=[pl.BlockSpec((32, A * 128), block)]
        + [whole(a) for a in args[1:]]
        + [pl.BlockSpec(memory_space=pltpu.HBM)] * len(held),
        out_specs=[pl.BlockSpec((4, A * 8, 128), lambda i: (i + first, 0, 0))]
        + [pl.BlockSpec((32, 19 * 128), block)] * 4,
        scratch_shapes=[
            pltpu.VMEM((16, A * 128), F32),
            pltpu.VMEM((16, A * 128), F32),
            pltpu.VMEM((128, 128), F32),
            pltpu.VMEM((256, 128), F32),
        ],
        out_shape=[jax.ShapeDtypeStruct((n // 8, A * 8, 128), BF)]
        + [jax.ShapeDtypeStruct((n, 19 * 128), BF)] * 4,
        input_output_aliases={given + i: i for i in range(len(held))},
        compiler_params=pltpu.CompilerParams(vmem_limit_bytes=PREP_MIB * MIB),
        cost_estimate=pl.CostEstimate(
            flops=20_000_000, bytes_accessed=4_000_000, transcendentals=0
        ),
        name="prep",
    )(*args, *held)


def repeat(step):
    @pl.loop(0, M // 4)
    def _(i):
        for u in range(4):
            step(4 * i + u)

    step(M - 1)


def spectra_kernel(w_ref, f_ref, p_ref, s):
    for g in range(8):
        y = jnp.concatenate([w_ref[2 * g], w_ref[2 * g + 1]], axis=1)
        s[:, 256 * g : 256 * g + 256] = jnp.dot(f_ref[...], y, preferred_element_type=F32)

    def turn(m):
        for i in range(2):
            row = pl.multiple_of(m * 16 + 8 * i, 8)
            v = jnp.concatenate([s[pl.ds(row, 8), 128 * g : 128 * g + 128] for g in range(16)], axis=0)
            p_ref[m, :, 128 * i : 128 * i + 128] = v.T.astype(BF)

    repeat(turn)


def spectra(w, fwd_k):
    v = pl.BlockSpec(memory_space=pltpu.VMEM)
    return pl.pallas_call(
        spectra_kernel,
        in_specs=[v, v],
        out_specs=v,
        out_shape=jax.ShapeDtypeStruct((M, 128, 256), BF),
        scratch_shapes=[pltpu.VMEM((2 * M * 8, 2048), F32)],
        compiler_params=pltpu.CompilerParams(vmem_limit_bytes=16 * MIB),
        cost_estimate=pl.CostEstimate(flops=1000, bytes_accessed=1000, transcendentals=0),
        name="spectra",
    )(w, fwd_k)


def ref_kernel(own_ref, far_ref, f_ref, r_ref, s):
    upper = lax.rem(lax.axis_index("dom") // 8, 2)
    for ref, place_of in ((own_ref, upper), (far_ref, 1 - upper)):
        for y in range(2):
            for xh in range(2):
                for t in range(9):
                    v = ref[y, xh, :, t * 128 : (t + 1) * 128].astype(F32)
                    row = pl.multiple_of(place_of * 288 + (y * 2 + xh) * 72 + 8 * t, 8)
                    s[pl.ds(row, 8), 0:128] = v[0:8]
                    s[pl.ds(row, 8), 128:256] = v[8:16]
    out = jnp.dot(f_ref[...], s[...].astype(BF), preferred_element_type=F32)
    for m in range(M):
        for i in range(2):
            r = 16 * m + 8 * i
            r_ref[m, :, 128 * i : 128 * i + 128] = jnp.concatenate(
                [out[r : r + 8, 0:128], out[r : r + 8, 128:256]], axis=0
            ).astype(BF)


def ref_spectra(own, far, fwd_k):
    v = pl.BlockSpec(memory_space=pltpu.VMEM)
    return pl.pallas_call(
        ref_kernel,
        in_specs=[v, v, v],
        out_specs=v,
        out_shape=jax.ShapeDtypeStruct((M, 16, 256), BF),
        scratch_shapes=[pltpu.VMEM((A * 8, 256), F32)],
        compiler_params=pltpu.CompilerParams(vmem_limit_bytes=8 * MIB),
        cost_estimate=pl.CostEstimate(flops=1000, bytes_accessed=1000, transcendentals=0),
        name="ref_spectra",
    )(own, far, fwd_k)


def score_kernel(*refs):
    p_ref, blocks, inv_ref, o_ref, xs = refs[0], refs[1:5], refs[5], refs[6], refs[7]
    xs[:, 2 * M * 8 :, :] = jnp.zeros((16, K_INV - 2 * M * 8, 256), BF)

    def cross(m):
        upper = p_ref[m]
        re, im = upper[:, 0:128], upper[:, 128:256]
        rhs = jnp.concatenate([upper, jnp.concatenate([im, -re], axis=1)], axis=0)
        lhs = jnp.concatenate([b[i, m] for b in blocks for i in range(4)], axis=0)
        x = jnp.dot(lhs, rhs, preferred_element_type=F32)
        row = pl.multiple_of(m * 16, 16)
        for g in range(16):
            for h in range(2):
                k = 16 * g + 8 * h
                xs[g, pl.ds(row, 16), 128 * h : 128 * h + 128] = jnp.concatenate(
                    [x[k : k + 8, 0:128], x[k : k + 8, 128:256]], axis=0
                ).astype(BF)

    repeat(cross)

    def four(i, best):
        for u in range(4):
            y = jnp.dot(inv_ref[...], xs[4 * i + u], preferred_element_type=F32)
            for t in range(A):
                best = jnp.maximum(best, y[8 * t : 8 * t + 8])
        return best

    best = lax.fori_loop(0, 4, four, jnp.full((8, 256), -jnp.inf, F32))
    best = jnp.max(best, axis=0, keepdims=True)
    o_ref[...] = jnp.maximum(best[:, 0:128], best[:, 128:256])


def scores_of(p, blocks, inv_k):
    v = pl.BlockSpec(memory_space=pltpu.VMEM)
    return pl.pallas_call(
        score_kernel,
        in_specs=[v] * 6,
        out_specs=v,
        out_shape=jax.ShapeDtypeStruct((1, 128), F32),
        scratch_shapes=[pltpu.VMEM((16, K_INV, 256), BF)],
        compiler_params=pltpu.CompilerParams(vmem_limit_bytes=20 * MIB),
        cost_estimate=pl.CostEstimate(flops=6_000_000_000, bytes_accessed=8_000_000, transcendentals=0),
        name="scores",
    )(p, *blocks, inv_k)


def sums_kernel(sc, c0, c1, c2, c3, tab_ref, mine, other, acc):
    width = 18 * 128
    lane = lax.broadcasted_iota(jnp.int32, (128, 256), 1).astype(F32)
    picks, groups = [], []
    for c in (c0, c1, c2, c3):
        meta = c[:, width : width + 128].astype(F32)
        picks.append(jnp.where(lane == meta[:, 0:1], 1.0, 0.0).astype(F32).T.astype(BF))
        groups.append(jnp.where(lane == meta[:, 1:2], 1.0, 0.0).astype(BF))
    pick = jnp.concatenate(picks, axis=1)
    group = jnp.concatenate(groups, axis=0)
    count = jnp.dot(pick, group, preferred_element_type=F32)
    flipped = tab_ref[...].T
    tab = jnp.concatenate([flipped, flipped], axis=1)
    wsum = jnp.dot(count, tab * tab, precision=lax.Precision.HIGHEST, preferred_element_type=F32)
    for t in range(9):
        cols = slice(256 * t, 256 * t + 256)
        x = jnp.concatenate([c[:, cols] for c in (c0, c1, c2, c3)], axis=0)
        acc[:, cols] = jnp.dot(pick, x, preferred_element_type=F32)
    left = lax.broadcasted_iota(jnp.int32, (256, 128), 1) < R
    for ref, core in ((mine, sc[2]), (other, 1 - sc[2])):
        for xh in range(2):
            start = pl.multiple_of((9 * xh + 4 * core) * 128, 128)
            ref[xh] = acc[:, pl.ds(start, 640)]
            mid = acc[:, (9 * xh + 4) * 128 : (9 * xh + 5) * 128]
            keep = jnp.logical_xor(left, core == 1)
            ref[xh, :, pl.ds(pl.multiple_of((1 - core) * 512, 128), 128)] = jnp.where(keep, mid, wsum)


def class_sums(sc, cs, tab):
    v = pl.BlockSpec(memory_space=pltpu.VMEM)
    shape = jax.ShapeDtypeStruct((2, 256, 640), F32)
    return pl.pallas_call(
        sums_kernel,
        in_specs=[pl.BlockSpec(memory_space=pltpu.SMEM)] + [v] * 5,
        out_specs=[v, v],
        out_shape=[shape, shape],
        scratch_shapes=[pltpu.VMEM((256, 18 * 128), F32)],
        compiler_params=pltpu.CompilerParams(vmem_limit_bytes=VMEM_LIMIT),
        cost_estimate=pl.CostEstimate(flops=700_000_000, bytes_accessed=5_000_000, transcendentals=0),
        name="class_sums",
    )(sc, *cs, tab)


def cut_x_kernel(sc, a_ref, b_ref, o0, o1, o2, o3):
    for dx, o in enumerate((o0, o1, o2, o3)):
        x = lax.rem(sc[1] + dx, 4)
        xh, xl = x // 2, lax.rem(x, 2)
        rows = pl.ds(pl.multiple_of(xl * 128, 128), 128)
        o[...] = (a_ref[xh, rows, :] + b_ref[xh, rows, :]).astype(o.dtype)


def cut_x(sc, a, b):
    v = pl.BlockSpec(memory_space=pltpu.VMEM)
    return pl.pallas_call(
        cut_x_kernel,
        in_specs=[pl.BlockSpec(memory_space=pltpu.SMEM), v, v],
        out_specs=[v] * 4,
        out_shape=[jax.ShapeDtypeStruct((128, 640), F32)] + [jax.ShapeDtypeStruct((128, 640), BF)] * 3,
        compiler_params=pltpu.CompilerParams(vmem_limit_bytes=VMEM_LIMIT),
        cost_estimate=pl.CostEstimate(flops=400_000, bytes_accessed=3_900_000, transcendentals=0),
        name="cut_x",
    )(sc, a, b)


def cut_z_kernel(sc, a0, a1, a2, a3, o0, o1, o2, o3):
    for dz, o in enumerate((o0, o1, o2, o3)):
        z = lax.rem(sc[3] + dz, 4)
        rows = pl.ds(pl.multiple_of(z * 32, 32), 32)
        far = a1[rows, :].astype(F32) + a2[rows, :].astype(F32) + a3[rows, :].astype(F32)
        o[...] = (a0[rows, :] + far).astype(o.dtype)


def cut_z(sc, parts):
    v = pl.BlockSpec(memory_space=pltpu.VMEM)
    return pl.pallas_call(
        cut_z_kernel,
        in_specs=[pl.BlockSpec(memory_space=pltpu.SMEM)] + [v] * 4,
        out_specs=[v] * 4,
        out_shape=[jax.ShapeDtypeStruct((32, 640), F32)] + [jax.ShapeDtypeStruct((32, 640), BF)] * 3,
        compiler_params=pltpu.CompilerParams(vmem_limit_bytes=VMEM_LIMIT),
        cost_estimate=pl.CostEstimate(flops=400_000, bytes_accessed=1_700_000, transcendentals=0),
        name="cut_z",
    )(sc, *parts)


def final_kernel(sc, a0, a1, a2, a3, o_ref):
    s = a0[...] + (a1[...].astype(F32) + a2[...].astype(F32) + a3[...].astype(F32))
    odd = sc[2] == 1
    left = lax.broadcasted_iota(jnp.int32, (32, 128), 1) < R
    tile = [s[:, 128 * t : 128 * t + 128] for t in range(5)]
    held = jnp.where(odd, tile[0], tile[4])
    turned = pltpu.roll(held, R, 1)
    weight = jnp.where(jnp.logical_xor(left, odd), turned, held)
    tile = [t / (weight + TAU) for t in tile]
    rolled = [pltpu.roll(t, R, 1) for t in tile]
    later = [jnp.where(left, rolled[t], rolled[t + 1]) for t in range(4)] + [rolled[4]]
    for t in range(4):
        o_ref[:, 128 * t : 128 * t + 128] = jnp.where(odd, later[t], tile[t])[0:25]
    o_ref[:, 512:576] = jnp.where(odd, later[4], tile[4])[0:25, 0:R]


def final(sc, parts):
    v = pl.BlockSpec(memory_space=pltpu.VMEM)
    return pl.pallas_call(
        final_kernel,
        in_specs=[pl.BlockSpec(memory_space=pltpu.SMEM)] + [v] * 4,
        out_specs=v,
        out_shape=jax.ShapeDtypeStruct((25, 576), F32),
        compiler_params=pltpu.CompilerParams(vmem_limit_bytes=2 * MIB),
        name="final",
    )(sc, *parts)


def place(y, x, z, core):
    return ((y % 4) * 4 + (x % 4) // 2 * 2 + core % 2) * 8 + (x % 2) * 4 + z % 4


def permutation(move):
    return [
        (place(y, x, z, c), place(*move(y, x, z, c)))
        for y in range(4)
        for x in range(4)
        for z in range(4)
        for c in range(2)
    ]


CORE = permutation(lambda y, x, z, c: (y, x, z, c + 1))
HIGH = permutation(lambda y, x, z, c: (y, x + 2, z, c))
LOW = permutation(lambda y, x, z, c: (y, x ^ 1, z, c))
Y_NEAR = permutation(lambda y, x, z, c: (y ^ 1, x, z, c))
Y_FAR = permutation(lambda y, x, z, c: (y + 2, x, z, c))
YS = [permutation(lambda y, x, z, c, d=d: (y + d, x, z, c)) for d in range(4)]
XS = [permutation(lambda y, x, z, c, d=d: (y, x + d, z, c)) for d in range(4)]
ZS = [permutation(lambda y, x, z, c, d=d: (y, x, z + d, c)) for d in range(4)]


def move(value, pairs):
    return lax.ppermute(value, AXES, pairs)


def after(values, *others):
    return lax.optimization_barrier((*values, *others))[: len(values)]


def join(own, other, upper):
    lower = upper == 0
    return jnp.stack([jnp.where(lower, own, other), jnp.where(lower, other, own)])


def per_device(particles, references, owner, class_offset, rotation, shifts, ctf_group, ctf_table):
    fwd_np, inv_np = tables()
    fwd_k, inv_k = jnp.asarray(fwd_np), jnp.asarray(inv_np)
    fx, fy = (jnp.asarray(t) for t in freq_tables())
    dom, cls = lax.axis_index("dom"), lax.axis_index("cls")
    y, xh, core = dom // 4, dom // 2 % 2, dom % 2
    xl, z = cls // 4, cls % 4
    sc = jnp.stack([y, xh * 2 + xl, core, z]).astype(jnp.int32)

    low, high = references[0:16], references[9:25]
    first = core == 0
    keep = jnp.where(first, low, high)
    give = jnp.where(first, high, low)
    got = move(give, CORE)
    block = jnp.where(
        first, jnp.concatenate([keep, got], axis=1), jnp.concatenate([got, keep], axis=1)
    )
    rows = [shifts.T, rotation[None], owner.T, class_offset[None], ctf_group[None]]
    table = ctf_table.T
    block, rows[1] = lax.optimization_barrier((block, rows[1]))
    half = prep(particles, rows, table, fx, fy, 0)
    far = move(block, HIGH)
    far, *half = lax.optimization_barrier((far, *half))
    pair = join(block, far, xh)
    pair, rows[1] = lax.optimization_barrier((pair, rows[1]))
    weighted, *sent = prep(particles, rows, table, fx, fy, 2, half)
    near = move(pair, Y_NEAR)
    near, weighted, *sent = lax.optimization_barrier((near, weighted, *sent))
    quad = join(pair, near, y % 2)
    opposite = move(quad, Y_FAR)

    across = move(sent[2], YS[2])
    part = spectra(weighted, fwd_k)
    own = ref_spectra(quad, opposite, fwd_k)
    up, down = move(own, ZS[1]), move(own, ZS[3])
    side = move(own, LOW)
    side_up, side_down = move(side, ZS[1]), move(side, ZS[3])
    one, three = after([sent[1], sent[3]], part, up, down)
    held = [sent[0], move(one, YS[1]), across, move(three, YS[3])]
    on_up, on_down = move(up, ZS[1]), move(side_down, ZS[3])
    early = jnp.stack([own, side, up, down])
    early_twin = move(early, CORE)
    held = after(held, side_up, side_down)
    mine, other = class_sums(sc, held, table)
    cut = cut_x(sc, mine, move(other, CORE))
    late = jnp.stack([side_up, side_down, on_up, on_down])
    late_twin = move(late, CORE)
    cut = [cut[0]] + [move(cut[d], XS[d]) for d in (1, 2, 3)]
    scores = scores_of(part, [early, early_twin, late, late_twin], inv_k)
    *cut, scores = lax.optimization_barrier((*cut, scores))
    cut = cut_z(sc, cut)
    cut = [cut[0]] + [move(cut[d], ZS[d]) for d in (1, 2, 3)]
    return scores[0], final(sc, cut)


def solution(mesh):
    return jax.shard_map(
        per_device,
        mesh=mesh,
        in_specs=(
            P(("dom", "cls"), None),
            P("cls", "dom"),
            P(("dom", "cls"), None),
            P(("dom", "cls")),
            P(("dom", "cls")),
            P(("dom", "cls"), None),
            P(("dom", "cls")),
            P(),
        ),
        out_specs=(P(("dom", "cls")), P("cls", "dom")),
        check_vma=False,
    )
```

```python
import functools

import jax
import jax.numpy as jnp
import numpy as np
from jax import lax
from jax.experimental import pallas as pl
from jax.experimental.pallas import tpu as pltpu
from jax.sharding import PartitionSpec as P

A = 72
M = 37
R = 64
BOX = 128
TAU = 1.0
AXES = ("dom", "cls")
BF = jnp.bfloat16
F32 = jnp.float32
MIB = 1024 * 1024
VMEM_LIMIT = 8 * MIB
PREP_MIB = 56
K_INV = 640


def tables():
    m = np.arange(M)[:, None]
    a = np.arange(A)[None, :]
    turn = 2.0 * np.pi * ((m * a) % A) / A
    fwd = np.stack([np.cos(turn), -np.sin(turn)], axis=1).reshape(2 * M, A)
    gain = np.where((np.arange(M) == 0) | (np.arange(M) == A // 2), 1.0, 2.0)[:, None]
    inv = np.stack([np.cos(turn) / A, -np.sin(turn) / A], axis=1).astype(BF).astype(np.float32)
    inv = (inv * gain[:, None, :]).reshape(2 * M, A).T
    eye = np.eye(8, dtype=np.float32)
    fwd_k = np.kron(fwd.astype(np.float32), eye).astype(BF)
    inv_k = np.zeros((A * 8, K_INV), np.float32)
    inv_k[:, : 2 * M * 8] = np.kron(inv, eye)
    return fwd_k, inv_k.astype(BF)


def freq_tables():
    angle = 2.0 * np.pi * np.arange(A // 2) / A
    radius = np.tile(np.arange(1, R + 1), 2)
    fx = np.cos(angle)[:, None] * radius[None, :] / BOX
    fy = np.sin(angle)[:, None] * radius[None, :] / BOX
    return fx.astype(np.float32), fy.astype(np.float32)


def cos_poly():
    n = 7
    nodes = (np.cos((np.arange(64) + 0.5) * np.pi / 64) + 1.0) / 8.0
    return [float(c) for c in np.polynomial.chebyshev.Chebyshev.fit(
        nodes, np.cos(2.0 * np.pi * np.sqrt(nodes)), n - 1, domain=[0.0, 0.25]
    ).convert(kind=np.polynomial.Polynomial).coef]


COEF = cos_poly()


def prep_kernel(first, x_ref, shift_ref, rot_ref, own_ref, off_ref, grp_ref, tab_ref, fx_ref, fy_ref, *refs):
    w_ref, c0, c1, c2, c3, ws, us, aux, tab = refs[-9:]
    dom, cls = lax.axis_index("dom"), lax.axis_index("cls")
    mine = 2 * (dom * 8 + cls)
    step = pl.program_id(0)

    @pl.when(step == 0)
    def _():
        shift_rows = shift_ref[...].astype(F32)
        group = grp_ref[...]
        rows = [
            shift_rows,
            rot_ref[...].astype(F32),
            (group - mine).astype(F32),
            (own_ref[...] * 32 + off_ref[...]).astype(F32),
            group.astype(F32),
            jnp.zeros((122, 128), F32),
        ]
        aux[...] = jnp.concatenate(rows, axis=0).T
        flipped = tab_ref[...].T
        tab[...] = jnp.concatenate([flipped, flipped], axis=1)

    here = aux[pl.ds(pl.multiple_of((step + first) * 16, 16), 16), :]
    lane = lax.broadcasted_iota(jnp.int32, (16, 128), 1)
    left = lane < R
    shift = jnp.where(left, 0.0, -0.25).astype(F32)
    sxb = jnp.broadcast_to(here[:, 0:1], (16, 128))
    syb = jnp.broadcast_to(here[:, 1:2], (16, 128))
    ctf = jnp.where(here[:, 3:4] > 0.5, tab[pl.ds(mine + 1, 1), :], tab[pl.ds(mine, 1), :])
    ctf_s = jnp.where(left, -ctf, ctf)
    for b in range(A // 4):
        done = []
        for a in (2 * b, 2 * b + 1):
            v = (sxb * fx_ref[a : a + 1, :] + syb * fy_ref[a : a + 1, :]) + shift
            v = v - jnp.round(v)
            q = v * v
            e = jnp.full_like(q, COEF[-1])
            for k in COEF[-2::-1]:
                e = e * q + k
            er = pltpu.roll(e, R, 1)
            cc = jnp.where(left, e, er) * ctf
            ss = jnp.where(left, er, e) * ctf_s
            x0 = x_ref[:, a * 128 : (a + 1) * 128].astype(F32)
            h = a + A // 2
            x1 = x_ref[:, h * 128 : (h + 1) * 128].astype(F32)
            w0 = x0 * cc + pltpu.roll(x0, R, 1) * ss
            w1 = x1 * cc - pltpu.roll(x1, R, 1) * ss
            ws[:, a * 128 : (a + 1) * 128] = w0
            ws[:, h * 128 : (h + 1) * 128] = w1
            done.append((w0, w1))
        for half in (0, 1):
            row = (2 * b + half * (A // 2)) * 8
            for g in (0, 1):
                w_ref[g, row : row + 16, :] = jnp.concatenate(
                    [done[0][half][8 * g : 8 * g + 8], done[1][half][8 * g : 8 * g + 8]], axis=0
                ).astype(BF)
    rotb = jnp.broadcast_to(here[:, 2:3], (16, 128)).astype(jnp.int32)
    bit = [(rotb & (1 << k)) != 0 for k in range(7)]
    for r in range(8):
        t = [ws[:, (r + 8 * n) * 128 : (r + 8 * n + 1) * 128] for n in range(9)]
        for k in range(4):
            t = [jnp.where(bit[3 + k], t[(n + (1 << k)) % 9], t[n]) for n in range(9)]
        for n in range(9):
            us[:, (r + 8 * n) * 128 : (r + 8 * n + 1) * 128] = t[n]
    for j0 in range(0, A, 8):
        t = [us[:, ((j0 + i) % A) * 128 : ((j0 + i) % A + 1) * 128] for i in range(15)]
        t = [jnp.where(bit[0], t[i + 1], t[i]) for i in range(14)]
        t = [jnp.where(bit[1], t[i + 2], t[i]) for i in range(12)]
        for i in range(8):
            ws[:, (j0 + i) * 128 : (j0 + i + 1) * 128] = jnp.where(bit[2], t[i + 4], t[i])
    meta = jnp.where(lane == 0, here[:, 4:5], jnp.where(lane == 1, here[:, 5:6], 0.0)).astype(BF)
    width = 18 * 128
    for dy, c_ref in enumerate((c0, c1, c2, c3)):
        dest = lax.rem(dom // 4 + dy, 4)
        start = pl.multiple_of(dest * width, 128)
        c_ref[:, 0:width] = ws[:, pl.ds(start, width)].astype(BF)
        c_ref[:, width : width + 128] = meta


def prep(particles, rows, table, fx, fy, first, held=()):
    n = particles.shape[0]
    whole = lambda a: pl.BlockSpec(a.shape, lambda i: (0,) * a.ndim)
    block = lambda i: (i + first, 0)
    args = [particles, *rows, table, fx, fy]
    given = len(args)
    return pl.pallas_call(
        functools.partial(prep_kernel, first),
        grid=(n // 32,),
        in_specs=[pl.BlockSpec((16, A * 128), block)]
        + [whole(a) for a in args[1:]]
        + [pl.BlockSpec(memory_space=pltpu.HBM)] * len(held),
        out_specs=[pl.BlockSpec((2, A * 8, 128), lambda i: (i + first, 0, 0))]
        + [pl.BlockSpec((16, 19 * 128), block)] * 4,
        scratch_shapes=[
            pltpu.VMEM((16, A * 128), F32),
            pltpu.VMEM((16, A * 128), F32),
            pltpu.VMEM((128, 128), F32),
            pltpu.VMEM((256, 128), F32),
        ],
        out_shape=[jax.ShapeDtypeStruct((n // 8, A * 8, 128), BF)]
        + [jax.ShapeDtypeStruct((n, 19 * 128), BF)] * 4,
        input_output_aliases={given + i: i for i in range(len(held))},
        compiler_params=pltpu.CompilerParams(vmem_limit_bytes=PREP_MIB * MIB),
        cost_estimate=pl.CostEstimate(
            flops=20_000_000, bytes_accessed=4_000_000, transcendentals=0
        ),
        name="prep",
    )(*args, *held)


def repeat(step):
    @pl.loop(0, M // 4)
    def _(i):
        for u in range(4):
            step(4 * i + u)

    step(M - 1)


def spectra_kernel(w_ref, f_ref, p_ref, s):
    for g in range(8):
        y = jnp.concatenate([w_ref[2 * g], w_ref[2 * g + 1]], axis=1)
        s[:, 256 * g : 256 * g + 256] = jnp.dot(f_ref[...], y, preferred_element_type=F32)

    def turn(m):
        for i in range(2):
            row = pl.multiple_of(m * 16 + 8 * i, 8)
            v = jnp.concatenate([s[pl.ds(row, 8), 128 * g : 128 * g + 128] for g in range(16)], axis=0)
            p_ref[m, :, 128 * i : 128 * i + 128] = v.T.astype(BF)

    repeat(turn)


def spectra(w, fwd_k):
    v = pl.BlockSpec(memory_space=pltpu.VMEM)
    return pl.pallas_call(
        spectra_kernel,
        in_specs=[v, v],
        out_specs=v,
        out_shape=jax.ShapeDtypeStruct((M, 128, 256), BF),
        scratch_shapes=[pltpu.VMEM((2 * M * 8, 2048), F32)],
        compiler_params=pltpu.CompilerParams(vmem_limit_bytes=16 * MIB),
        cost_estimate=pl.CostEstimate(flops=1000, bytes_accessed=1000, transcendentals=0),
        name="spectra",
    )(w, fwd_k)


def ref_kernel(b_ref, f_ref, r_ref, s):
    for y in range(4):
        for xh in range(2):
            for t in range(9):
                v = b_ref[y, xh, :, t * 128 : (t + 1) * 128].astype(F32)
                row = (y * 2 + xh) * 72 + 8 * t
                s[row : row + 8, 0:128] = v[0:8]
                s[row : row + 8, 128:256] = v[8:16]
    out = jnp.dot(f_ref[...], s[...].astype(BF), preferred_element_type=F32)
    for m in range(M):
        for i in range(2):
            r = 16 * m + 8 * i
            r_ref[m, :, 128 * i : 128 * i + 128] = jnp.concatenate(
                [out[r : r + 8, 0:128], out[r : r + 8, 128:256]], axis=0
            ).astype(BF)


def ref_spectra(blocks, fwd_k):
    v = pl.BlockSpec(memory_space=pltpu.VMEM)
    return pl.pallas_call(
        ref_kernel,
        in_specs=[v, v],
        out_specs=v,
        out_shape=jax.ShapeDtypeStruct((M, 16, 256), BF),
        scratch_shapes=[pltpu.VMEM((A * 8, 256), F32)],
        compiler_params=pltpu.CompilerParams(vmem_limit_bytes=8 * MIB),
        cost_estimate=pl.CostEstimate(flops=1000, bytes_accessed=1000, transcendentals=0),
        name="ref_spectra",
    )(blocks, fwd_k)


def score_kernel(*refs):
    p_ref, blocks, inv_ref, o_ref, xs = refs[0], refs[1:5], refs[5], refs[6], refs[7]
    xs[:, 2 * M * 8 :, :] = jnp.zeros((16, K_INV - 2 * M * 8, 256), BF)

    def cross(m):
        upper = p_ref[m]
        re, im = upper[:, 0:128], upper[:, 128:256]
        rhs = jnp.concatenate([upper, jnp.concatenate([im, -re], axis=1)], axis=0)
        lhs = jnp.concatenate([b[i, m] for b in blocks for i in range(4)], axis=0)
        x = jnp.dot(lhs, rhs, preferred_element_type=F32)
        row = pl.multiple_of(m * 16, 16)
        for g in range(16):
            for h in range(2):
                k = 16 * g + 8 * h
                xs[g, pl.ds(row, 16), 128 * h : 128 * h + 128] = jnp.concatenate(
                    [x[k : k + 8, 0:128], x[k : k + 8, 128:256]], axis=0
                ).astype(BF)

    repeat(cross)

    def four(i, best):
        for u in range(4):
            y = jnp.dot(inv_ref[...], xs[4 * i + u], preferred_element_type=F32)
            for t in range(A):
                best = jnp.maximum(best, y[8 * t : 8 * t + 8])
        return best

    best = lax.fori_loop(0, 4, four, jnp.full((8, 256), -jnp.inf, F32))
    best = jnp.max(best, axis=0, keepdims=True)
    o_ref[...] = jnp.maximum(best[:, 0:128], best[:, 128:256])


def scores_of(p, blocks, inv_k):
    v = pl.BlockSpec(memory_space=pltpu.VMEM)
    return pl.pallas_call(
        score_kernel,
        in_specs=[v] * 6,
        out_specs=v,
        out_shape=jax.ShapeDtypeStruct((1, 128), F32),
        scratch_shapes=[pltpu.VMEM((16, K_INV, 256), BF)],
        compiler_params=pltpu.CompilerParams(vmem_limit_bytes=20 * MIB),
        cost_estimate=pl.CostEstimate(flops=6_000_000_000, bytes_accessed=8_000_000, transcendentals=0),
        name="scores",
    )(p, *blocks, inv_k)


def sums_kernel(sc, c0, c1, c2, c3, tab_ref, mine, other, acc):
    width = 18 * 128
    lane = lax.broadcasted_iota(jnp.int32, (128, 256), 1).astype(F32)
    picks, groups = [], []
    for c in (c0, c1, c2, c3):
        meta = c[:, width : width + 128].astype(F32)
        picks.append(jnp.where(lane == meta[:, 0:1], 1.0, 0.0).astype(F32).T.astype(BF))
        groups.append(jnp.where(lane == meta[:, 1:2], 1.0, 0.0).astype(BF))
    pick = jnp.concatenate(picks, axis=1)
    group = jnp.concatenate(groups, axis=0)
    count = jnp.dot(pick, group, preferred_element_type=F32)
    flipped = tab_ref[...].T
    tab = jnp.concatenate([flipped, flipped], axis=1)
    wsum = jnp.dot(count, tab * tab, precision=lax.Precision.HIGHEST, preferred_element_type=F32)
    for t in range(9):
        cols = slice(256 * t, 256 * t + 256)
        x = jnp.concatenate([c[:, cols] for c in (c0, c1, c2, c3)], axis=0)
        acc[:, cols] = jnp.dot(pick, x, preferred_element_type=F32)
    left = lax.broadcasted_iota(jnp.int32, (256, 128), 1) < R
    for ref, core in ((mine, sc[2]), (other, 1 - sc[2])):
        for xh in range(2):
            start = pl.multiple_of((9 * xh + 4 * core) * 128, 128)
            ref[xh] = acc[:, pl.ds(start, 640)]
            mid = acc[:, (9 * xh + 4) * 128 : (9 * xh + 5) * 128]
            keep = jnp.logical_xor(left, core == 1)
            ref[xh, :, pl.ds(pl.multiple_of((1 - core) * 512, 128), 128)] = jnp.where(keep, mid, wsum)


def class_sums(sc, cs, tab):
    v = pl.BlockSpec(memory_space=pltpu.VMEM)
    shape = jax.ShapeDtypeStruct((2, 256, 640), F32)
    return pl.pallas_call(
        sums_kernel,
        in_specs=[pl.BlockSpec(memory_space=pltpu.SMEM)] + [v] * 5,
        out_specs=[v, v],
        out_shape=[shape, shape],
        scratch_shapes=[pltpu.VMEM((256, 18 * 128), F32)],
        compiler_params=pltpu.CompilerParams(vmem_limit_bytes=VMEM_LIMIT),
        cost_estimate=pl.CostEstimate(flops=700_000_000, bytes_accessed=5_000_000, transcendentals=0),
        name="class_sums",
    )(sc, *cs, tab)


def cut_x_kernel(sc, a_ref, b_ref, o0, o1, o2, o3):
    for dx, o in enumerate((o0, o1, o2, o3)):
        x = lax.rem(sc[1] + dx, 4)
        xh, xl = x // 2, lax.rem(x, 2)
        rows = pl.ds(pl.multiple_of(xl * 128, 128), 128)
        o[...] = (a_ref[xh, rows, :] + b_ref[xh, rows, :]).astype(o.dtype)


def cut_x(sc, a, b):
    v = pl.BlockSpec(memory_space=pltpu.VMEM)
    return pl.pallas_call(
        cut_x_kernel,
        in_specs=[pl.BlockSpec(memory_space=pltpu.SMEM), v, v],
        out_specs=[v] * 4,
        out_shape=[jax.ShapeDtypeStruct((128, 640), F32)] + [jax.ShapeDtypeStruct((128, 640), BF)] * 3,
        compiler_params=pltpu.CompilerParams(vmem_limit_bytes=VMEM_LIMIT),
        cost_estimate=pl.CostEstimate(flops=400_000, bytes_accessed=3_900_000, transcendentals=0),
        name="cut_x",
    )(sc, a, b)


def cut_z_kernel(sc, a0, a1, a2, a3, o0, o1, o2, o3):
    for dz, o in enumerate((o0, o1, o2, o3)):
        z = lax.rem(sc[3] + dz, 4)
        rows = pl.ds(pl.multiple_of(z * 32, 32), 32)
        far = a1[rows, :].astype(F32) + a2[rows, :].astype(F32) + a3[rows, :].astype(F32)
        o[...] = (a0[rows, :] + far).astype(o.dtype)


def cut_z(sc, parts):
    v = pl.BlockSpec(memory_space=pltpu.VMEM)
    return pl.pallas_call(
        cut_z_kernel,
        in_specs=[pl.BlockSpec(memory_space=pltpu.SMEM)] + [v] * 4,
        out_specs=[v] * 4,
        out_shape=[jax.ShapeDtypeStruct((32, 640), F32)] + [jax.ShapeDtypeStruct((32, 640), BF)] * 3,
        compiler_params=pltpu.CompilerParams(vmem_limit_bytes=VMEM_LIMIT),
        cost_estimate=pl.CostEstimate(flops=400_000, bytes_accessed=1_700_000, transcendentals=0),
        name="cut_z",
    )(sc, *parts)


def final_kernel(sc, a0, a1, a2, a3, o_ref):
    s = a0[...] + (a1[...].astype(F32) + a2[...].astype(F32) + a3[...].astype(F32))
    odd = sc[2] == 1
    left = lax.broadcasted_iota(jnp.int32, (32, 128), 1) < R
    tile = [s[:, 128 * t : 128 * t + 128] for t in range(5)]
    held = jnp.where(odd, tile[0], tile[4])
    turned = pltpu.roll(held, R, 1)
    weight = jnp.where(jnp.logical_xor(left, odd), turned, held)
    tile = [t / (weight + TAU) for t in tile]
    rolled = [pltpu.roll(t, R, 1) for t in tile]
    later = [jnp.where(left, rolled[t], rolled[t + 1]) for t in range(4)] + [rolled[4]]
    for t in range(4):
        o_ref[:, 128 * t : 128 * t + 128] = jnp.where(odd, later[t], tile[t])[0:25]
    o_ref[:, 512:576] = jnp.where(odd, later[4], tile[4])[0:25, 0:R]


def final(sc, parts):
    v = pl.BlockSpec(memory_space=pltpu.VMEM)
    return pl.pallas_call(
        final_kernel,
        in_specs=[pl.BlockSpec(memory_space=pltpu.SMEM)] + [v] * 4,
        out_specs=v,
        out_shape=jax.ShapeDtypeStruct((25, 576), F32),
        compiler_params=pltpu.CompilerParams(vmem_limit_bytes=2 * MIB),
        name="final",
    )(sc, *parts)


def place(y, x, z, core):
    return ((y % 4) * 4 + (x % 4) // 2 * 2 + core % 2) * 8 + (x % 2) * 4 + z % 4


def permutation(move):
    return [
        (place(y, x, z, c), place(*move(y, x, z, c)))
        for y in range(4)
        for x in range(4)
        for z in range(4)
        for c in range(2)
    ]


CORE = permutation(lambda y, x, z, c: (y, x, z, c + 1))
HIGH = permutation(lambda y, x, z, c: (y, x + 2, z, c))
LOW = permutation(lambda y, x, z, c: (y, x ^ 1, z, c))
Y_NEAR = permutation(lambda y, x, z, c: (y ^ 1, x, z, c))
Y_FAR = permutation(lambda y, x, z, c: (y + 2, x, z, c))
YS = [permutation(lambda y, x, z, c, d=d: (y + d, x, z, c)) for d in range(4)]
XS = [permutation(lambda y, x, z, c, d=d: (y, x + d, z, c)) for d in range(4)]
ZS = [permutation(lambda y, x, z, c, d=d: (y, x, z + d, c)) for d in range(4)]


def move(value, pairs):
    return lax.ppermute(value, AXES, pairs)


def after(values, *others):
    return lax.optimization_barrier((*values, *others))[: len(values)]


def join(own, other, upper):
    lower = upper == 0
    return jnp.stack([jnp.where(lower, own, other), jnp.where(lower, other, own)])


def per_device(particles, references, owner, class_offset, rotation, shifts, ctf_group, ctf_table):
    fwd_np, inv_np = tables()
    fwd_k, inv_k = jnp.asarray(fwd_np), jnp.asarray(inv_np)
    fx, fy = (jnp.asarray(t) for t in freq_tables())
    dom, cls = lax.axis_index("dom"), lax.axis_index("cls")
    y, xh, core = dom // 4, dom // 2 % 2, dom % 2
    xl, z = cls // 4, cls % 4
    sc = jnp.stack([y, xh * 2 + xl, core, z]).astype(jnp.int32)

    low, high = references[0:16], references[9:25]
    first = core == 0
    keep = jnp.where(first, low, high)
    give = jnp.where(first, high, low)
    got = move(give, CORE)
    block = jnp.where(
        first, jnp.concatenate([keep, got], axis=1), jnp.concatenate([got, keep], axis=1)
    )
    rows = [shifts.T, rotation[None], owner.T, class_offset[None], ctf_group[None]]
    table = ctf_table.T
    block, rows[1] = lax.optimization_barrier((block, rows[1]))
    half = prep(particles, rows, table, fx, fy, 0)
    far = move(block, HIGH)
    far, *half = lax.optimization_barrier((far, *half))
    pair = join(block, far, xh)
    pair, rows[1] = lax.optimization_barrier((pair, rows[1]))
    weighted, *sent = prep(particles, rows, table, fx, fy, 4, half)
    near = move(pair, Y_NEAR)
    near, weighted, *sent = lax.optimization_barrier((near, weighted, *sent))
    quad = join(pair, near, y % 2)
    octet = join(quad, move(quad, Y_FAR), y // 2).reshape(4, 2, 16, 1152)

    across = move(sent[2], YS[2])
    part = spectra(weighted, fwd_k)
    own = ref_spectra(octet, fwd_k)
    up, down = move(own, ZS[1]), move(own, ZS[3])
    side = move(own, LOW)
    (ready,) = after([side], across)
    side_up, side_down = move(ready, ZS[1]), move(ready, ZS[3])
    one, three = after([sent[1], sent[3]], part, up, down)
    held = [sent[0], move(one, YS[1]), across, move(three, YS[3])]
    on_up, on_down = move(up, ZS[1]), move(side_down, ZS[3])
    early = jnp.stack([own, side, up, down])
    early_twin = move(early, CORE)
    held = after(held, side_up, side_down)
    mine, other = class_sums(sc, held, table)
    cut = cut_x(sc, mine, move(other, CORE))
    late = jnp.stack([side_up, side_down, on_up, on_down])
    late_twin = move(late, CORE)
    cut = [cut[0]] + [move(cut[d], XS[d]) for d in (1, 2, 3)]
    scores = scores_of(part, [early, early_twin, late, late_twin], inv_k)
    *cut, scores = lax.optimization_barrier((*cut, scores))
    cut = cut_z(sc, cut)
    cut = [cut[0]] + [move(cut[d], ZS[d]) for d in (1, 2, 3)]
    return scores[0], final(sc, cut)


def solution(mesh):
    return jax.shard_map(
        per_device,
        mesh=mesh,
        in_specs=(
            P(("dom", "cls"), None),
            P("cls", "dom"),
            P(("dom", "cls"), None),
            P(("dom", "cls")),
            P(("dom", "cls")),
            P(("dom", "cls"), None),
            P(("dom", "cls")),
            P(),
        ),
        out_specs=(P(("dom", "cls")), P("cls", "dom")),
        check_vma=False,
    )
```
